32 devices in a mesh: dp: 8 (over z, y), ctx: 4 (over x, core).
Axes of the slice: x: 2, y: 2, z: 4, core: 2. Of those that a mesh axis runs over, the one named last changes fastest.
Arguments:
- tokens: bfloat16 [8, 1024, 1024], P('dp', 'ctx'), may hold values from -6 to 6
- doc_ids: int32 [8, 1024], P('dp', 'ctx'), may hold values from 0 to 7, never falling along the last dimension, each value on 1 to 512 neighbouring positions
- w_query: bfloat16 [1024, 1024], P(('dp', 'ctx')), may hold values from -0.1875 to 0.1875
- key_weight: bfloat16 [1024, 512], P(('dp', 'ctx')), may hold values from -0.1875 to 0.1875
- value_weight: bfloat16 [1024, 512], P(('dp', 'ctx')), may hold values from -0.1875 to 0.1875
- w_output: bfloat16 [1024, 1024], P(None, ('dp', 'ctx')), may hold values from -1.5 to 1.5
- w_gate: bfloat16 [1024, 4608], P(('dp', 'ctx')), may hold values from -0.1875 to 0.1875
- w_up: bfloat16 [1024, 4608], P(('dp', 'ctx')), may hold values from -0.1875 to 0.1875
- w_down: bfloat16 [4608, 1024], P(None, ('dp', 'ctx')), may hold values from -0.09375 to 0.09375
- norm_gains: bfloat16 [2, 1024], P(None, ('dp', 'ctx')), may hold values from 0.5 to 1.5
- head_norm_gains: bfloat16 [2, 64], replicated, may hold values from 0.5 to 1.5
- out_grad: bfloat16 [8, 1024, 1024], P('dp', 'ctx'), may hold values from -6 to 6
Outputs:
- layer_out: bfloat16 [8, 1024, 1024], P('dp', 'ctx')
- input_grad: bfloat16 [8, 1024, 1024], P('dp', 'ctx')
- grad_query: bfloat16 [1024, 1024], P(('dp', 'ctx'))
- grad_key: bfloat16 [1024, 512], P(('dp', 'ctx'))
- grad_value: bfloat16 [1024, 512], P(('dp', 'ctx'))
- grad_output: bfloat16 [1024, 1024], P(None, ('dp', 'ctx'))
- grad_gate: bfloat16 [1024, 4608], P(('dp', 'ctx'))
- grad_up: bfloat16 [1024, 4608], P(('dp', 'ctx'))
- grad_down: bfloat16 [4608, 1024], P(None, ('dp', 'ctx'))
- grad_norms: bfloat16 [2, 1024], P(None, ('dp', 'ctx'))
- grad_heads: bfloat16 [2, 64], replicated
The draws below stay inside these ranges and needn't reach their ends.
Inputs may be any that keep to these rules, and one draw needn't show every extreme that they name: `doc_ids`: along each sequence the numbers never fall; each document spans 1 to 512 tokens.
All inputs are finite; a program needn't handle non-finite values.
Results may differ from the reference program's by a relative error of at most 0.015.
Values may be sent and summed in bfloat16 or wider, within the bound.
No kernel may reach another device: no remote copies, remote signals or barrier semaphores. Data moves between devices by JAX's collectives and lax.ppermute only.
A program may use at most 320 MiB of HBM per device.

```python
import math
import jax
import jax.numpy as jnp
import numpy as np
from jax import lax

MODEL_WIDTH = 1024
QUERY_HEADS = 16
KEY_VALUE_HEADS = 8
HEAD_SIZE = 64
FF = 4608
LEN = 1024
DOCS = 8
DOC_MOST = 512
SEQS_ALL = 8


def block_scale(key, dims, split, smallest, top_value):
    def one(axis_at, shards_of):
        heights = jax.random.uniform(jax.random.fold_in(jax.random.fold_in(key, 6), axis_at), (shards_of,), jnp.float32, smallest / len(split), top_value / len(split))
        return jnp.repeat(jnp.exp(heights), dims[axis_at] // shards_of).reshape((-1,) + (1,) * (len(dims) - axis_at - 1))

    factor_of = one(*split[0])
    for cut in split[1:]:
        factor_of = factor_of * one(*cut)
    return factor_of


def profile(amount, total, bound, skew):
    weights = [(1 << 20) // math.isqrt(standing ** skew) + 1 for standing in range(2, amount + 1)]
    surplus, counts = total - bound - (amount - 1), [1] * (amount - 1)
    while surplus > 0:
        movable = [i for i in range(amount - 1) if counts[i] < bound]
        pool, left = sum([weights[i] for i in movable]), surplus
        for i in movable:
            extra = min(bound - counts[i], max(1, left * weights[i] // pool), surplus)
            counts[i] = counts[i] + extra
            surplus = surplus - extra
    return np.array([bound] + counts)


def ragged_sizes(stream_key, number_of, total, bound, lean):
    if number_of == 2:
        one = jax.random.randint(stream_key, (), max(1, total - bound), min(bound, total - 1) + 1)
        return jnp.stack([one, total - one])
    lengths = jnp.asarray(profile(number_of, total, bound, lean), jnp.int32)
    twos = (number_of - 1) // 2
    source_of, receiver = lengths[1:1 + 2 * twos:2], lengths[2:2 + 2 * twos:2]
    margin = jnp.minimum(source_of - 1, bound - receiver)
    shifted = jax.random.randint(jax.random.fold_in(stream_key, 1), (twos,), 0, 1 << 20) % (margin + 1)
    lengths = lengths.at[1:1 + 2 * twos:2].set(source_of - shifted).at[2:2 + 2 * twos:2].set(receiver + shifted)
    return lengths[jax.random.permutation(jax.random.fold_in(stream_key, 2), number_of)]


def centred(stream_key, shape, spread, most, pieces=(), held_as=jnp.bfloat16):
    values = spread * jax.random.normal(stream_key, shape, jnp.float32)
    if pieces:
        values = values * block_scale(stream_key, shape, pieces, -0.22, 0.18)
    return jnp.clip(values, -most, most).astype(held_as)


def setup_inputs(seed: int = 0) -> dict:
    keys = jax.random.split(jax.random.key(seed), 13)
    return {
        "tokens": centred(keys[0], (SEQS_ALL, LEN, MODEL_WIDTH), 1.0, 6.0, ((0, 8), (1, 4))),
        "doc_ids": jax.vmap(lambda own: jnp.searchsorted(jnp.cumsum(ragged_sizes(own, DOCS, LEN, DOC_MOST, 2)), jnp.arange(LEN), side="right"))(jax.random.split(keys[1], SEQS_ALL)).reshape((SEQS_ALL, LEN)).astype(jnp.int32),
        "w_query": centred(keys[2], (MODEL_WIDTH, QUERY_HEADS * HEAD_SIZE), MODEL_WIDTH ** -0.5, 0.1875, ((0, 32),)),
        "key_weight": centred(keys[3], (MODEL_WIDTH, KEY_VALUE_HEADS * HEAD_SIZE), MODEL_WIDTH ** -0.5, 0.1875, ((0, 32),)),
        "value_weight": centred(keys[4], (MODEL_WIDTH, KEY_VALUE_HEADS * HEAD_SIZE), MODEL_WIDTH ** -0.5, 0.1875, ((0, 32),)),
        "w_output": centred(keys[5], (QUERY_HEADS * HEAD_SIZE, MODEL_WIDTH), (max(QUERY_HEADS * HEAD_SIZE // 64, 1)) ** -0.5, 1.5, ((1, 32),)),
        "w_gate": centred(keys[6], (MODEL_WIDTH, FF), MODEL_WIDTH ** -0.5, 0.1875, ((0, 32),)),
        "w_up": centred(keys[7], (MODEL_WIDTH, FF), MODEL_WIDTH ** -0.5, 0.1875, ((0, 32),)),
        "w_down": centred(keys[8], (FF, MODEL_WIDTH), FF ** -0.5, 0.09375, ((1, 32),)),
        "norm_gains": jnp.clip(1.0 + 0.1 * jax.random.normal(keys[9], (2, MODEL_WIDTH), jnp.float32), 0.5, 1.5).astype(jnp.bfloat16),
        "head_norm_gains": jnp.clip(1.0 + 0.1 * jax.random.normal(keys[10], (2, HEAD_SIZE), jnp.float32), 0.5, 1.5).astype(jnp.bfloat16),
        "out_grad": centred(keys[11], (SEQS_ALL, LEN, MODEL_WIDTH), 1.0, 6.0, ((0, 8), (1, 4))),
    }


@jax.custom_vjp
def lower_precision(v):
    return lax.optimization_barrier(v.astype(jnp.bfloat16)).astype(jnp.float32)

@jax.custom_vjp
def low_back(v):
    return v

def low_keep(v):
    return (lower_precision(v), None)

def low_pass(kept, grad):
    return (grad,)

def back_keep(v):
    return (v, None)

def back_low(kept, grad):
    return (lower_precision(grad),)
lower_precision.defvjp(low_keep, low_pass)
low_back.defvjp(back_keep, back_low)
EPS = 1e-05
THETA = 1000000.0

def rms_scale(values, gain_row):
    return values * lax.rsqrt(lax.optimization_barrier(jnp.mean(values * values, -1, keepdims=True)) + EPS) * gain_row

def rope_tables(positions, width_all):
    half_width = width_all // 2
    freqs = THETA ** (-(2.0 * jnp.arange(half_width, dtype=jnp.float32)) / width_all)
    angles = positions.astype(jnp.float32)[..., None] * freqs
    angles = jnp.concatenate([angles, angles], -1)
    return (jnp.cos(angles), jnp.sin(angles))

def rotate(values, cosine_table, sine_table):
    half_width = values.shape[-1] // 2
    turned = jnp.concatenate([-values[..., half_width:], values[..., :half_width]], -1)
    return values * cosine_table + turned * sine_table

def head_prepare(projected, gain_row, cosine_table, sine_table, head_count):
    shaped = projected.reshape(projected.shape[:-1] + (head_count, gain_row.shape[0]))
    normed = rms_scale(shaped, gain_row)
    return rotate(normed, cosine_table[..., None, :], sine_table[..., None, :])

def matmul_high(left_in, right_in):
    return jnp.matmul(left_in, right_in, precision=lax.Precision.HIGHEST)

def attend_one(query_rows, key_row_matrix, value_row_matrix, doc_row):
    length_total = doc_row.shape[0]
    index_row = jnp.arange(length_total, dtype=jnp.int32)
    visible = (doc_row[None, :] == doc_row[:, None]) & (index_row[None, :] <= index_row[:, None])
    grouped_heads = query_rows.reshape(length_total, KEY_VALUE_HEADS, QUERY_HEADS // KEY_VALUE_HEADS, HEAD_SIZE)
    raw = jnp.einsum('tkgd,skd->kgts', grouped_heads, key_row_matrix, precision=lax.Precision.HIGHEST) * (1.0 / math.sqrt(HEAD_SIZE))
    scores = low_back(raw)
    scores = jnp.where(visible[None, None], scores, -1e+30)
    top_row = lax.optimization_barrier(jnp.max(scores, -1, keepdims=True))
    expd = jnp.exp(scores - top_row)
    probs = expd / lax.optimization_barrier(jnp.sum(expd, -1, keepdims=True))
    mixed = jnp.einsum('kgts,skd->tkgd', lower_precision(probs), value_row_matrix, precision=lax.Precision.HIGHEST)
    return mixed.reshape(length_total, QUERY_HEADS * HEAD_SIZE)

def forward(inputs, doc_rows, w_query, key_weight, value_weight, w_output, w_gate, w_up, w_down, norm_gains, head_norm_gains):
    sequence_count = inputs.shape[0]
    length_total = inputs.shape[1]
    index_row = jnp.arange(length_total, dtype=jnp.int32)
    earlier = lax.optimization_barrier(jnp.sum((doc_rows[:, None, :] < doc_rows[:, :, None]).astype(jnp.int32), -1))
    positions = index_row[None, :] - earlier
    cosine_table, sine_table = rope_tables(positions, HEAD_SIZE)
    normed_one = lower_precision(rms_scale(inputs, norm_gains[0]))
    q_pre = low_back(matmul_high(normed_one, w_query))
    key_before_norm = low_back(matmul_high(normed_one, key_weight))
    value_flattened = low_back(lower_precision(matmul_high(normed_one, value_weight)))
    query_rows = lower_precision(head_prepare(q_pre, head_norm_gains[0], cosine_table, sine_table, QUERY_HEADS))
    key_row_matrix = lower_precision(head_prepare(key_before_norm, head_norm_gains[1], cosine_table, sine_table, KEY_VALUE_HEADS))
    value_row_matrix = value_flattened.reshape(sequence_count, length_total, KEY_VALUE_HEADS, HEAD_SIZE)
    mixed = lax.map(jax.checkpoint(lambda packed: attend_one(packed[0], packed[1], packed[2], packed[3])), (query_rows, key_row_matrix, value_row_matrix, doc_rows))
    attn_out = low_back(lower_precision(mixed))
    resid = inputs + low_back(matmul_high(attn_out, w_output))
    normed_two = lower_precision(rms_scale(resid, norm_gains[1]))
    gate_act = low_back(matmul_high(normed_two, w_gate))
    up_act = low_back(matmul_high(normed_two, w_up))
    hidden = lower_precision(jax.nn.silu(gate_act) * up_act)
    return resid + low_back(matmul_high(hidden, w_down))

def reference(tokens, doc_ids, w_query, key_weight, value_weight, w_output, w_gate, w_up, w_down, norm_gains, head_norm_gains, out_grad):
    params = tuple((weight_in.astype(jnp.float32) for weight_in in (w_query, key_weight, value_weight, w_output, w_gate, w_up, w_down, norm_gains, head_norm_gains)))
    group_rows = 4
    blocks = SEQS_ALL // group_rows
    shaped_in = tokens.reshape(blocks, group_rows, LEN, MODEL_WIDTH)
    shaped_ids = doc_ids.reshape(blocks, group_rows, LEN)
    shaped_grad = out_grad.reshape(blocks, group_rows, LEN, MODEL_WIDTH)

    def step(carry, packed):
        block_in, block_ids, block_grad = packed

        def apply(inputs, *weights):
            return forward(inputs, block_ids, *weights)
        result, pull = jax.vjp(apply, block_in.astype(jnp.float32), *params)
        pulled = pull(block_grad.astype(jnp.float32))
        carry = tuple((held_sum + fresh_sum for held_sum, fresh_sum in zip(carry, pulled[1:])))
        return (carry, (result.astype(jnp.bfloat16), pulled[0].astype(jnp.bfloat16)))
    start_sums = tuple((jnp.zeros_like(weight_in) for weight_in in params))
    totals, (outs_all, grads_all) = lax.scan(step, start_sums, (shaped_in, shaped_ids, shaped_grad))
    return (outs_all.reshape(SEQS_ALL, LEN, MODEL_WIDTH), grads_all.reshape(SEQS_ALL, LEN, MODEL_WIDTH), totals[0].astype(jnp.bfloat16), totals[1].astype(jnp.bfloat16), totals[2].astype(jnp.bfloat16), totals[3].astype(jnp.bfloat16), totals[4].astype(jnp.bfloat16), totals[5].astype(jnp.bfloat16), totals[6].astype(jnp.bfloat16), totals[7].astype(jnp.bfloat16), totals[8].astype(jnp.bfloat16))
```

```python
import math

import jax
import jax.numpy as jnp
from jax import lax
from jax.sharding import PartitionSpec as P

EPS = 1e-05
THETA = 1000000.0
BF = jnp.bfloat16
F32 = jnp.float32
ALL = ("dp", "ctx")


def add_low(a, b):
    return (a.astype(F32) + b.astype(F32)).astype(BF)


def flip(value, axis, size, bits):
    return lax.ppermute(value, axis, [(i, i ^ bits) for i in range(size)])


def gather_ctx(own):
    core = flip(own, "ctx", 4, 1)
    across = flip(own, "ctx", 4, 2)
    return [own, core, across, flip(across, "ctx", 4, 1)]


def scatter_ctx(parts):
    far = flip(parts[3], "ctx", 4, 1)
    near = flip(parts[1], "ctx", 4, 1)
    far_sum = add_low(parts[2], far)
    far_in = flip(far_sum, "ctx", 4, 2)
    return parts[0].astype(F32) + near.astype(F32) + far_in.astype(F32)


def exchange_ctx(parts):
    return [parts[0]] + [flip(parts[j], "ctx", 4, j) for j in range(1, 4)]


def place(parts, where, axis):
    size = parts[0].shape[axis]
    shape = list(parts[0].shape)
    shape[axis] = size * len(parts)
    out = jnp.zeros(shape, parts[0].dtype)
    for part, at in zip(parts, where):
        out = lax.dynamic_update_slice_in_dim(out, part, at * size, axis)
    return out


def ring(value, size):
    return lax.ppermute(value, "dp", [(i, (i + 2) % size) for i in range(size)])


def gather_dp(block, size):
    if size < 4 or size > 8:
        return lax.all_gather(block, "dp", axis=0, tiled=True)
    me = lax.axis_index("dp")
    parts, where = [], []
    for step in range(size // 2):
        at = (me - 2 * step) % size
        parts += [block, flip(block, "dp", size, 1)]
        where += [at, at ^ 1]
        if step + 1 < size // 2:
            block = ring(block, size)
    return place(parts, where, 0)


def scatter_dp(whole, size):
    if size < 4 or size > 8:
        return lax.psum_scatter(whole, "dp", scatter_dimension=0, tiled=True).astype(F32)
    me = lax.axis_index("dp")
    rows = whole.shape[0] // size

    def part(at):
        return lax.dynamic_slice_in_dim(whole, at * rows, rows, 0)

    total = None
    for step in range(size // 2):
        at = (me - 2 * (step + 1)) % size
        near = flip(part(at ^ 1), "dp", size, 1)
        own = part(at).astype(F32) + near.astype(F32)
        if total is not None:
            own = own + ring(total, size).astype(F32)
        total = own.astype(BF)
    return own


def sum_all(value, dp_size):
    for bits in (1, 2):
        value = value + flip(value, "ctx", 4, bits)
    bits = 1
    while bits < dp_size:
        value = value + flip(value, "dp", dp_size, bits)
        bits *= 2
    return value


def dot(a, b):
    return lax.dot_general(a, b, (((1,), (0,)), ((), ())), preferred_element_type=F32)


def dot_nt(a, b):
    return lax.dot_general(a, b, (((1,), (1,)), ((), ())), preferred_element_type=F32)


def dot_tn(a, b):
    return lax.dot_general(a, b, (((0,), (0,)), ((), ())), preferred_element_type=F32)


def rms_scale(values, gain_row):
    return values * lax.rsqrt(jnp.mean(values * values, -1, keepdims=True) + EPS) * gain_row


def rope_tables(positions, width_all):
    half_width = width_all // 2
    freqs = THETA ** (-(2.0 * jnp.arange(half_width, dtype=jnp.float32)) / width_all)
    angles = positions.astype(jnp.float32)[..., None] * freqs
    angles = jnp.concatenate([angles, angles], -1)
    return (jnp.cos(angles), jnp.sin(angles))


def rotate(values, cosine_table, sine_table):
    half_width = values.shape[-1] // 2
    turned = jnp.concatenate([-values[..., half_width:], values[..., :half_width]], -1)
    return values * cosine_table + turned * sine_table


def head_prepare(projected, gain_row, cosine_table, sine_table, head_count):
    shaped = projected.reshape(projected.shape[:-1] + (head_count, gain_row.shape[0]))
    normed = rms_scale(shaped, gain_row)
    return rotate(normed, cosine_table[..., None, :], sine_table[..., None, :])


def split_parts(tall, count):
    rows = tall.shape[0] // count
    return [lax.slice_in_dim(tall, j * rows, (j + 1) * rows, axis=0) for j in range(count)]


def on_device(
    dp_size,
    tokens,
    doc_ids,
    w_query,
    key_weight,
    value_weight,
    w_output,
    w_gate,
    w_up,
    w_down,
    norm_gains,
    head_norm_gains,
    out_grad,
):
    local_len, model_dim = tokens.shape[1:]
    tokens, out_grad, doc_row = tokens[0], out_grad[0], doc_ids[0]
    head_dim = head_norm_gains.shape[1]
    q_cols, kv_cols = w_query.shape[1] // 4, key_weight.shape[1] // 4
    q_heads, kv_heads = q_cols // head_dim, kv_cols // head_dim
    group_size = q_heads // kv_heads
    scale_by = 1.0 / math.sqrt(head_dim)
    shard = norm_gains.shape[1]
    ff_cols = w_gate.shape[1] // 4
    me = lax.axis_index("ctx")
    places = [me ^ j for j in range(4)]

    def spread(pieces):
        sent = []
        for at in places:
            cut = [
                lax.dynamic_slice_in_dim(p, at * (p.shape[1] // 4), p.shape[1] // 4, 1)
                for p in pieces
            ]
            sent.append(jnp.concatenate(cut, 1))
        block = place(exchange_ctx(sent), places, 0)
        return gather_dp(block, dp_size)

    gains_full = lax.all_gather(norm_gains, ALL, axis=1, tiled=True).astype(F32)
    attn_w = spread([w_query, key_weight, value_weight, w_output.T])
    wq = attn_w[:, :q_cols]
    wk = attn_w[:, q_cols : q_cols + kv_cols]
    wv = attn_w[:, q_cols + kv_cols : q_cols + 2 * kv_cols]
    wo_t = attn_w[:, q_cols + 2 * kv_cols :]
    wg = spread([w_gate])
    wu = spread([w_up])
    wd_t = spread([w_down.T])

    head_full = head_norm_gains.astype(F32)
    docs = jnp.concatenate(gather_ctx(doc_row.reshape(1, -1)), 1)[0]
    all_tokens = jnp.concatenate(gather_ctx(tokens), 0)
    all_grad = jnp.concatenate(gather_ctx(out_grad), 0)
    index = jnp.concatenate(
        [at * local_len + jnp.arange(local_len, dtype=jnp.int32) for at in places]
    )
    earlier = jnp.sum((docs[None, :] < docs[:, None]).astype(jnp.int32), -1)
    positions = index - earlier
    visible = (docs[None, :] == docs[:, None]) & (index[None, :] <= index[:, None])
    cosine_table, sine_table = rope_tables(positions, head_dim)

    inputs = all_tokens.astype(F32)
    normed_one = rms_scale(inputs, gains_full[0]).astype(BF)
    q_pre = dot(normed_one, wq)
    k_pre = dot(normed_one, wk)
    value_rows = dot(normed_one, wv).astype(BF)
    query_rows = head_prepare(q_pre, head_full[0], cosine_table, sine_table, q_heads).astype(BF)
    key_rows = head_prepare(k_pre, head_full[1], cosine_table, sine_table, kv_heads).astype(BF)
    value_rows = value_rows.reshape(-1, kv_heads, head_dim)
    grouped = query_rows.reshape(-1, kv_heads, group_size, head_dim)

    def attend_scores():
        raw = (
            jnp.einsum("tkgd,skd->kgts", grouped, key_rows, preferred_element_type=F32) * scale_by
        )
        return jnp.where(visible[None, None], raw, -1e30)

    scores = attend_scores()
    top_row = jnp.max(scores, -1, keepdims=True)
    expd = jnp.exp(scores - top_row)
    total_row = jnp.sum(expd, -1, keepdims=True)
    probs = expd / total_row
    log_total = top_row + jnp.log(total_row)
    mixed = jnp.einsum(
        "kgts,skd->tkgd", probs.astype(BF), value_rows, preferred_element_type=F32
    )
    attn_out = mixed.reshape(-1, q_cols).astype(BF)
    resid_sum = scatter_ctx(split_parts(dot_nt(attn_out, wo_t).astype(BF), 4))
    resid = tokens.astype(F32) + resid_sum
    normed_own = rms_scale(resid, gains_full[1]).astype(BF)
    normed_two = jnp.concatenate(gather_ctx(normed_own), 0)

    gate_act = dot(normed_two, wg)
    up_act = dot(normed_two, wu)
    hidden = (jax.nn.silu(gate_act) * up_act).astype(BF)
    grad_hidden = dot(all_grad, wd_t)
    _, gate_pull = jax.vjp(lambda g, u: jax.nn.silu(g) * u, gate_act, up_act)
    grad_gate_full, grad_up_full = gate_pull(grad_hidden)
    grad_gate = grad_gate_full.astype(BF)
    grad_up = grad_up_full.astype(BF)
    grad_two_part = (dot_nt(grad_gate, wg) + dot_nt(grad_up, wu)).astype(BF)
    grad_norm_two = scatter_ctx(split_parts(grad_two_part, 4))
    _, second_pull = jax.vjp(rms_scale, resid, gains_full[1])
    grad_resid_norm, grad_gain_two = second_pull(grad_norm_two)
    grad_resid = out_grad.astype(F32) + grad_resid_norm
    down_part = dot_nt(hidden, wd_t).astype(BF)
    layer_out = (resid + scatter_ctx(split_parts(down_part, 4))).astype(BF)

    def collect(whole, widths):
        mine = scatter_dp(whole.astype(BF), dp_size).astype(BF)
        sent = [lax.dynamic_slice_in_dim(mine, at * shard, shard, 0) for at in places]
        got = exchange_ctx(sent)
        outs, start = [], 0
        for width in widths:
            cut = [g[:, start : start + width] for g in got]
            outs.append(place(cut, places, 1))
            start += width
        return outs

    (grad_g_out,) = collect(dot_tn(normed_two, grad_gate), (ff_cols,))
    (grad_u_out,) = collect(dot_tn(normed_two, grad_up), (ff_cols,))
    (grad_d_out,) = collect(dot_tn(all_grad, hidden), (ff_cols,))

    grad_attn = jnp.concatenate(gather_ctx(grad_resid.astype(BF)), 0)
    grad_mixed = dot(grad_attn, wo_t).astype(BF)
    grad_grouped = grad_mixed.reshape(-1, kv_heads, group_size, head_dim)
    probs = jnp.exp(attend_scores() - log_total)
    grad_probs = jnp.einsum(
        "tkgd,skd->kgts", grad_grouped, value_rows, preferred_element_type=F32
    )
    value_part = jnp.einsum(
        "kgts,tkgd->skd", probs.astype(BF), grad_grouped, preferred_element_type=F32
    )
    inner_row = jnp.sum(probs * grad_probs, -1, keepdims=True)
    grad_scores = (probs * (grad_probs - inner_row)).astype(BF)
    grad_queries = (
        jnp.einsum("kgts,skd->tkgd", grad_scores, key_rows, preferred_element_type=F32) * scale_by
    )
    grad_keys = (
        jnp.einsum("kgts,tkgd->skd", grad_scores, grouped, preferred_element_type=F32) * scale_by
    )
    _, query_pull = jax.vjp(
        lambda v, g: head_prepare(v, g, cosine_table, sine_table, q_heads), q_pre, head_full[0]
    )
    grad_q_pre, grad_q_gain = query_pull(grad_queries.reshape(-1, q_heads, head_dim))
    _, key_pull = jax.vjp(
        lambda v, g: head_prepare(v, g, cosine_table, sine_table, kv_heads), k_pre, head_full[1]
    )
    grad_k_pre, grad_k_gain = key_pull(grad_keys)
    grad_qkv = jnp.concatenate(
        [grad_q_pre.astype(BF), grad_k_pre.astype(BF), value_part.reshape(-1, kv_cols).astype(BF)],
        1,
    )
    w_qkv = attn_w[:, : q_cols + 2 * kv_cols]
    grad_one_part = dot_nt(grad_qkv, w_qkv)
    _, first_pull = jax.vjp(rms_scale, inputs, gains_full[0])
    grad_gain_one = first_pull(grad_one_part)[1]
    grad_norm_one = scatter_ctx(split_parts(grad_one_part.astype(BF), 4))
    _, own_pull = jax.vjp(rms_scale, tokens.astype(F32), gains_full[0])
    input_grad = (grad_resid + own_pull(grad_norm_one)[0]).astype(BF)
    grad_attn_w = jnp.concatenate([dot_tn(normed_one, grad_qkv), dot_tn(grad_attn, attn_out)], 1)
    grad_q_out, grad_k_out, grad_v_out, grad_o_out = collect(
        grad_attn_w, (q_cols, kv_cols, kv_cols, q_cols)
    )
    small = jnp.concatenate([grad_gain_one, grad_gain_two, grad_q_gain, grad_k_gain])
    small = sum_all(small.reshape(1, -1), dp_size)[0]
    norm_total = small[: 2 * model_dim].reshape(2, model_dim)
    head_sum = small[2 * model_dim :].reshape(2, head_dim)
    norm_own = lax.dynamic_slice_in_dim(norm_total, lax.axis_index(ALL) * shard, shard, 1)
    return (
        layer_out[None],
        input_grad[None],
        grad_q_out,
        grad_k_out,
        grad_v_out,
        grad_o_out.T,
        grad_g_out,
        grad_u_out,
        grad_d_out.T,
        norm_own.astype(BF),
        head_sum.astype(BF),
    )


def solution(mesh):
    def step(*arrays):
        return on_device(mesh.shape["dp"], *arrays)

    in_specs = (
        P("dp", "ctx", None),
        P("dp", "ctx"),
        P(("dp", "ctx"), None),
        P(("dp", "ctx"), None),
        P(("dp", "ctx"), None),
        P(None, ("dp", "ctx")),
        P(("dp", "ctx"), None),
        P(("dp", "ctx"), None),
        P(None, ("dp", "ctx")),
        P(None, ("dp", "ctx")),
        P(),
        P("dp", "ctx", None),
    )
    out_specs = (
        P("dp", "ctx", None),
        P("dp", "ctx", None),
        P(("dp", "ctx"), None),
        P(("dp", "ctx"), None),
        P(("dp", "ctx"), None),
        P(None, ("dp", "ctx")),
        P(("dp", "ctx"), None),
        P(("dp", "ctx"), None),
        P(None, ("dp", "ctx")),
        P(None, ("dp", "ctx")),
        P(),
    )
    return jax.shard_map(step, mesh=mesh, in_specs=in_specs, out_specs=out_specs, check_vma=False)
```

```python
import functools

import jax
import jax.numpy as jnp
from jax import lax
from jax.experimental import pallas as pl
from jax.experimental.pallas import tpu as pltpu
from jax.sharding import PartitionSpec as P

EPS = 1e-05
THETA = 1000000.0
BF = jnp.bfloat16
F32 = jnp.float32
ALL = ("dp", "ctx")


def add_low(a, b):
    return (a.astype(F32) + b.astype(F32)).astype(BF)


def flip(value, axis, size, bits):
    return lax.ppermute(value, axis, [(i, i ^ bits) for i in range(size)])


def gather_ctx(own):
    core = flip(own, "ctx", 4, 1)
    across = flip(own, "ctx", 4, 2)
    return [own, core, across, flip(across, "ctx", 4, 1)]


def scatter_ctx(parts):
    far = flip(parts[3], "ctx", 4, 1)
    near = flip(parts[1], "ctx", 4, 1)
    far_sum = add_low(parts[2], far)
    far_in = flip(far_sum, "ctx", 4, 2)
    return parts[0], near, far_in


def sum_parts(parts):
    return parts[0].astype(F32) + parts[1].astype(F32) + parts[2].astype(F32)


def exchange_ctx(parts):
    return [parts[0]] + [flip(parts[j], "ctx", 4, j) for j in range(1, 4)]


def place(parts, where, axis):
    size = parts[0].shape[axis]
    shape = list(parts[0].shape)
    shape[axis] = size * len(parts)
    out = jnp.zeros(shape, parts[0].dtype)
    for part, at in zip(parts, where):
        out = lax.dynamic_update_slice_in_dim(out, part, at * size, axis)
    return out


def after(value, *events):
    return lax.optimization_barrier((value,) + events)[0]


def ordered(dp_size):
    return dp_size == 8


def dp_order(dp_size):
    me = lax.axis_index("dp")
    return [((me - 2 * (i // 2)) % dp_size) ^ (i % 2) for i in range(dp_size)]


def ring(value, size):
    return lax.ppermute(value, "dp", [(i, (i + 2) % size) for i in range(size)])


def gather_dp(block, size, events):
    if not ordered(size):
        return lax.all_gather(block, "dp", axis=0, tiled=True)
    parts = []
    for step in range(size // 2):
        block = after(block, *events[step])
        parts += [block, flip(block, "dp", size, 1)]
        if step + 1 < size // 2:
            block = ring(block, size)
    return parts


def scatter_dp(whole, size):
    if not ordered(size):
        return lax.psum_scatter(whole, "dp", scatter_dimension=0, tiled=True).astype(F32)
    rows = whole.shape[0] // size
    total = None
    for step in range(size // 2):
        at = 2 * ((step + 1) % (size // 2))
        near = flip(whole[(at + 1) * rows : (at + 2) * rows], "dp", size, 1)
        own = whole[at * rows : (at + 1) * rows].astype(F32) + near.astype(F32)
        if total is not None:
            own = own + ring(total, size).astype(F32)
        total = own.astype(BF)
    return own


def from_order(value, dp_size):
    if not ordered(dp_size):
        return value
    cols = value.shape[1] // dp_size
    parts = [value[:, i * cols : (i + 1) * cols] for i in range(dp_size)]
    return place(parts, dp_order(dp_size), 1)


def sum_all(value, dp_size):
    for bits in (1, 2):
        value = value + flip(value, "ctx", 4, bits)
    bits = 1
    while bits < dp_size:
        value = value + flip(value, "dp", dp_size, bits)
        bits *= 2
    return value


def dot(a, b):
    return lax.dot_general(a, b, (((1,), (0,)), ((), ())), preferred_element_type=F32)


def dot_nt(a, b):
    return lax.dot_general(a, b, (((1,), (1,)), ((), ())), preferred_element_type=F32)


def dot_tn(a, b):
    return lax.dot_general(a, b, (((0,), (0,)), ((), ())), preferred_element_type=F32)


VMEM = pl.BlockSpec(memory_space=pltpu.VMEM)
SMEM = pl.BlockSpec(memory_space=pltpu.SMEM)
LANES = 128
HIGH = lax.Precision.HIGHEST


def call(body, outs, ins, scratch=(), scalars=0, limit=32, flops=1000000):
    return pl.pallas_call(
        body,
        out_shape=[jax.ShapeDtypeStruct(shape, kind) for shape, kind in outs],
        in_specs=[SMEM] * scalars + [VMEM] * (len(ins) - scalars),
        out_specs=[VMEM] * len(outs),
        scratch_shapes=list(scratch),
        compiler_params=pltpu.CompilerParams(vmem_limit_bytes=limit << 20),
        cost_estimate=pl.CostEstimate(flops=flops, bytes_accessed=1000, transcendentals=0),
    )(*ins)


def pack_body(order_ref, tokens_ref, grad_ref, docs_ref, out_ref):
    rows = tokens_ref.shape[0]
    out_ref[:rows, :] = tokens_ref[...]
    out_ref[rows : 2 * rows, :] = grad_ref[...]
    out_ref[2 * rows :, :] = jnp.broadcast_to(
        docs_ref[...].astype(F32), (out_ref.shape[0] - 2 * rows, LANES)
    ).astype(BF)


def pack_inputs(order, tokens, out_grad, doc_row):
    rows, width = tokens.shape
    doc_blocks = rows // LANES
    moved = pl.BlockSpec((rows, LANES), lambda i, order_ref: (0, order_ref[i]))
    return pl.pallas_call(
        pack_body,
        out_shape=jax.ShapeDtypeStruct((2 * rows + 16, width), BF),
        grid_spec=pltpu.PrefetchScalarGridSpec(
            num_scalar_prefetch=1,
            grid=(width // LANES,),
            in_specs=[
                moved,
                moved,
                pl.BlockSpec((1, LANES), lambda i, order_ref: (0, lax.rem(i, doc_blocks))),
            ],
            out_specs=pl.BlockSpec((2 * rows + 16, LANES), lambda i, order_ref: (0, i)),
        ),
    )(order, tokens, out_grad, doc_row.reshape(1, -1))


def sum_body(order_ref, base_ref, one_ref, two_ref, three_ref, out_ref):
    total = one_ref[...].astype(F32) + two_ref[...].astype(F32) + three_ref[...].astype(F32)
    out_ref[...] = (base_ref[...] + total).astype(BF)


def sum_out(order, base, parts):
    rows, width = base.shape
    own = pl.BlockSpec((rows, LANES), lambda i, order_ref: (0, i))
    return pl.pallas_call(
        sum_body,
        out_shape=jax.ShapeDtypeStruct((rows, width), BF),
        grid_spec=pltpu.PrefetchScalarGridSpec(
            num_scalar_prefetch=1,
            grid=(width // LANES,),
            in_specs=[own] * 4,
            out_specs=pl.BlockSpec((rows, LANES), lambda i, order_ref: (0, order_ref[i])),
        ),
    )(order, base, *parts)


def lane_masks(rows):
    lane = lax.broadcasted_iota(jnp.int32, (rows, LANES), 1)
    return lane < 64, lax.rem(lane, 64) < 32


def half_sums(squares):
    row = lax.broadcasted_iota(jnp.int32, (LANES, LANES), 0) // 64
    col = lax.broadcasted_iota(jnp.int32, (LANES, LANES), 1) // 64
    return jnp.dot(
        squares, (row == col).astype(F32), preferred_element_type=F32, precision=HIGH
    )


def turn(value, first):
    return jnp.where(first, pltpu.roll(value, 96, 1), pltpu.roll(value, 32, 1))


def doubled(value, left):
    other = pltpu.roll(value, 64, 1)
    return jnp.where(left, value, other), jnp.where(left, other, value)


def prepare_body(rows, *refs):
    packs, blocks = refs[:4], refs[4:12]
    cos_ref, sin_ref, head_ref = refs[12:15]
    normed_ref, qk_pre_ref, q_ref, kd_ref, vd_ref, kt_ref, vt_ref = refs[15:22]
    wqkv_ref, wo_ref, gains_ref, all_ref = refs[22:26]
    for i, block in enumerate(blocks):
        at = i * LANES
        wqkv_ref[at : at + LANES, :] = block[:LANES, :512]
        wo_ref[at : at + LANES, :] = block[:LANES, 512:]
        gains_ref[:, at : at + LANES] = block[LANES : LANES + 8, :LANES].astype(F32)
    for j, pack in enumerate(packs):
        all_ref[j * rows : (j + 1) * rows, :] = pack[:rows, :]
    left, first = lane_masks(LANES)
    gain = gains_ref[0:1, :]
    q_gain, k_gain = head_ref[0:1, :], head_ref[1:2, :]

    def chunk(i, _):
        at = pl.ds(pl.multiple_of(i * LANES, LANES), LANES)
        x = all_ref[at, :].astype(F32)
        scale = lax.rsqrt(jnp.mean(x * x, -1, keepdims=True) + EPS)
        normed = (x * scale * gain).astype(BF)
        normed_ref[at, :] = normed
        pre = jnp.dot(normed, wqkv_ref[...], preferred_element_type=F32)
        qk_pre_ref[at, :] = pre[:, :384]
        cos, sin = cos_ref[at, :], sin_ref[at, :]
        turned = []
        for b in range(3):
            u = pre[:, b * LANES : (b + 1) * LANES]
            u = u * lax.rsqrt(half_sums(u * u) * (1.0 / 64) + EPS) * (k_gain if b == 2 else q_gain)
            turned.append(u * cos + turn(u, first) * sin)
        q_ref[0, at, :] = turned[0].astype(BF)
        q_ref[1, at, :] = turned[1].astype(BF)
        key, value = turned[2], pre[:, 384:]
        for both, flat, one in ((kd_ref, kt_ref, key), (vd_ref, vt_ref, value)):
            low, high = doubled(one, left)
            both[0, at, :] = low.astype(BF)
            both[1, at, :] = high.astype(BF)
            flat[:, at] = one.T.astype(BF)
        return 0

    lax.fori_loop(0, all_ref.shape[0] // LANES, chunk, 0)


def two_heads(block, left):
    zero = jnp.zeros_like(block)
    return jnp.concatenate([jnp.where(left, block, zero), jnp.where(left, zero, block)], 0)


def seen(start_row, first_key, rows, first_query):
    shape = (rows, 2 * rows)
    key = lax.broadcasted_iota(jnp.int32, shape, 0)
    mask = key + first_key >= start_row
    if first_query is not None:
        lane = lax.broadcasted_iota(jnp.int32, shape, 1)
        mask = mask & (key <= jnp.where(lane < rows, lane, lane - rows))
    return mask


LOG2E = 1.4426950408889634
SCORE = LOG2E / 8.0


def attend_body(rows, info_ref, q_ref, kd_ref, vt_ref, start_ref, wo_ref, *refs):
    parts = refs[:4]
    out_ref, wide_ref, lse_ref, sum_ref, acc_ref = refs[4:9]
    me = info_ref[0]
    left = lax.broadcasted_iota(jnp.int32, (rows, LANES), 1) < 64

    def one(step, _):
        kv, a = step // 4, lax.rem(step, 4)
        at_q = pl.ds(pl.multiple_of((a ^ me) * rows, rows), rows)
        q2 = two_heads(q_ref[kv, at_q, :], left)
        start_row = start_ref[a ^ me]
        sum_ref[...] = jnp.zeros_like(sum_ref)
        acc_ref[...] = jnp.zeros_like(acc_ref)
        for d in range(3):

            @pl.when((a >= d) & (info_ref[1 + a] < (a - d + 1) * rows))
            def _():
                at_k = pl.ds(pl.multiple_of(((a - d) ^ me) * rows, rows), rows)
                scores = dot_nt(kd_ref[kv, at_k, :], q2)
                mask = seen(start_row, (a - d) * rows, rows, a if d == 0 else None)
                p = jnp.where(mask, jnp.exp2(scores * SCORE), 0.0)
                sum_ref[...] += jnp.sum(p, 0, keepdims=True)
                half = pl.ds(pl.multiple_of(kv * 64, 64), 64)
                acc_ref[...] += dot(vt_ref[half, at_k], p.astype(BF))

        total = sum_ref[...]
        lse_ref[kv * 4 + (a ^ me)] = jnp.log2(total)
        mixed = acc_ref[...] / total
        mixed = jnp.concatenate([mixed[:, :rows], mixed[:, rows:]], 0).T
        wide_ref[kv, at_q, :] = mixed
        out_ref[kv, at_q, :] = mixed.astype(BF)
        return 0

    lax.fori_loop(0, 8, one, 0)
    for j in range(4):
        at = slice(j * rows, (j + 1) * rows)
        both = jnp.concatenate([out_ref[0, at, :], out_ref[1, at, :]], 1)
        parts[j][...] = dot_nt(both, wo_ref[...]).astype(BF)


def attend_back_body(rows, *refs):
    info_ref, g0, g1, g2, g3, q_ref, kd_ref, vd_ref, kt_ref, start_ref, wide_ref, lse_ref = refs[:12]
    qk_pre_ref, cos_ref, sin_ref, head_ref, wqkv_ref, wo_ref = refs[12:18]
    parts, low_ref, head_sum_ref = refs[18:22], refs[22], refs[23]
    mixed_ref, dq_ref, dk_ref, dv_ref, acc_ref = refs[24:29]
    me = info_ref[0]
    left = lax.broadcasted_iota(jnp.int32, (rows, LANES), 1) < 64
    for j, g in enumerate((g0, g1, g2, g3)):
        grad = dot(g[...], wo_ref[...]).astype(BF)
        mixed_ref[0, j * rows : (j + 1) * rows, :] = grad[:, :LANES]
        mixed_ref[1, j * rows : (j + 1) * rows, :] = grad[:, LANES:]
    dk_ref[...] = jnp.zeros_like(dk_ref)
    dv_ref[...] = jnp.zeros_like(dv_ref)
    pick = (
        lax.broadcasted_iota(jnp.int32, (8, LANES), 1) // 64
        == lax.broadcasted_iota(jnp.int32, (8, LANES), 0)
    ).astype(F32)

    def one(step, _):
        kv, a = step // 4, lax.rem(step, 4)
        at_q = pl.ds(pl.multiple_of((a ^ me) * rows, rows), rows)
        q2 = two_heads(q_ref[kv, at_q, :], left)
        grad = mixed_ref[kv, at_q, :]
        g2 = two_heads(grad, left)
        inner = lax.dot_general(
            pick,
            grad.astype(F32) * wide_ref[kv, at_q, :],
            (((1,), (1,)), ((), ())),
            preferred_element_type=F32,
            precision=HIGH,
        )
        inner = jnp.concatenate([inner[0:1], inner[1:2]], 1)
        lse = lse_ref[kv * 4 + (a ^ me)]
        start_row = start_ref[a ^ me]
        acc_ref[...] = jnp.zeros_like(acc_ref)
        for d in range(3):

            @pl.when((a >= d) & (info_ref[1 + a] < (a - d + 1) * rows))
            def _():
                at_k = pl.ds(pl.multiple_of(((a - d) ^ me) * rows, rows), rows)
                scores = dot_nt(kd_ref[kv, at_k, :], q2)
                mask = seen(start_row, (a - d) * rows, rows, a if d == 0 else None)
                p = jnp.where(mask, jnp.exp2(scores * SCORE - lse), 0.0)
                gp = dot_nt(vd_ref[kv, at_k, :], g2)
                gs = (p * (gp - inner)).astype(BF)
                dv_ref[kv, at_k, :] += dot(p.astype(BF), g2)
                dk_ref[kv, at_k, :] += dot(gs, q2)
                half = pl.ds(pl.multiple_of(kv * 64, 64), 64)
                acc_ref[...] += dot(kt_ref[half, at_k], gs)

        both = acc_ref[...] * 0.125
        dq_ref[kv, at_q, :] = jnp.concatenate([both[:, :rows], both[:, rows:]], 0).T
        return 0

    lax.fori_loop(0, 8, one, 0)
    left, first = lane_masks(LANES)
    head_sum_ref[...] = jnp.zeros_like(head_sum_ref)

    def folded(ref, at):
        low, high = ref[0, at, :], ref[1, at, :]
        low, high = low + pltpu.roll(low, 64, 1), high + pltpu.roll(high, 64, 1)
        return jnp.where(left, low, high)

    def chunk(i, _):
        at = pl.ds(pl.multiple_of(i * LANES, LANES), LANES)
        cos, sin = cos_ref[at, :], sin_ref[at, :]
        for b in range(3):
            u = qk_pre_ref[at, b * LANES : (b + 1) * LANES]
            g = folded(dk_ref, at) * 0.125 if b == 2 else dq_ref[b, at, :]
            w = g * cos - turn(g, first) * sin
            row = 1 if b == 2 else 0
            gain = head_ref[row : row + 1, :]
            r = lax.rsqrt(half_sums(u * u) * (1.0 / 64) + EPS)
            head_sum_ref[row : row + 1, :] += jnp.sum(w * u * r, 0, keepdims=True)
            w = w * gain
            back = r * w - u * (r * r * r) * (half_sums(w * u) * (1.0 / 64))
            low_ref[at, b * LANES : (b + 1) * LANES] = back.astype(BF)
        low_ref[at, 384:] = folded(dv_ref, at).astype(BF)
        return 0

    lax.fori_loop(0, low_ref.shape[0] // LANES, chunk, 0)
    for j in range(4):
        grad = dot_nt(low_ref[j * rows : (j + 1) * rows, :], wqkv_ref[...])
        parts[j][...] = grad.astype(BF)


def rms_scale(values, gain_row):
    return values * lax.rsqrt(jnp.mean(values * values, -1, keepdims=True) + EPS) * gain_row


def split_parts(tall, count):
    rows = tall.shape[0] // count
    return [lax.slice_in_dim(tall, j * rows, (j + 1) * rows, axis=0) for j in range(count)]


def on_device(
    dp_size,
    tokens,
    doc_ids,
    w_query,
    key_weight,
    value_weight,
    w_output,
    w_gate,
    w_up,
    w_down,
    norm_gains,
    head_norm_gains,
    out_grad,
):
    local_len, model_dim = tokens.shape[1:]
    tokens, out_grad, doc_row = tokens[0], out_grad[0], doc_ids[0]
    head_dim = head_norm_gains.shape[1]
    q_cols, kv_cols = w_query.shape[1] // 4, key_weight.shape[1] // 4
    shard = norm_gains.shape[1]
    ff_cols = w_gate.shape[1] // 4
    me = lax.axis_index("ctx")
    places = [me ^ j for j in range(4)]
    full_len = 4 * local_len
    block_order = jnp.stack(dp_order(dp_size)) if ordered(dp_size) else jnp.arange(8)
    block_order = block_order.astype(jnp.int32)

    def pieces_of(weights):
        sent = []
        for at in places:
            cut = [
                lax.dynamic_slice_in_dim(w, at * (w.shape[1] // 4), w.shape[1] // 4, 1)
                for w in weights
            ]
            sent.append(jnp.concatenate(cut, 1))
        return sent

    wide = 2 * q_cols + 2 * kv_cols
    sent = pieces_of([w_query, key_weight, value_weight, w_output.T])
    extra = jnp.pad(norm_gains, ((0, 6), (0, wide - shard)))
    got = exchange_ctx([jnp.concatenate([p, extra], 0) for p in sent])
    gains_block = place([g[shard : shard + 2, :shard] for g in got], places, 1)
    block = jnp.concatenate(
        [
            place([g[:shard] for g in got], places, 0),
            jnp.pad(gains_block, ((0, 6), (0, wide - 4 * shard))),
        ],
        0,
    )
    pack = pack_inputs(block_order, tokens, out_grad, doc_row)
    packs = gather_ctx(pack)
    blocks = gather_dp(block, dp_size, [()] * 4)
    if not ordered(dp_size):
        rows = 4 * shard + 8
        blocks = blocks.reshape(dp_size, rows, wide)
        whole_w = blocks[:, : 4 * shard].reshape(8, LANES, wide)
        whole_g = blocks[:, 4 * shard :, : 4 * shard].transpose(1, 0, 2).reshape(8, 8, LANES)
        whole_g = jnp.pad(whole_g.transpose(1, 0, 2), ((0, 0), (0, 0), (0, wide - LANES)))
        blocks = [jnp.concatenate([whole_w[i], whole_g[i]], 0) for i in range(8)]
    ff_sent = pieces_of([w_gate, w_up, w_down.T])
    ff_block = place(exchange_ctx([after(p, pack) for p in ff_sent]), places, 0)

    docs = jnp.concatenate([p[2 * local_len, :local_len] for p in packs])
    index = jnp.concatenate(
        [at * local_len + jnp.arange(local_len, dtype=jnp.int32) for at in places]
    )
    starts = jnp.sum((docs[None, :] < docs[:, None]).astype(jnp.int32), -1)
    positions = (index - starts).astype(F32)
    half = head_dim // 2
    lane = jnp.arange(LANES)
    freqs = THETA ** (-(2.0 * (lane % half).astype(F32)) / head_dim)
    angles = positions[:, None] * freqs
    cosine = jnp.cos(angles)
    sine = jnp.sin(angles) * jnp.where(lane % head_dim < half, -1.0, 1.0)
    starts = starts.reshape(4, local_len)
    info = jnp.concatenate([me[None], jnp.stack([starts[at, 0] for at in places])])
    info = info.astype(jnp.int32)
    starts = jnp.concatenate([starts, starts], 1).reshape(4, 1, 2 * local_len)
    head_gains = jnp.concatenate([head_norm_gains, head_norm_gains], 1).astype(F32)

    normed_one, qk_pre, queries, keys, values, keys_t, values_t, w_qkv, wo_t, gains = call(
        functools.partial(prepare_body, local_len),
        [
            ((full_len, model_dim), BF),
            ((full_len, q_cols + kv_cols), F32),
            ((2, full_len, LANES), BF),
            ((2, full_len, LANES), BF),
            ((2, full_len, LANES), BF),
            ((LANES, full_len), BF),
            ((LANES, full_len), BF),
            ((model_dim, q_cols + 2 * kv_cols), BF),
            ((model_dim, q_cols), BF),
            ((8, model_dim), F32),
        ],
        [*packs, *blocks, cosine, sine, head_gains],
        [pltpu.VMEM((full_len, model_dim), BF)],
    )
    *resid_parts, attn_out, attn_wide, lse = call(
        functools.partial(attend_body, local_len),
        [((local_len, model_dim), BF)] * 4
        + [
            ((2, full_len, LANES), BF),
            ((2, full_len, LANES), F32),
            ((8, 1, 2 * local_len), F32),
        ],
        [info, queries, keys, values_t, starts, wo_t],
        [pltpu.VMEM((1, 2 * local_len), F32), pltpu.VMEM((head_dim, 2 * local_len), F32)],
        scalars=1,
    )
    attn_out = jnp.concatenate([attn_out[0], attn_out[1]], 1)
    ff_w = gather_dp(ff_block, dp_size, [(w_qkv,), (w_qkv,), (lse,), (lse,)])
    if ordered(dp_size):
        ff_w = jnp.concatenate(ff_w, 0)
    wg, wu, wd_t = ff_w[:, :ff_cols], ff_w[:, ff_cols : 2 * ff_cols], ff_w[:, 2 * ff_cols :]
    own_tokens = pack[:local_len].astype(F32)
    own_grad = pack[local_len : 2 * local_len].astype(F32)
    all_grad = jnp.concatenate([p[local_len : 2 * local_len] for p in packs], 0)
    resid = own_tokens + sum_parts(scatter_ctx(resid_parts))
    normed_own = rms_scale(resid, gains[1]).astype(BF)
    normed_two = jnp.concatenate(gather_ctx(normed_own), 0)

    gate_act = dot(normed_two, wg)
    up_act = dot(normed_two, wu)
    hidden = (jax.nn.silu(gate_act) * up_act).astype(BF)
    grad_hidden = dot(all_grad, wd_t)
    _, gate_pull = jax.vjp(lambda g, u: jax.nn.silu(g) * u, gate_act, up_act)
    grad_gate_full, grad_up_full = gate_pull(grad_hidden)
    grad_gate = grad_gate_full.astype(BF)
    grad_up = grad_up_full.astype(BF)
    grad_two_part = (dot_nt(grad_gate, wg) + dot_nt(grad_up, wu)).astype(BF)
    grad_norm_two = sum_parts(scatter_ctx(split_parts(grad_two_part, 4)))
    _, second_pull = jax.vjp(rms_scale, resid, gains[1])
    grad_resid_norm, grad_gain_two = second_pull(grad_norm_two)
    grad_resid = own_grad + grad_resid_norm
    down_part = dot_nt(hidden, wd_t).astype(BF)
    layer_out = sum_out(block_order, resid, scatter_ctx(split_parts(down_part, 4)))

    def collect(whole, widths):
        mine = scatter_dp(whole.astype(BF), dp_size).astype(BF)
        sent = [lax.dynamic_slice_in_dim(mine, at * shard, shard, 0) for at in places]
        got = exchange_ctx(sent)
        outs, start = [], 0
        for width in widths:
            cut = [g[:, start : start + width] for g in got]
            outs.append(place(cut, places, 1))
            start += width
        return outs

    (grad_d_out,) = collect(dot_tn(all_grad, hidden), (ff_cols,))
    grad_gate_up = jnp.concatenate([grad_gate, grad_up], 1)
    grad_g_out, grad_u_out = collect(dot_tn(normed_two, grad_gate_up), (ff_cols, ff_cols))

    grad_attn = gather_ctx(grad_resid.astype(BF))
    *one_parts, grad_qkv, head_sums = call(
        functools.partial(attend_back_body, local_len),
        [((local_len, model_dim), BF)] * 4
        + [((full_len, q_cols + 2 * kv_cols), BF), ((8, LANES), F32)],
        [
            info,
            *grad_attn,
            queries,
            keys,
            values,
            keys_t,
            starts,
            attn_wide,
            lse,
            qk_pre,
            cosine,
            sine,
            head_gains,
            w_qkv,
            wo_t,
        ],
        [
            pltpu.VMEM((2, full_len, LANES), BF),
            pltpu.VMEM((2, full_len, LANES), F32),
            pltpu.VMEM((2, full_len, LANES), F32),
            pltpu.VMEM((2, full_len, LANES), F32),
            pltpu.VMEM((head_dim, 2 * local_len), F32),
        ],
        scalars=1,
    )
    grad_norm_one = sum_parts(scatter_ctx(one_parts))
    _, first_pull = jax.vjp(rms_scale, own_tokens, gains[0])
    grad_input_norm, grad_gain_one = first_pull(grad_norm_one)
    input_grad = from_order((grad_resid + grad_input_norm).astype(BF), dp_size)
    grad_attn = jnp.concatenate(grad_attn, 0)
    grad_attn_w = jnp.concatenate([dot_tn(normed_one, grad_qkv), dot_tn(grad_attn, attn_out)], 1)
    grad_q_out, grad_k_out, grad_v_out, grad_o_out = collect(
        grad_attn_w, (q_cols, kv_cols, kv_cols, q_cols)
    )
    head_sums = head_sums[:2, :head_dim] + head_sums[:2, head_dim:]
    gain_rows = from_order(jnp.stack([grad_gain_one, grad_gain_two]), dp_size)
    small = jnp.concatenate([gain_rows.reshape(-1), head_sums.reshape(-1)])
    small = sum_all(small.reshape(1, -1), dp_size)[0]
    norm_total = small[: 2 * model_dim].reshape(2, model_dim)
    head_sum = small[2 * model_dim :].reshape(2, head_dim)
    norm_own = lax.dynamic_slice_in_dim(norm_total, lax.axis_index(ALL) * shard, shard, 1)
    return (
        layer_out[None],
        input_grad[None],
        grad_q_out,
        grad_k_out,
        grad_v_out,
        grad_o_out.T,
        grad_g_out,
        grad_u_out,
        grad_d_out.T,
        norm_own.astype(BF),
        head_sum.astype(BF),
    )


def solution(mesh):
    def step(*arrays):
        return on_device(mesh.shape["dp"], *arrays)

    in_specs = (
        P("dp", "ctx", None),
        P("dp", "ctx"),
        P(("dp", "ctx"), None),
        P(("dp", "ctx"), None),
        P(("dp", "ctx"), None),
        P(None, ("dp", "ctx")),
        P(("dp", "ctx"), None),
        P(("dp", "ctx"), None),
        P(None, ("dp", "ctx")),
        P(None, ("dp", "ctx")),
        P(),
        P("dp", "ctx", None),
    )
    out_specs = (
        P("dp", "ctx", None),
        P("dp", "ctx", None),
        P(("dp", "ctx"), None),
        P(("dp", "ctx"), None),
        P(("dp", "ctx"), None),
        P(None, ("dp", "ctx")),
        P(("dp", "ctx"), None),
        P(("dp", "ctx"), None),
        P(None, ("dp", "ctx")),
        P(None, ("dp", "ctx")),
        P(),
    )
    return jax.shard_map(step, mesh=mesh, in_specs=in_specs, out_specs=out_specs, check_vma=False)
```

```python
import functools

import jax
import jax.numpy as jnp
from jax import lax
from jax.experimental import pallas as pl
from jax.experimental.pallas import tpu as pltpu
from jax.sharding import PartitionSpec as P

EPS = 1e-05
THETA = 1000000.0
BF = jnp.bfloat16
F32 = jnp.float32
ALL = ("dp", "ctx")


def add_low(*terms):
    total = terms[0].astype(F32)
    for term in terms[1:]:
        total = total + term.astype(F32)
    return total.astype(BF)


def flip(value, axis, size, bits):
    return lax.ppermute(value, axis, [(i, i ^ bits) for i in range(size)])


def gather_ctx(own):
    core = flip(own, "ctx", 4, 1)
    across = flip(own, "ctx", 4, 2)
    return [own, core, across, flip(across, "ctx", 4, 1)]


def scatter_ctx(parts):
    far = flip(parts[3], "ctx", 4, 1)
    near = flip(parts[1], "ctx", 4, 1)
    far_sum = add_low(parts[2], far)
    far_in = flip(far_sum, "ctx", 4, 2)
    return parts[0], near, far_in


def sum_parts(parts):
    return parts[0].astype(F32) + parts[1].astype(F32) + parts[2].astype(F32)


def exchange_ctx(parts):
    return [parts[0]] + [flip(parts[j], "ctx", 4, j) for j in range(1, 4)]


def place(parts, where, axis):
    size = parts[0].shape[axis]
    shape = list(parts[0].shape)
    shape[axis] = size * len(parts)
    out = jnp.zeros(shape, parts[0].dtype)
    for part, at in zip(parts, where):
        out = lax.dynamic_update_slice_in_dim(out, part, at * size, axis)
    return out


def after(values, events):
    values = tuple(values)
    return list(lax.optimization_barrier(values + tuple(events))[: len(values)])


def ordered(dp_size):
    return dp_size == 8


def dp_order(dp_size):
    me = lax.axis_index("dp")
    return [((me - 2 * (i % 4)) % dp_size) ^ (i // 4) for i in range(dp_size)]


def across_y(value):
    return flip(value, "dp", 8, 1)


def along_z(value):
    return lax.ppermute(value, "dp", [(i, (i + 2) % 8) for i in range(8)])


def gather_blocks(block, level):
    zs, ys, arrived = [block], [], []
    for hop in range(3):
        ys.append(across_y(zs[-1]))
        zs.append(along_z(zs[-1]))
        arrived.append((ys[-1], zs[-1]))
    if level:
        half = block.shape[0] // 2
        last = [across_y(zs[3][:half]), along_z(ys[2][half:])]
    else:
        last = [across_y(zs[3])]
    arrived.append(tuple(last))
    return zs + ys + last, arrived


def scatter_blocks(chunks, level, gate=None):
    near, far = chunks[:4], chunks[4:]
    half = near[0].shape[0] // 2
    if level:
        first = across_y(far[1][:half])
        early = along_z(far[1][half:])
        second = jnp.concatenate([far[2][:half], add_low(far[2][half:], early)], 0)
        total = jnp.concatenate([add_low(near[1][:half], first), near[1][half:]], 0)
    else:
        second = far[2]
        total = add_low(near[1], across_y(far[1]))
    stages = [(total, second)]
    for mine, other in ((near[2], second), (near[3], far[3])):
        total = add_low(mine, across_y(other), along_z(total))
        stages.append((total,))
    return (near[0], across_y(far[0]), along_z(total)), stages


def sum_all(value, dp_size):
    for bits in (1, 2):
        value = value + flip(value, "ctx", 4, bits)
    bits = 1
    while bits < dp_size:
        value = value + flip(value, "dp", dp_size, bits)
        bits *= 2
    return value


def dot(a, b):
    return lax.dot_general(a, b, (((1,), (0,)), ((), ())), preferred_element_type=F32)


def dot_nt(a, b):
    return lax.dot_general(a, b, (((1,), (1,)), ((), ())), preferred_element_type=F32)


def dot_tn(a, b):
    return lax.dot_general(a, b, (((0,), (0,)), ((), ())), preferred_element_type=F32)


VMEM = pl.BlockSpec(memory_space=pltpu.VMEM)
SMEM = pl.BlockSpec(memory_space=pltpu.SMEM)
LANES = 128
HIGH = lax.Precision.HIGHEST


def call(body, outs, ins, scratch=(), scalars=0, limit=32, flops=1000000):
    return pl.pallas_call(
        body,
        out_shape=[jax.ShapeDtypeStruct(shape, kind) for shape, kind in outs],
        in_specs=[SMEM] * scalars + [VMEM] * (len(ins) - scalars),
        out_specs=[VMEM] * len(outs),
        scratch_shapes=list(scratch),
        compiler_params=pltpu.CompilerParams(vmem_limit_bytes=limit << 20),
        cost_estimate=pl.CostEstimate(flops=flops, bytes_accessed=1000, transcendentals=0),
    )(*ins)


def pack_body(order_ref, tokens_ref, grad_ref, docs_ref, out_ref):
    rows = tokens_ref.shape[0]
    out_ref[:rows, :] = tokens_ref[...]
    out_ref[rows : 2 * rows, :] = grad_ref[...]
    out_ref[2 * rows :, :] = jnp.broadcast_to(
        docs_ref[...].astype(F32), (out_ref.shape[0] - 2 * rows, LANES)
    ).astype(BF)


def pack_inputs(order, tokens, out_grad, doc_row):
    rows, width = tokens.shape
    doc_blocks = rows // LANES
    moved = pl.BlockSpec((rows, LANES), lambda i, order_ref: (0, order_ref[i]))
    return pl.pallas_call(
        pack_body,
        out_shape=jax.ShapeDtypeStruct((2 * rows + 16, width), BF),
        grid_spec=pltpu.PrefetchScalarGridSpec(
            num_scalar_prefetch=1,
            grid=(width // LANES,),
            in_specs=[
                moved,
                moved,
                pl.BlockSpec((1, LANES), lambda i, order_ref: (0, lax.rem(i, doc_blocks))),
            ],
            out_specs=pl.BlockSpec((2 * rows + 16, LANES), lambda i, order_ref: (0, i)),
        ),
    )(order, tokens, out_grad, doc_row.reshape(1, -1))


def sum_body(order_ref, base_ref, one_ref, two_ref, three_ref, out_ref):
    total = one_ref[...].astype(F32) + two_ref[...].astype(F32) + three_ref[...].astype(F32)
    out_ref[...] = (base_ref[...] + total).astype(BF)


def sum_out(order, base, parts):
    rows, width = base.shape
    own = pl.BlockSpec((rows, LANES), lambda i, order_ref: (0, i))
    return pl.pallas_call(
        sum_body,
        out_shape=jax.ShapeDtypeStruct((rows, width), BF),
        grid_spec=pltpu.PrefetchScalarGridSpec(
            num_scalar_prefetch=1,
            grid=(width // LANES,),
            in_specs=[own] * 4,
            out_specs=pl.BlockSpec((rows, LANES), lambda i, order_ref: (0, order_ref[i])),
        ),
    )(order, base, *parts)


def lane_masks(rows):
    lane = lax.broadcasted_iota(jnp.int32, (rows, LANES), 1)
    return lane < 64, lax.rem(lane, 64) < 32


def half_sums(squares):
    row = lax.broadcasted_iota(jnp.int32, (LANES, LANES), 0) // 64
    col = lax.broadcasted_iota(jnp.int32, (LANES, LANES), 1) // 64
    return jnp.dot(
        squares, (row == col).astype(F32), preferred_element_type=F32, precision=HIGH
    )


def turn(value, first):
    return jnp.where(first, pltpu.roll(value, 96, 1), pltpu.roll(value, 32, 1))


def doubled(value, left):
    other = pltpu.roll(value, 64, 1)
    return jnp.where(left, value, other), jnp.where(left, other, value)


def prepare_body(rows, *refs):
    packs, blocks = refs[:4], refs[4:12]
    cos_ref, sin_ref, head_ref = refs[12:15]
    normed_ref, qk_pre_ref, q_ref, kd_ref, vd_ref, kt_ref, vt_ref = refs[15:22]
    wqkv_ref, wo_ref, gains_ref, all_ref = refs[22:26]
    for i, block in enumerate(blocks):
        at = i * LANES
        wqkv_ref[at : at + LANES, :] = block[:LANES, :512]
        wo_ref[at : at + LANES, :] = block[:LANES, 512:]
        gains_ref[:, at : at + LANES] = block[LANES : LANES + 8, :LANES].astype(F32)
    for j, pack in enumerate(packs):
        all_ref[j * rows : (j + 1) * rows, :] = pack[:rows, :]
    left, first = lane_masks(LANES)
    gain = gains_ref[0:1, :]
    q_gain, k_gain = head_ref[0:1, :], head_ref[1:2, :]

    def chunk(i, _):
        at = pl.ds(pl.multiple_of(i * LANES, LANES), LANES)
        x = all_ref[at, :].astype(F32)
        scale = lax.rsqrt(jnp.mean(x * x, -1, keepdims=True) + EPS)
        normed = (x * scale * gain).astype(BF)
        normed_ref[at, :] = normed
        pre = jnp.dot(normed, wqkv_ref[...], preferred_element_type=F32)
        qk_pre_ref[at, :] = pre[:, :384]
        cos, sin = cos_ref[at, :], sin_ref[at, :]
        turned = []
        for b in range(3):
            u = pre[:, b * LANES : (b + 1) * LANES]
            u = u * lax.rsqrt(half_sums(u * u) * (1.0 / 64) + EPS) * (k_gain if b == 2 else q_gain)
            turned.append(u * cos + turn(u, first) * sin)
        q_ref[0, at, :] = turned[0].astype(BF)
        q_ref[1, at, :] = turned[1].astype(BF)
        key, value = turned[2], pre[:, 384:]
        for both, flat, one in ((kd_ref, kt_ref, key), (vd_ref, vt_ref, value)):
            low, high = doubled(one, left)
            both[0, at, :] = low.astype(BF)
            both[1, at, :] = high.astype(BF)
            flat[:, at] = one.T.astype(BF)
        return 0

    lax.fori_loop(0, all_ref.shape[0] // LANES, chunk, 0)


def two_heads(block, left):
    zero = jnp.zeros_like(block)
    return jnp.concatenate([jnp.where(left, block, zero), jnp.where(left, zero, block)], 0)


def seen(start_row, first_key, rows, first_query):
    shape = (rows, 2 * rows)
    key = lax.broadcasted_iota(jnp.int32, shape, 0)
    mask = key + first_key >= start_row
    if first_query is not None:
        lane = lax.broadcasted_iota(jnp.int32, shape, 1)
        mask = mask & (key <= jnp.where(lane < rows, lane, lane - rows))
    return mask


LOG2E = 1.4426950408889634
SCORE = LOG2E / 8.0


def attend_body(rows, info_ref, q_ref, kd_ref, vt_ref, start_ref, wo_ref, *refs):
    parts = refs[:4]
    out_ref, wide_ref, lse_ref, sum_ref, acc_ref = refs[4:9]
    me = info_ref[0]
    left = lax.broadcasted_iota(jnp.int32, (rows, LANES), 1) < 64

    def one(step, _):
        kv, a = step // 4, lax.rem(step, 4)
        at_q = pl.ds(pl.multiple_of((a ^ me) * rows, rows), rows)
        q2 = two_heads(q_ref[kv, at_q, :], left)
        start_row = start_ref[a ^ me]
        sum_ref[...] = jnp.zeros_like(sum_ref)
        acc_ref[...] = jnp.zeros_like(acc_ref)
        for d in range(3):

            @pl.when((a >= d) & (info_ref[1 + a] < (a - d + 1) * rows))
            def _():
                at_k = pl.ds(pl.multiple_of(((a - d) ^ me) * rows, rows), rows)
                scores = dot_nt(kd_ref[kv, at_k, :], q2)
                mask = seen(start_row, (a - d) * rows, rows, a if d == 0 else None)
                p = jnp.where(mask, jnp.exp2(scores * SCORE), 0.0)
                sum_ref[...] += jnp.sum(p, 0, keepdims=True)
                half = pl.ds(pl.multiple_of(kv * 64, 64), 64)
                acc_ref[...] += dot(vt_ref[half, at_k], p.astype(BF))

        total = sum_ref[...]
        lse_ref[kv * 4 + (a ^ me)] = jnp.log2(total)
        mixed = acc_ref[...] / total
        mixed = jnp.concatenate([mixed[:, :rows], mixed[:, rows:]], 0).T
        wide_ref[kv, at_q, :] = mixed
        out_ref[at_q, columns(kv, LANES)] = mixed.astype(BF)
        return 0

    lax.fori_loop(0, 8, one, 0)
    for j in range(4):
        at = slice(j * rows, (j + 1) * rows)
        parts[j][...] = dot_nt(out_ref[at, :], wo_ref[...]).astype(BF)


def attend_back_body(rows, *refs):
    info_ref, g0, g1, g2, g3, q_ref, kd_ref, vd_ref, kt_ref, start_ref, wide_ref, lse_ref = refs[:12]
    qk_pre_ref, cos_ref, sin_ref, head_ref, wqkv_ref, wo_ref, normed_ref, gains_ref = refs[12:20]
    parts, low_ref, head_sum_ref, gain_sum_ref, grad_ref = refs[20:24], *refs[24:28]
    mixed_ref, dq_ref, dk_ref, dv_ref, acc_ref = refs[28:33]
    me = info_ref[0]
    left = lax.broadcasted_iota(jnp.int32, (rows, LANES), 1) < 64
    for j, g in enumerate((g0, g1, g2, g3)):
        grad_ref[j * rows : (j + 1) * rows, :] = g[...]
        grad = dot(g[...], wo_ref[...]).astype(BF)
        mixed_ref[0, j * rows : (j + 1) * rows, :] = grad[:, :LANES]
        mixed_ref[1, j * rows : (j + 1) * rows, :] = grad[:, LANES:]
    dk_ref[...] = jnp.zeros_like(dk_ref)
    dv_ref[...] = jnp.zeros_like(dv_ref)
    pick = (
        lax.broadcasted_iota(jnp.int32, (8, LANES), 1) // 64
        == lax.broadcasted_iota(jnp.int32, (8, LANES), 0)
    ).astype(F32)

    def one(step, _):
        kv, a = step // 4, lax.rem(step, 4)
        at_q = pl.ds(pl.multiple_of((a ^ me) * rows, rows), rows)
        q2 = two_heads(q_ref[kv, at_q, :], left)
        grad = mixed_ref[kv, at_q, :]
        g2 = two_heads(grad, left)
        inner = lax.dot_general(
            pick,
            grad.astype(F32) * wide_ref[kv, at_q, :],
            (((1,), (1,)), ((), ())),
            preferred_element_type=F32,
            precision=HIGH,
        )
        inner = jnp.concatenate([inner[0:1], inner[1:2]], 1)
        lse = lse_ref[kv * 4 + (a ^ me)]
        start_row = start_ref[a ^ me]
        acc_ref[...] = jnp.zeros_like(acc_ref)
        for d in range(3):

            @pl.when((a >= d) & (info_ref[1 + a] < (a - d + 1) * rows))
            def _():
                at_k = pl.ds(pl.multiple_of(((a - d) ^ me) * rows, rows), rows)
                scores = dot_nt(kd_ref[kv, at_k, :], q2)
                mask = seen(start_row, (a - d) * rows, rows, a if d == 0 else None)
                p = jnp.where(mask, jnp.exp2(scores * SCORE - lse), 0.0)
                gp = dot_nt(vd_ref[kv, at_k, :], g2)
                gs = (p * (gp - inner)).astype(BF)
                dv_ref[kv, at_k, :] += dot(p.astype(BF), g2)
                dk_ref[kv, at_k, :] += dot(gs, q2)
                half = pl.ds(pl.multiple_of(kv * 64, 64), 64)
                acc_ref[...] += dot(kt_ref[half, at_k], gs)

        both = acc_ref[...] * 0.125
        dq_ref[kv, at_q, :] = jnp.concatenate([both[:, :rows], both[:, rows:]], 0).T
        return 0

    lax.fori_loop(0, 8, one, 0)
    left, first = lane_masks(LANES)
    head_sum_ref[...] = jnp.zeros_like(head_sum_ref)

    def folded(ref, at):
        low, high = ref[0, at, :], ref[1, at, :]
        low, high = low + pltpu.roll(low, 64, 1), high + pltpu.roll(high, 64, 1)
        return jnp.where(left, low, high)

    def chunk(i, _):
        at = pl.ds(pl.multiple_of(i * LANES, LANES), LANES)
        cos, sin = cos_ref[at, :], sin_ref[at, :]
        for b in range(3):
            u = qk_pre_ref[at, b * LANES : (b + 1) * LANES]
            g = folded(dk_ref, at) * 0.125 if b == 2 else dq_ref[b, at, :]
            w = g * cos - turn(g, first) * sin
            row = 1 if b == 2 else 0
            gain = head_ref[row : row + 1, :]
            r = lax.rsqrt(half_sums(u * u) * (1.0 / 64) + EPS)
            head_sum_ref[row : row + 1, :] += jnp.sum(w * u * r, 0, keepdims=True)
            w = w * gain
            back = r * w - u * (r * r * r) * (half_sums(w * u) * (1.0 / 64))
            low_ref[at, b * LANES : (b + 1) * LANES] = back.astype(BF)
        low_ref[at, 384:] = folded(dv_ref, at).astype(BF)
        return 0

    lax.fori_loop(0, low_ref.shape[0] // LANES, chunk, 0)
    gain_sum = jnp.zeros((1, normed_ref.shape[1]), F32)
    for j in range(4):
        at = slice(j * rows, (j + 1) * rows)
        grad = dot_nt(low_ref[at, :], wqkv_ref[...])
        parts[j][...] = grad.astype(BF)
        gain_sum = gain_sum + jnp.sum(grad * normed_ref[at, :].astype(F32), 0, keepdims=True)
    gain_sum_ref[...] = gain_sum / gains_ref[0:1, :]


def columns(at, width):
    return pl.ds(pl.multiple_of(at * width, LANES), width)


def spread_body(widths, me_ref, *refs):
    weights, outs = refs[: len(widths)], refs[-4:]
    rows = weights[0].shape[0]
    me = me_ref[0]
    for j, out in enumerate(outs):
        start = 0
        for weight, width in zip(weights, widths):
            out[:rows, start : start + width] = weight[:, columns(me ^ j, width)]
            start += width
    if len(refs) > len(widths) + 4:
        gains = refs[len(widths)][...].astype(F32)
        gains = jnp.concatenate([gains, jnp.zeros((6, rows), F32)], 0)
        gains = jnp.concatenate([gains] * (LANES // rows), 1)
        lane = lax.broadcasted_iota(jnp.int32, (8, LANES), 1)
        gains = jnp.where(lane // rows == me, gains, 0.0).astype(BF)
        for out in outs:
            out[rows:, :] = jnp.zeros((8, out.shape[1]), BF)
            out[rows:, :LANES] = gains


def join_body(rows, me_ref, *refs):
    pieces, out = refs[:4], refs[4]
    me = me_ref[0]
    for j, piece in enumerate(pieces):
        out[pl.ds(pl.multiple_of((me ^ j) * rows, rows), rows), :] = piece[:rows, :]
    if pieces[0].shape[0] > rows:
        below = [piece[rows:, :].astype(F32) for piece in pieces]
        out[4 * rows :, :] = (below[0] + below[1] + below[2] + below[3]).astype(BF)


def part_body(me_ref, one_ref, two_ref, three_ref, *refs):
    outs, total_ref = refs[:4], refs[4]
    total = one_ref[...].astype(F32) + two_ref[...].astype(F32) + three_ref[...].astype(F32)
    total_ref[...] = total
    rows = outs[0].shape[0]
    for j, out in enumerate(outs):
        at = pl.ds(pl.multiple_of((me_ref[0] ^ j) * rows, rows), rows)
        out[...] = total_ref[at, :].astype(BF)


def land_body(widths, me_ref, *refs):
    pieces, outs = refs[:4], refs[4:]
    me = me_ref[0]
    start = 0
    for out, width in zip(outs, widths):
        for j, piece in enumerate(pieces):
            out[:, columns(me ^ j, width)] = piece[:, start : start + width]
        start += width


def small_body(order_ref, one_ref, two_ref, head_ref, out_ref):
    out_ref[...] = jnp.zeros_like(out_ref)
    for i in range(one_ref.shape[1] // LANES):
        at = columns(order_ref[i], LANES)
        out_ref[0:1, at] = one_ref[:, i * LANES : (i + 1) * LANES]
        out_ref[1:2, at] = two_ref[:, i * LANES : (i + 1) * LANES]
    out_ref[2:4, :LANES] = head_ref[0:2, :]


def feed_body(rows, pieces, *refs):
    normed, packs, weights = refs[:4], refs[4:8], refs[8 : 8 + pieces]
    parts = refs[8 + pieces : 12 + pieces]
    hidden_ref, gate_ref, up_ref, down_ref, normed_ref, grad_ref = refs[12 + pieces : 18 + pieces]
    w_ref, part_ref = refs[18 + pieces :]
    ff = hidden_ref.shape[1]
    row = 0
    for weight in weights:
        w_ref[row : row + weight.shape[0], :] = weight[...]
        down_ref[row : row + weight.shape[0], :] = weight[:, 2 * ff :]
        row += weight.shape[0]
    for j in range(4):
        normed_ref[j * rows : (j + 1) * rows, :] = normed[j][...]
        grad_ref[j * rows : (j + 1) * rows, :] = packs[j][rows : 2 * rows, :]

    def one(i, _):
        at = pl.ds(pl.multiple_of(i * rows, rows), rows)
        x = normed_ref[at, :]
        gate, up = dot(x, w_ref[:, :ff]), dot(x, w_ref[:, ff : 2 * ff])
        grad = dot(grad_ref[at, :], w_ref[:, 2 * ff :])
        sig = 1.0 / (1.0 + jnp.exp(-gate))
        silu = gate * sig
        hidden_ref[at, :] = (silu * up).astype(BF)
        grad_gate = (grad * up * (sig * (1.0 + gate * (1.0 - sig)))).astype(BF)
        grad_up = (grad * silu).astype(BF)
        gate_ref[at, :] = grad_gate
        up_ref[at, :] = grad_up
        total = dot_nt(grad_gate, w_ref[:, :ff]) + dot_nt(grad_up, w_ref[:, ff : 2 * ff])
        part_ref[at, :] = total.astype(BF)
        return 0

    lax.fori_loop(0, 4, one, 0)
    for j in range(4):
        parts[j][...] = part_ref[j * rows : (j + 1) * rows, :]


def down_body(rows, hidden_ref, down_ref, *parts):
    for j in range(4):
        at = slice(j * rows, (j + 1) * rows)
        parts[j][...] = dot_nt(hidden_ref[at, :], down_ref[...]).astype(BF)


def attn_weights_body(normed_ref, grad_qkv_ref, grad_ref, out_ref, *chunks):
    cut = grad_qkv_ref.shape[1]
    one = dot_tn(normed_ref[...], grad_qkv_ref[...]).astype(BF)
    two = dot_tn(grad_ref[...], out_ref[...]).astype(BF)
    for i, chunk in enumerate(chunks):
        at = slice(i * LANES, (i + 1) * LANES)
        chunk[:, :cut] = one[at]
        chunk[:, cut:] = two[at]


def rms_scale(values, gain_row):
    return values * lax.rsqrt(jnp.mean(values * values, -1, keepdims=True) + EPS) * gain_row


def place_all(pieces, me, widths):
    outs, start = [], 0
    for width in widths:
        cut = [p[:, start : start + width] for p in pieces]
        outs.append(place(cut, [me ^ j for j in range(4)], 1))
        start += width
    return outs


def on_device(
    dp_size,
    tokens,
    doc_ids,
    w_query,
    key_weight,
    value_weight,
    w_output,
    w_gate,
    w_up,
    w_down,
    norm_gains,
    head_norm_gains,
    out_grad,
):
    local_len, model_dim = tokens.shape[1:]
    tokens, out_grad, doc_row = tokens[0], out_grad[0], doc_ids[0]
    head_dim = head_norm_gains.shape[1]
    q_cols, kv_cols = w_query.shape[1] // 4, key_weight.shape[1] // 4
    shard = norm_gains.shape[1]
    ff_cols = w_gate.shape[1] // 4
    me = lax.axis_index("ctx")
    places = [me ^ j for j in range(4)]
    full_len = 4 * local_len
    fast = ordered(dp_size)
    block_order = jnp.stack(dp_order(dp_size)) if fast else jnp.arange(model_dim // LANES)
    block_order = block_order.astype(jnp.int32)
    me_row = me.reshape(1).astype(jnp.int32)
    attn_widths = (q_cols, kv_cols, kv_cols, q_cols)
    ff_widths = (ff_cols, ff_cols, ff_cols)
    wide, ff_wide = sum(attn_widths), sum(ff_widths)
    attn_local = [w_query, key_weight, value_weight, w_output.T]
    ff_local = [w_gate, w_up, w_down.T]

    pack = pack_inputs(block_order, tokens, out_grad, doc_row)
    if fast:
        sent = call(
            functools.partial(spread_body, attn_widths),
            [((shard + 8, wide), BF)] * 4,
            [me_row, *attn_local, norm_gains],
            scalars=1,
        )
        got = exchange_ctx(sent)
        (block,) = call(
            functools.partial(join_body, shard),
            [((4 * shard + 8, wide), BF)],
            [me_row, *got],
            scalars=1,
        )
        blocks, arrived = gather_blocks(block, False)
        (pack,) = after([pack], got)
        ff_sent = call(
            functools.partial(spread_body, ff_widths),
            [((shard, ff_wide), BF)] * 4,
            [me_row, *ff_local],
            scalars=1,
        )
        ff_got = exchange_ctx(after(ff_sent, arrived[0]))
        (ff_block,) = call(
            functools.partial(join_body, shard),
            [((4 * shard, ff_wide), BF)],
            [me_row, *ff_got],
            scalars=1,
        )
        (ff_block,) = after([ff_block], arrived[3])
        ff_w, ff_arrived = gather_blocks(ff_block, True)
    else:

        def pieces_of(weights):
            sent = []
            for at in places:
                cut = [
                    lax.dynamic_slice_in_dim(w, at * (w.shape[1] // 4), w.shape[1] // 4, 1)
                    for w in weights
                ]
                sent.append(jnp.concatenate(cut, 1))
            return sent

        def whole(weights):
            block = place(exchange_ctx(pieces_of(weights)), places, 0)
            return lax.all_gather(block, "dp", axis=0, tiled=True)

        gains = lax.all_gather(norm_gains, ALL, axis=1, tiled=True).reshape(2, -1, LANES)
        gains = jnp.pad(gains.transpose(1, 0, 2), ((0, 0), (0, 6), (0, wide - LANES)))
        blocks = jnp.concatenate([whole(attn_local).reshape(-1, LANES, wide), gains], 1)
        blocks = [blocks[i] for i in range(blocks.shape[0])]
        ff_w = [whole(ff_local)]
        arrived = ff_arrived = [()] * 4

    core_pack, far_pack = flip(pack, "ctx", 4, 1), flip(pack, "ctx", 4, 2)
    (far_pack,) = after([far_pack], arrived[2])
    packs = [pack, core_pack, far_pack, flip(far_pack, "ctx", 4, 1)]

    docs = jnp.concatenate([p[2 * local_len, :local_len] for p in packs])
    index = jnp.concatenate(
        [at * local_len + jnp.arange(local_len, dtype=jnp.int32) for at in places]
    )
    starts = jnp.sum((docs[None, :] < docs[:, None]).astype(jnp.int32), -1)
    positions = (index - starts).astype(F32)
    half = head_dim // 2
    lane = jnp.arange(LANES)
    freqs = THETA ** (-(2.0 * (lane % half).astype(F32)) / head_dim)
    angles = positions[:, None] * freqs
    cosine = jnp.cos(angles)
    sine = jnp.sin(angles) * jnp.where(lane % head_dim < half, -1.0, 1.0)
    starts = starts.reshape(4, local_len)
    info = jnp.concatenate([me[None], jnp.stack([starts[at, 0] for at in places])])
    info = info.astype(jnp.int32)
    starts = jnp.concatenate([starts, starts], 1).reshape(4, 1, 2 * local_len)
    head_gains = jnp.concatenate([head_norm_gains, head_norm_gains], 1).astype(F32)

    part_shapes = [((local_len, model_dim), BF)] * 4
    normed_one, qk_pre, queries, keys, values, keys_t, values_t, w_qkv, wo_t, gains = call(
        functools.partial(prepare_body, local_len),
        [
            ((full_len, model_dim), BF),
            ((full_len, q_cols + kv_cols), F32),
            ((2, full_len, LANES), BF),
            ((2, full_len, LANES), BF),
            ((2, full_len, LANES), BF),
            ((LANES, full_len), BF),
            ((LANES, full_len), BF),
            ((model_dim, q_cols + 2 * kv_cols), BF),
            ((model_dim, q_cols), BF),
            ((8, model_dim), F32),
        ],
        [*packs, *blocks, cosine, sine, head_gains],
        [pltpu.VMEM((full_len, model_dim), BF)],
    )
    *resid_parts, attn_out, attn_wide, lse = call(
        functools.partial(attend_body, local_len),
        part_shapes
        + [
            ((full_len, q_cols), BF),
            ((2, full_len, LANES), F32),
            ((8, 1, 2 * local_len), F32),
        ],
        [info, queries, keys, values_t, starts, wo_t],
        [pltpu.VMEM((1, 2 * local_len), F32), pltpu.VMEM((head_dim, 2 * local_len), F32)],
        scalars=1,
    )
    resid_parts = after(resid_parts, ff_arrived[0])
    own_tokens = pack[:local_len].astype(F32)
    own_grad = pack[local_len : 2 * local_len].astype(F32)
    resid = own_tokens + sum_parts(scatter_ctx(resid_parts))
    normed_own = rms_scale(resid, gains[1]).astype(BF)
    (normed_own,) = after([normed_own], ff_arrived[1])
    normed_two = gather_ctx(normed_own)

    ff_shape = ((full_len, ff_cols), BF)
    *two_parts, hidden, grad_gate, grad_up, w_down_own, normed_all, grad_all = call(
        functools.partial(feed_body, local_len, len(ff_w)),
        part_shapes
        + [ff_shape] * 3
        + [((model_dim, ff_cols), BF)]
        + [((full_len, model_dim), BF)] * 2,
        [*normed_two, *packs, *ff_w],
        [pltpu.VMEM((model_dim, ff_wide), BF), pltpu.VMEM((full_len, model_dim), BF)],
        limit=56,
    )
    grad_norm_two = scatter_ctx(two_parts)

    def ff_chunks(at):
        cut = [dot_tn(normed_all[:, at], g).astype(BF) for g in (grad_gate, grad_up)]
        cut.append(dot_tn(grad_all[:, at], hidden).astype(BF))
        rows = cut[0].shape[0] // 4
        return [
            jnp.concatenate([c[r * rows : (r + 1) * rows] for c in cut], 1) for r in range(4)
        ]

    def collect(chunks, widths, level):
        wide = chunks[0].shape[1]
        if fast:
            last, stages = scatter_blocks(chunks, level)
            pieces = call(
                part_body,
                [((shard, wide), BF)] * 4,
                [me_row, *last],
                [pltpu.VMEM((4 * shard, wide), F32)],
                scalars=1,
            )
            outs = call(
                functools.partial(land_body, widths),
                [((shard, 4 * width), BF) for width in widths],
                [me_row, *exchange_ctx(pieces)],
                scalars=1,
            )
            return outs, stages
        mine = lax.psum_scatter(jnp.concatenate(chunks, 0), "dp", scatter_dimension=0, tiled=True)
        pieces = [lax.dynamic_slice_in_dim(mine, at * shard, shard, 0) for at in places]
        return place_all(exchange_ctx(pieces), me, widths), [(), (), ()]

    middle = model_dim // 2
    far_chunks = ff_chunks(slice(middle, None))
    near_chunks = ff_chunks(slice(0, middle))
    (grad_g_out, grad_u_out, grad_d_out), stages = collect(
        near_chunks + far_chunks, ff_widths, True
    )
    grad_norm_two = sum_parts(after(grad_norm_two, stages[0]))
    _, second_pull = jax.vjp(rms_scale, resid, gains[1])
    grad_resid_norm, grad_gain_two = second_pull(grad_norm_two)
    grad_resid = own_grad + grad_resid_norm
    down_parts = call(
        functools.partial(down_body, local_len), part_shapes, [hidden, w_down_own]
    )

    grad_attn = after(gather_ctx(grad_resid.astype(BF)), stages[1])
    *one_parts, grad_qkv, head_sums, gain_one, grad_attn_all = call(
        functools.partial(attend_back_body, local_len),
        part_shapes
        + [
            ((full_len, q_cols + 2 * kv_cols), BF),
            ((8, LANES), F32),
            ((1, model_dim), F32),
            ((full_len, model_dim), BF),
        ],
        [
            info,
            *grad_attn,
            queries,
            keys,
            values,
            keys_t,
            starts,
            attn_wide,
            lse,
            qk_pre,
            cosine,
            sine,
            head_gains,
            w_qkv,
            wo_t,
            normed_one,
            gains,
        ],
        [
            pltpu.VMEM((2, full_len, LANES), BF),
            pltpu.VMEM((2, full_len, LANES), F32),
            pltpu.VMEM((2, full_len, LANES), F32),
            pltpu.VMEM((2, full_len, LANES), F32),
            pltpu.VMEM((head_dim, 2 * local_len), F32),
        ],
        scalars=1,
        limit=40,
    )
    layer_out = sum_out(block_order, resid, scatter_ctx(after(down_parts, grad_attn)))
    attn_chunks = call(
        attn_weights_body,
        [((LANES, wide), BF)] * 8,
        [normed_one, grad_qkv, grad_attn_all, attn_out],
    )
    (grad_q_out, grad_k_out, grad_v_out, grad_o_out), _ = collect(attn_chunks, attn_widths, False)
    grad_norm_one = sum_parts(scatter_ctx(one_parts))
    _, first_pull = jax.vjp(lambda u: rms_scale(u, gains[0]), own_tokens)
    zeros = jnp.zeros_like(pack[:local_len])
    input_grad = sum_out(
        block_order, grad_resid + first_pull(grad_norm_one)[0], (zeros, zeros, zeros)
    )
    (small,) = call(
        small_body,
        [((4, model_dim), F32)],
        [block_order, gain_one, grad_gain_two.reshape(1, -1), head_sums],
        scalars=1,
    )
    small = sum_all(small, dp_size)
    norm_own = lax.dynamic_slice_in_dim(small[:2], lax.axis_index(ALL) * shard, shard, 1)
    head_sum = small[2:, :head_dim] + small[2:, head_dim : 2 * head_dim]
    return (
        layer_out[None],
        input_grad[None],
        grad_q_out,
        grad_k_out,
        grad_v_out,
        grad_o_out.T,
        grad_g_out,
        grad_u_out,
        grad_d_out.T,
        norm_own.astype(BF),
        head_sum.astype(BF),
    )


def solution(mesh):
    def step(*arrays):
        return on_device(mesh.shape["dp"], *arrays)

    in_specs = (
        P("dp", "ctx", None),
        P("dp", "ctx"),
        P(("dp", "ctx"), None),
        P(("dp", "ctx"), None),
        P(("dp", "ctx"), None),
        P(None, ("dp", "ctx")),
        P(("dp", "ctx"), None),
        P(("dp", "ctx"), None),
        P(None, ("dp", "ctx")),
        P(None, ("dp", "ctx")),
        P(),
        P("dp", "ctx", None),
    )
    out_specs = (
        P("dp", "ctx", None),
        P("dp", "ctx", None),
        P(("dp", "ctx"), None),
        P(("dp", "ctx"), None),
        P(("dp", "ctx"), None),
        P(None, ("dp", "ctx")),
        P(("dp", "ctx"), None),
        P(("dp", "ctx"), None),
        P(None, ("dp", "ctx")),
        P(None, ("dp", "ctx")),
        P(),
    )
    return jax.shard_map(step, mesh=mesh, in_specs=in_specs, out_specs=out_specs, check_vma=False)
```

```python
import functools

import jax
import jax.numpy as jnp
from jax import lax
from jax.experimental import pallas as pl
from jax.experimental.pallas import tpu as pltpu
from jax.sharding import PartitionSpec as P

EPS = 1e-05
THETA = 1000000.0
BF = jnp.bfloat16
F32 = jnp.float32
ALL = ("dp", "ctx")


def add_low(*terms):
    total = terms[0].astype(F32)
    for term in terms[1:]:
        total = total + term.astype(F32)
    return total.astype(BF)


def flip(value, axis, size, bits):
    return lax.ppermute(value, axis, [(i, i ^ bits) for i in range(size)])


def gather_ctx(own):
    core = flip(own, "ctx", 4, 1)
    across = flip(own, "ctx", 4, 2)
    return [own, core, across, flip(across, "ctx", 4, 1)]


def scatter_ctx(parts):
    far = flip(parts[3], "ctx", 4, 1)
    near = flip(parts[1], "ctx", 4, 1)
    return parts[0], near, flip(add_low(parts[2], far), "ctx", 4, 2)


def sum_parts(parts):
    return parts[0].astype(F32) + parts[1].astype(F32) + parts[2].astype(F32)


def exchange_ctx(parts):
    return [parts[0]] + [flip(parts[j], "ctx", 4, j) for j in range(1, 4)]


def place(parts, where, axis):
    size = parts[0].shape[axis]
    shape = list(parts[0].shape)
    shape[axis] = size * len(parts)
    out = jnp.zeros(shape, parts[0].dtype)
    for part, at in zip(parts, where):
        out = lax.dynamic_update_slice_in_dim(out, part, at * size, axis)
    return out


def bar(*trees):
    return lax.optimization_barrier(trees)


def ordered(dp_size):
    return dp_size == 8


def dp_order(dp_size):
    me = lax.axis_index("dp")
    return [((me - 2 * (i % 4)) % dp_size) ^ (i // 4) for i in range(dp_size)]


def across_y(value):
    return flip(value, "dp", 8, 1)


def along_z(value):
    return lax.ppermute(value, "dp", [(i, (i + 2) % 8) for i in range(8)])


def sum_all(value, dp_size):
    for bits in (1, 2):
        value = value + flip(value, "ctx", 4, bits)
    bits = 1
    while bits < dp_size:
        value = value + flip(value, "dp", dp_size, bits)
        bits *= 2
    return value


def dot(a, b):
    return lax.dot_general(a, b, (((1,), (0,)), ((), ())), preferred_element_type=F32)


def dot_nt(a, b):
    return lax.dot_general(a, b, (((1,), (1,)), ((), ())), preferred_element_type=F32)


def dot_tn(a, b):
    return lax.dot_general(a, b, (((0,), (0,)), ((), ())), preferred_element_type=F32)


VMEM = pl.BlockSpec(memory_space=pltpu.VMEM)
SMEM = pl.BlockSpec(memory_space=pltpu.SMEM)
LANES = 128
HIGH = lax.Precision.HIGHEST


HEAVY = 10**11


def call(body, outs, ins, scratch=(), scalars=0, limit=4, flops=1000000, held=False):
    def spec(shape):
        if held:
            return VMEM
        zeros = (0,) * len(shape)
        return pl.BlockSpec(tuple(shape), lambda i: zeros, pipeline_mode=pl.Buffered(1))

    return pl.pallas_call(
        body,
        out_shape=[jax.ShapeDtypeStruct(shape, kind) for shape, kind in outs],
        grid=() if held else (1,),
        in_specs=[SMEM] * scalars + [spec(x.shape) for x in ins[scalars:]],
        out_specs=[spec(shape) for shape, _ in outs],
        scratch_shapes=list(scratch),
        compiler_params=pltpu.CompilerParams(vmem_limit_bytes=limit << 20),
        cost_estimate=pl.CostEstimate(flops=flops, bytes_accessed=1000, transcendentals=0),
    )(*ins)


def pack_body(order_ref, tokens_ref, docs_ref, out_ref):
    rows = tokens_ref.shape[0]
    for i in range(tokens_ref.shape[1] // LANES):
        at = pl.ds(pl.multiple_of(order_ref[i] * LANES, LANES), LANES)
        out_ref[:rows, i * LANES : (i + 1) * LANES] = tokens_ref[:, at]
    if docs_ref is not None:
        below = jnp.broadcast_to(docs_ref[...].astype(F32), (16, rows)).astype(BF)
        out_ref[rows:, :rows] = below
        out_ref[rows:, rows:] = jnp.zeros((16, out_ref.shape[1] - rows), BF)


def pack_rows(order, rows, doc_row=None):
    if doc_row is None:
        body = lambda order_ref, rows_ref, out_ref: pack_body(order_ref, rows_ref, None, out_ref)
        return call(body, [(rows.shape, BF)], [order, rows], scalars=1)[0]
    shape = (rows.shape[0] + 16, rows.shape[1])
    return call(pack_body, [(shape, BF)], [order, rows, doc_row.reshape(1, -1)], scalars=1)[0]


def sum_body(order_ref, base_ref, *refs):
    parts, out_ref = refs[:-1], refs[-1]
    for i in range(base_ref.shape[1] // LANES):
        at = slice(i * LANES, (i + 1) * LANES)
        total = base_ref[:, at]
        if parts:
            part = parts[0][:, at].astype(F32)
            for ref in parts[1:]:
                part = part + ref[:, at].astype(F32)
            total = total + part
        to = pl.ds(pl.multiple_of(order_ref[i] * LANES, LANES), LANES)
        out_ref[:, to] = total.astype(BF)


def sum_out(order, base, parts):
    return call(sum_body, [(base.shape, BF)], [order, base, *parts], scalars=1)[0]


def lane_masks(rows):
    lane = lax.broadcasted_iota(jnp.int32, (rows, LANES), 1)
    return lane < 64, lax.rem(lane, 64) < 32


def half_sums(squares):
    row = lax.broadcasted_iota(jnp.int32, (LANES, LANES), 0) // 64
    col = lax.broadcasted_iota(jnp.int32, (LANES, LANES), 1) // 64
    return jnp.dot(
        squares, (row == col).astype(F32), preferred_element_type=F32, precision=HIGH
    )


def turn(value, first):
    return jnp.where(first, pltpu.roll(value, 96, 1), pltpu.roll(value, 32, 1))


def doubled(value, left):
    other = pltpu.roll(value, 64, 1)
    return jnp.where(left, value, other), jnp.where(left, other, value)


def prepare_body(rows, *refs):
    packs, blocks = refs[:4], refs[4:12]
    cos_ref, sin_ref, head_ref = refs[12:15]
    normed_ref, qk_pre_ref, q_ref, kd_ref, vd_ref, kt_ref, vt_ref = refs[15:22]
    wqkv_ref, wo_ref, gains_ref, all_ref = refs[22:26]
    for i, block in enumerate(blocks):
        at = i * LANES
        wqkv_ref[at : at + LANES, :] = block[:LANES, :512]
        wo_ref[at : at + LANES, :] = block[:LANES, 512:]
        gains_ref[:, at : at + LANES] = block[LANES : LANES + 8, :LANES].astype(F32)
    for j, pack in enumerate(packs):
        all_ref[j * rows : (j + 1) * rows, :] = pack[:rows, :]
    left, first = lane_masks(LANES)
    gain = gains_ref[0:1, :]
    q_gain, k_gain = head_ref[0:1, :], head_ref[1:2, :]

    def chunk(i, _):
        at = pl.ds(pl.multiple_of(i * LANES, LANES), LANES)
        x = all_ref[at, :].astype(F32)
        scale = lax.rsqrt(jnp.mean(x * x, -1, keepdims=True) + EPS)
        normed = (x * scale * gain).astype(BF)
        normed_ref[at, :] = normed
        pre = jnp.dot(normed, wqkv_ref[...], preferred_element_type=F32)
        qk_pre_ref[at, :] = pre[:, :384]
        cos, sin = cos_ref[at, :], sin_ref[at, :]
        turned = []
        for b in range(3):
            u = pre[:, b * LANES : (b + 1) * LANES]
            u = u * lax.rsqrt(half_sums(u * u) * (1.0 / 64) + EPS) * (k_gain if b == 2 else q_gain)
            turned.append(u * cos + turn(u, first) * sin)
        q_ref[0, at, :] = turned[0].astype(BF)
        q_ref[1, at, :] = turned[1].astype(BF)
        key, value = turned[2], pre[:, 384:]
        for both, flat, one in ((kd_ref, kt_ref, key), (vd_ref, vt_ref, value)):
            low, high = doubled(one, left)
            both[0, at, :] = low.astype(BF)
            both[1, at, :] = high.astype(BF)
            flat[:, at] = one.T.astype(BF)
        return 0

    lax.fori_loop(0, all_ref.shape[0] // LANES, chunk, 0)


def two_heads(block, left):
    zero = jnp.zeros_like(block)
    return jnp.concatenate([jnp.where(left, block, zero), jnp.where(left, zero, block)], 0)


def seen(start_row, first_key, rows, first_query):
    shape = (rows, 2 * rows)
    key = lax.broadcasted_iota(jnp.int32, shape, 0)
    mask = key + first_key >= start_row
    if first_query is not None:
        lane = lax.broadcasted_iota(jnp.int32, shape, 1)
        mask = mask & (key <= jnp.where(lane < rows, lane, lane - rows))
    return mask


LOG2E = 1.4426950408889634
SCORE = LOG2E / 8.0


def attend_body(rows, info_ref, q_ref, kd_ref, vt_ref, start_ref, wo_ref, *refs):
    parts = refs[:4]
    out_ref, wide_ref, lse_ref, sum_ref, acc_ref = refs[4:9]
    me = info_ref[0]
    left = lax.broadcasted_iota(jnp.int32, (rows, LANES), 1) < 64

    def one(step, _):
        kv, a = step // 4, lax.rem(step, 4)
        at_q = pl.ds(pl.multiple_of((a ^ me) * rows, rows), rows)
        q2 = two_heads(q_ref[kv, at_q, :], left)
        start_row = start_ref[a ^ me]
        sum_ref[...] = jnp.zeros_like(sum_ref)
        acc_ref[...] = jnp.zeros_like(acc_ref)
        for d in range(3):

            @pl.when((a >= d) & (info_ref[1 + a] < (a - d + 1) * rows))
            def _():
                at_k = pl.ds(pl.multiple_of(((a - d) ^ me) * rows, rows), rows)
                scores = dot_nt(kd_ref[kv, at_k, :], q2)
                mask = seen(start_row, (a - d) * rows, rows, a if d == 0 else None)
                p = jnp.where(mask, jnp.exp2(scores * SCORE), 0.0)
                sum_ref[...] += jnp.sum(p, 0, keepdims=True)
                half = pl.ds(pl.multiple_of(kv * 64, 64), 64)
                acc_ref[...] += dot(vt_ref[half, at_k], p.astype(BF))

        total = sum_ref[...]
        lse_ref[kv * 4 + (a ^ me)] = jnp.log2(total)
        mixed = acc_ref[...] / total
        mixed = jnp.concatenate([mixed[:, :rows], mixed[:, rows:]], 0).T
        wide_ref[kv, at_q, :] = mixed
        out_ref[at_q, columns(kv, LANES)] = mixed.astype(BF)
        return 0

    lax.fori_loop(0, 8, one, 0)
    for j in range(4):
        at = slice(j * rows, (j + 1) * rows)
        parts[j][...] = dot_nt(out_ref[at, :], wo_ref[...]).astype(BF)


def attend_back_body(rows, *refs):
    info_ref, g0, g1, g2, g3, q_ref, kd_ref, vd_ref, kt_ref, start_ref, wide_ref, lse_ref = refs[:12]
    qk_pre_ref, cos_ref, sin_ref, head_ref, wqkv_ref, wo_ref, normed_ref, gains_ref = refs[12:20]
    parts, low_ref, head_sum_ref, gain_sum_ref, grad_ref = refs[20:24], *refs[24:28]
    mixed_ref, dq_ref, dk_ref, dv_ref, acc_ref = refs[28:33]
    me = info_ref[0]
    left = lax.broadcasted_iota(jnp.int32, (rows, LANES), 1) < 64
    for j, g in enumerate((g0, g1, g2, g3)):
        grad_ref[j * rows : (j + 1) * rows, :] = g[...]
        grad = dot(g[...], wo_ref[...]).astype(BF)
        mixed_ref[0, j * rows : (j + 1) * rows, :] = grad[:, :LANES]
        mixed_ref[1, j * rows : (j + 1) * rows, :] = grad[:, LANES:]
    dk_ref[...] = jnp.zeros_like(dk_ref)
    dv_ref[...] = jnp.zeros_like(dv_ref)
    pick = (
        lax.broadcasted_iota(jnp.int32, (8, LANES), 1) // 64
        == lax.broadcasted_iota(jnp.int32, (8, LANES), 0)
    ).astype(F32)

    def one(step, _):
        kv, a = step // 4, lax.rem(step, 4)
        at_q = pl.ds(pl.multiple_of((a ^ me) * rows, rows), rows)
        q2 = two_heads(q_ref[kv, at_q, :], left)
        grad = mixed_ref[kv, at_q, :]
        g2 = two_heads(grad, left)
        inner = lax.dot_general(
            pick,
            grad.astype(F32) * wide_ref[kv, at_q, :],
            (((1,), (1,)), ((), ())),
            preferred_element_type=F32,
            precision=HIGH,
        )
        inner = jnp.concatenate([inner[0:1], inner[1:2]], 1)
        lse = lse_ref[kv * 4 + (a ^ me)]
        start_row = start_ref[a ^ me]
        acc_ref[...] = jnp.zeros_like(acc_ref)
        for d in range(3):

            @pl.when((a >= d) & (info_ref[1 + a] < (a - d + 1) * rows))
            def _():
                at_k = pl.ds(pl.multiple_of(((a - d) ^ me) * rows, rows), rows)
                scores = dot_nt(kd_ref[kv, at_k, :], q2)
                mask = seen(start_row, (a - d) * rows, rows, a if d == 0 else None)
                p = jnp.where(mask, jnp.exp2(scores * SCORE - lse), 0.0)
                gp = dot_nt(vd_ref[kv, at_k, :], g2)
                gs = (p * (gp - inner)).astype(BF)
                dv_ref[kv, at_k, :] += dot(p.astype(BF), g2)
                dk_ref[kv, at_k, :] += dot(gs, q2)
                half = pl.ds(pl.multiple_of(kv * 64, 64), 64)
                acc_ref[...] += dot(kt_ref[half, at_k], gs)

        both = acc_ref[...] * 0.125
        dq_ref[kv, at_q, :] = jnp.concatenate([both[:, :rows], both[:, rows:]], 0).T
        return 0

    lax.fori_loop(0, 8, one, 0)
    left, first = lane_masks(LANES)
    head_sum_ref[...] = jnp.zeros_like(head_sum_ref)

    def folded(ref, at):
        low, high = ref[0, at, :], ref[1, at, :]
        low, high = low + pltpu.roll(low, 64, 1), high + pltpu.roll(high, 64, 1)
        return jnp.where(left, low, high)

    def chunk(i, _):
        at = pl.ds(pl.multiple_of(i * LANES, LANES), LANES)
        cos, sin = cos_ref[at, :], sin_ref[at, :]
        for b in range(3):
            u = qk_pre_ref[at, b * LANES : (b + 1) * LANES]
            g = folded(dk_ref, at) * 0.125 if b == 2 else dq_ref[b, at, :]
            w = g * cos - turn(g, first) * sin
            row = 1 if b == 2 else 0
            gain = head_ref[row : row + 1, :]
            r = lax.rsqrt(half_sums(u * u) * (1.0 / 64) + EPS)
            head_sum_ref[row : row + 1, :] += jnp.sum(w * u * r, 0, keepdims=True)
            w = w * gain
            back = r * w - u * (r * r * r) * (half_sums(w * u) * (1.0 / 64))
            low_ref[at, b * LANES : (b + 1) * LANES] = back.astype(BF)
        low_ref[at, 384:] = folded(dv_ref, at).astype(BF)
        return 0

    lax.fori_loop(0, low_ref.shape[0] // LANES, chunk, 0)
    gain_sum = jnp.zeros((1, normed_ref.shape[1]), F32)
    for j in range(4):
        at = slice(j * rows, (j + 1) * rows)
        grad = dot_nt(low_ref[at, :], wqkv_ref[...])
        parts[j][...] = grad.astype(BF)
        gain_sum = gain_sum + jnp.sum(grad * normed_ref[at, :].astype(F32), 0, keepdims=True)
    gain_sum_ref[...] = gain_sum / gains_ref[0:1, :]


def columns(at, width):
    return pl.ds(pl.multiple_of(at * width, LANES), width)


def spread_body(widths, me_ref, *refs):
    weights, outs = refs[: len(widths)], refs[-4:]
    rows = weights[0].shape[0]
    me = me_ref[0]
    for j, out in enumerate(outs):
        start = 0
        for weight, width in zip(weights, widths):
            out[:rows, start : start + width] = weight[:, columns(me ^ j, width)]
            start += width
    if len(refs) > len(widths) + 4:
        gains = refs[len(widths)][...].astype(F32)
        gains = jnp.concatenate([gains, jnp.zeros((6, rows), F32)], 0)
        gains = jnp.concatenate([gains] * (LANES // rows), 1)
        lane = lax.broadcasted_iota(jnp.int32, (8, LANES), 1)
        gains = jnp.where(lane // rows == me, gains, 0.0).astype(BF)
        for out in outs:
            out[rows:, :] = jnp.zeros((8, out.shape[1]), BF)
            out[rows:, :LANES] = gains


def join_body(rows, me_ref, *refs):
    pieces, out = refs[:4], refs[4]
    me = me_ref[0]
    for j, piece in enumerate(pieces):
        out[pl.ds(pl.multiple_of((me ^ j) * rows, rows), rows), :] = piece[:rows, :]
    if pieces[0].shape[0] > rows:
        below = [piece[rows:, :].astype(F32) for piece in pieces]
        out[4 * rows :, :] = (below[0] + below[1] + below[2] + below[3]).astype(BF)


def part_body(me_ref, one_ref, two_ref, three_ref, *refs):
    outs, total_ref = refs[:4], refs[4]
    total = one_ref[...].astype(F32) + two_ref[...].astype(F32) + three_ref[...].astype(F32)
    total_ref[...] = total
    rows = outs[0].shape[0]
    for j, out in enumerate(outs):
        at = pl.ds(pl.multiple_of((me_ref[0] ^ j) * rows, rows), rows)
        out[...] = total_ref[at, :].astype(BF)


def land_body(widths, me_ref, *refs):
    pieces, outs = refs[:4], refs[4:]
    me = me_ref[0]
    start = 0
    for out, width in zip(outs, widths):
        for j, piece in enumerate(pieces):
            out[:, columns(me ^ j, width)] = piece[:, start : start + width]
        start += width


def small_body(order_ref, one_ref, two_ref, head_ref, *refs):
    out_ref = refs[-1]
    out_ref[...] = jnp.zeros_like(out_ref)
    for i in range(one_ref.shape[1] // LANES):
        at = columns(order_ref[i], LANES)
        out_ref[0:1, at] = one_ref[:, i * LANES : (i + 1) * LANES]
        out_ref[1:2, at] = two_ref[:, i * LANES : (i + 1) * LANES]
    out_ref[2:4, :LANES] = head_ref[0:2, :]


def feed_body(rows, pieces, *refs):
    normed, packs, weights = refs[:4], refs[4:8], refs[8 : 8 + pieces]
    parts = refs[8 + pieces : 12 + pieces]
    hidden_ref, gate_ref, up_ref, down_ref, normed_ref, grad_ref = refs[12 + pieces : 18 + pieces]
    w_ref, part_ref = refs[18 + pieces :]
    ff = hidden_ref.shape[1]
    row = 0
    for weight in weights:
        w_ref[row : row + weight.shape[0], :] = weight[...]
        down_ref[row : row + weight.shape[0], :] = weight[:, 2 * ff :]
        row += weight.shape[0]
    for j in range(4):
        normed_ref[j * rows : (j + 1) * rows, :] = normed[j][...]
        grad_ref[j * rows : (j + 1) * rows, :] = packs[j][...]

    def one(i, _):
        at = pl.ds(pl.multiple_of(i * rows, rows), rows)
        x = normed_ref[at, :]
        gate, up = dot(x, w_ref[:, :ff]), dot(x, w_ref[:, ff : 2 * ff])
        grad = dot(grad_ref[at, :], w_ref[:, 2 * ff :])
        sig = 1.0 / (1.0 + jnp.exp(-gate))
        silu = gate * sig
        hidden_ref[at, :] = (silu * up).astype(BF)
        grad_gate = (grad * up * (sig * (1.0 + gate * (1.0 - sig)))).astype(BF)
        grad_up = (grad * silu).astype(BF)
        gate_ref[at, :] = grad_gate
        up_ref[at, :] = grad_up
        total = dot_nt(grad_gate, w_ref[:, :ff]) + dot_nt(grad_up, w_ref[:, ff : 2 * ff])
        part_ref[at, :] = total.astype(BF)
        return 0

    lax.fori_loop(0, 4, one, 0)
    for j in range(4):
        parts[j][...] = part_ref[j * rows : (j + 1) * rows, :]


def down_body(rows, hidden_ref, down_ref, *parts):
    for j in range(4):
        at = slice(j * rows, (j + 1) * rows)
        parts[j][...] = dot_nt(hidden_ref[at, :], down_ref[...]).astype(BF)


def attn_weights_body(normed_ref, grad_qkv_ref, grad_ref, out_ref, *chunks):
    cut = grad_qkv_ref.shape[1]
    one = dot_tn(normed_ref[...], grad_qkv_ref[...]).astype(BF)
    two = dot_tn(grad_ref[...], out_ref[...]).astype(BF)
    for i, chunk in enumerate(chunks):
        at = slice(i * LANES, (i + 1) * LANES)
        chunk[:, :cut] = one[at]
        chunk[:, cut:] = two[at]


def rms_scale(values, gain_row):
    return values * lax.rsqrt(jnp.mean(values * values, -1, keepdims=True) + EPS) * gain_row


def place_all(pieces, me, widths):
    outs, start = [], 0
    for width in widths:
        cut = [p[:, start : start + width] for p in pieces]
        outs.append(place(cut, [me ^ j for j in range(4)], 1))
        start += width
    return outs


def on_device(
    dp_size,
    tokens,
    doc_ids,
    w_query,
    key_weight,
    value_weight,
    w_output,
    w_gate,
    w_up,
    w_down,
    norm_gains,
    head_norm_gains,
    out_grad,
):
    local_len, model_dim = tokens.shape[1:]
    tokens, out_grad, doc_row = tokens[0], out_grad[0], doc_ids[0]
    head_dim = head_norm_gains.shape[1]
    q_cols, kv_cols = w_query.shape[1] // 4, key_weight.shape[1] // 4
    shard = norm_gains.shape[1]
    ff_cols = w_gate.shape[1] // 4
    me = lax.axis_index("ctx")
    places = [me ^ j for j in range(4)]
    full_len = 4 * local_len
    fast = ordered(dp_size)
    block_order = jnp.stack(dp_order(dp_size)) if fast else jnp.arange(model_dim // LANES)
    block_order = block_order.astype(jnp.int32)
    me_row = me.reshape(1).astype(jnp.int32)
    attn_widths = (q_cols, kv_cols, kv_cols, q_cols)
    ff_widths = (ff_cols, ff_cols, ff_cols)
    wide, ff_wide = sum(attn_widths), sum(ff_widths)
    attn_local = [w_query, key_weight, value_weight, w_output.T]
    ff_local = [w_gate, w_up, w_down.T]

    pack = pack_rows(block_order, tokens, doc_row)
    grad_pack = pack_rows(block_order, out_grad)
    if fast:
        sent = call(
            functools.partial(spread_body, attn_widths),
            [((shard + 8, wide), BF)] * 4,
            [me_row, *attn_local, norm_gains],
            scalars=1,
        )
        ff_sent = call(
            functools.partial(spread_body, ff_widths),
            [((shard, ff_wide), BF)] * 4,
            [me_row, *ff_local],
            scalars=1,
        )
        got, ff_sent = bar(exchange_ctx(sent), ff_sent)
        ff_got = exchange_ctx(ff_sent)
        (block,) = call(
            functools.partial(join_body, shard),
            [((4 * shard + 8, wide), BF)],
            [me_row, *got],
            scalars=1,
        )
        y0, z1, pack = bar(across_y(block), along_z(block), pack)
        core_pack, far_pack = flip(pack, "ctx", 4, 1), flip(pack, "ctx", 4, 2)
        y1, z2 = bar(across_y(z1), along_z(z1))
        (ff_block,) = call(
            functools.partial(join_body, shard),
            [((4 * shard, ff_wide), BF)],
            [me_row, *ff_got],
            scalars=1,
        )
        y2, z3, far_pack, grad_pack, ff_block = bar(
            across_y(z2), along_z(z2), far_pack, grad_pack, ff_block
        )
        far_core_pack = flip(far_pack, "ctx", 4, 1)
        y3, ff_block, far_core_pack = bar(across_y(z3), ff_block, far_core_pack)
        ff_z1, ff_y0 = along_z(ff_block), across_y(ff_block)
        blocks = [block, z1, z2, z3, y0, y1, y2, y3]
    else:

        def pieces_of(weights):
            sent = []
            for at in places:
                cut = [
                    lax.dynamic_slice_in_dim(w, at * (w.shape[1] // 4), w.shape[1] // 4, 1)
                    for w in weights
                ]
                sent.append(jnp.concatenate(cut, 1))
            return sent

        def whole(weights):
            block = place(exchange_ctx(pieces_of(weights)), places, 0)
            return lax.all_gather(block, "dp", axis=0, tiled=True)

        gains = lax.all_gather(norm_gains, ALL, axis=1, tiled=True).reshape(2, -1, LANES)
        gains = jnp.pad(gains.transpose(1, 0, 2), ((0, 0), (0, 6), (0, wide - LANES)))
        blocks = jnp.concatenate([whole(attn_local).reshape(-1, LANES, wide), gains], 1)
        blocks = [blocks[i] for i in range(blocks.shape[0])]
        ff_w = [whole(ff_local)]
        core_pack, far_pack = flip(pack, "ctx", 4, 1), flip(pack, "ctx", 4, 2)
        far_core_pack = flip(far_pack, "ctx", 4, 1)

    packs = [pack, core_pack, far_pack, far_core_pack]
    grad_packs = gather_ctx(grad_pack)
    docs = jnp.concatenate([p[local_len, :local_len] for p in packs])
    index = jnp.concatenate(
        [at * local_len + jnp.arange(local_len, dtype=jnp.int32) for at in places]
    )
    starts = jnp.sum((docs[None, :] < docs[:, None]).astype(jnp.int32), -1)
    positions = (index - starts).astype(F32)
    half = head_dim // 2
    lane = jnp.arange(LANES)
    freqs = THETA ** (-(2.0 * (lane % half).astype(F32)) / head_dim)
    angles = positions[:, None] * freqs
    cosine = jnp.cos(angles)
    sine = jnp.sin(angles) * jnp.where(lane % head_dim < half, -1.0, 1.0)
    starts = starts.reshape(4, local_len)
    info = jnp.concatenate([me[None], jnp.stack([starts[at, 0] for at in places])])
    info = info.astype(jnp.int32)
    starts = jnp.concatenate([starts, starts], 1).reshape(4, 1, 2 * local_len)
    head_gains = jnp.concatenate([head_norm_gains, head_norm_gains], 1).astype(F32)

    part_shapes = [((local_len, model_dim), BF)] * 4
    normed_one, qk_pre, queries, keys, values, keys_t, values_t, w_qkv, wo_t, gains = call(
        functools.partial(prepare_body, local_len),
        [
            ((full_len, model_dim), BF),
            ((full_len, q_cols + kv_cols), F32),
            ((2, full_len, LANES), BF),
            ((2, full_len, LANES), BF),
            ((2, full_len, LANES), BF),
            ((LANES, full_len), BF),
            ((LANES, full_len), BF),
            ((model_dim, q_cols + 2 * kv_cols), BF),
            ((model_dim, q_cols), BF),
            ((8, model_dim), F32),
        ],
        [*packs, *blocks, cosine, sine, head_gains],
        [pltpu.VMEM((full_len, model_dim), BF)],
        limit=28,
        flops=HEAVY,
    )
    if fast:
        queries, keys, ff_z1, ff_y0 = bar(queries, keys, ff_z1, ff_y0)
        ff_z2, ff_y1 = along_z(ff_z1), across_y(ff_z1)
    *resid_parts, attn_out, attn_wide, lse = call(
        functools.partial(attend_body, local_len),
        part_shapes
        + [
            ((full_len, q_cols), BF),
            ((2, full_len, LANES), F32),
            ((8, 1, 2 * local_len), F32),
        ],
        [info, queries, keys, values_t, starts, wo_t],
        [pltpu.VMEM((1, 2 * local_len), F32), pltpu.VMEM((head_dim, 2 * local_len), F32)],
        scalars=1,
        limit=20,
    )
    own_tokens = pack[:local_len].astype(F32)
    own_grad = grad_pack.astype(F32)
    resid_sum = scatter_ctx(resid_parts)
    if fast:
        resid_sum, ff_z2, ff_y1 = bar(resid_sum, ff_z2, ff_y1)
        ff_z3, ff_y2 = along_z(ff_z2), across_y(ff_z2)
    resid = own_tokens + sum_parts(resid_sum)
    normed_own = rms_scale(resid, gains[1]).astype(BF)
    normed_core, normed_far = flip(normed_own, "ctx", 4, 1), flip(normed_own, "ctx", 4, 2)
    if fast:
        normed_far, ff_z3, ff_y2 = bar(normed_far, ff_z3, ff_y2)
        cut = ff_block.shape[0] // 2
        ff_w = [ff_block, ff_z1, ff_z2, ff_z3, ff_y0, ff_y1, ff_y2]
        ff_w += [across_y(ff_z3[:cut]), along_z(ff_y2[cut:])]
    normed_two = [normed_own, normed_core, normed_far, flip(normed_far, "ctx", 4, 1)]

    ff_shape = ((full_len, ff_cols), BF)
    *two_parts, hidden, grad_gate, grad_up, w_down_own, normed_all, grad_all = call(
        functools.partial(feed_body, local_len, len(ff_w)),
        part_shapes
        + [ff_shape] * 3
        + [((model_dim, ff_cols), BF)]
        + [((full_len, model_dim), BF)] * 2,
        [*normed_two, *grad_packs, *ff_w],
        [pltpu.VMEM((model_dim, ff_wide), BF), pltpu.VMEM((full_len, model_dim), BF)],
        limit=50,
    )
    near_two, far_two = flip(two_parts[1], "ctx", 4, 1), flip(two_parts[3], "ctx", 4, 1)
    near_two, far_two, normed_all, grad_all = bar(near_two, far_two, normed_all, grad_all)
    far_two = flip(add_low(two_parts[2], far_two), "ctx", 4, 2)

    def ff_chunks(at):
        cut = [dot_tn(normed_all[:, at], g).astype(BF) for g in (grad_gate, grad_up)]
        cut.append(dot_tn(grad_all[:, at], hidden).astype(BF))
        rows = cut[0].shape[0] // 4
        return [
            jnp.concatenate([c[r * rows : (r + 1) * rows] for c in cut], 1) for r in range(4)
        ]

    def pieces_of_sum(last):
        wide = last[0].shape[1]
        return call(
            part_body,
            [((shard, wide), BF)] * 4,
            [me_row, *last],
            [pltpu.VMEM((4 * shard, wide), F32)],
            scalars=1,
            limit=12,
        )

    def land(pieces, widths):
        return call(
            functools.partial(land_body, widths),
            [((shard, 4 * width), BF) for width in widths],
            [me_row, *pieces],
            scalars=1,
        )

    def plain_sums(chunks, widths):
        mine = lax.psum_scatter(jnp.concatenate(chunks, 0), "dp", scatter_dimension=0, tiled=True)
        pieces = [lax.dynamic_slice_in_dim(mine, at * shard, shard, 0) for at in places]
        return place_all(exchange_ctx(pieces), me, widths)

    def tick(value):
        def body(in_ref, out_ref):
            out_ref[...] = in_ref[...]

        return call(body, [((8, LANES), BF)], [value[:8, :LANES]], flops=HEAVY)[0]

    middle = model_dim // 2
    far = ff_chunks(slice(middle, None))
    if fast:
        cut = 4 * shard // 2
        first, early = across_y(far[1][:cut]), along_z(far[1][cut:])
        grad_gate, grad_up, hidden, tick_one = bar(grad_gate, grad_up, hidden, tick(far[3]))
    near = ff_chunks(slice(0, middle))
    if fast:
        second = jnp.concatenate([far[2][:cut], add_low(far[2][cut:], early)], 0)
        total = jnp.concatenate([add_low(near[1][:cut], first), near[1][cut:]], 0)
        near_two, far_two, total, second = bar(near_two, far_two, total, second)
        total, second = along_z(total), across_y(second)
    grad_norm_two = sum_parts((two_parts[0], near_two, far_two))
    _, second_pull = jax.vjp(rms_scale, resid, gains[1])
    grad_resid_norm, grad_gain_two = second_pull(grad_norm_two)
    grad_resid = own_grad + grad_resid_norm
    (*down_parts,) = call(
        functools.partial(down_body, local_len), part_shapes, [hidden, w_down_own], limit=16
    )

    grad_low = grad_resid.astype(BF)
    grad_core, grad_far = flip(grad_low, "ctx", 4, 1), flip(grad_low, "ctx", 4, 2)
    if fast:
        grad_far, down_parts = bar(grad_far, down_parts)
    down_near, down_far = flip(down_parts[1], "ctx", 4, 1), flip(down_parts[3], "ctx", 4, 1)
    down_far = add_low(down_parts[2], down_far)
    grad_attn = [grad_low, grad_core, grad_far, flip(grad_far, "ctx", 4, 1)]
    if fast:
        total, third = bar(add_low(near[2], second, total), far[3])
        grad_attn, down_far, tick_two = bar(grad_attn, down_far, tick(total))
        total, third = along_z(total), across_y(third)
    down_far = flip(down_far, "ctx", 4, 2)
    *one_parts, grad_qkv, head_sums, gain_one, grad_attn_all = call(
        functools.partial(attend_back_body, local_len),
        part_shapes
        + [
            ((full_len, q_cols + 2 * kv_cols), BF),
            ((8, LANES), F32),
            ((1, model_dim), F32),
            ((full_len, model_dim), BF),
        ],
        [
            info,
            *grad_attn,
            queries,
            keys,
            values,
            keys_t,
            starts,
            attn_wide,
            lse,
            qk_pre,
            cosine,
            sine,
            head_gains,
            w_qkv,
            wo_t,
            normed_one,
            gains,
        ],
        [
            pltpu.VMEM((2, full_len, LANES), BF),
            pltpu.VMEM((2, full_len, LANES), F32),
            pltpu.VMEM((2, full_len, LANES), F32),
            pltpu.VMEM((2, full_len, LANES), F32),
            pltpu.VMEM((head_dim, 2 * local_len), F32),
        ],
        scalars=1,
        limit=36,
    )
    layer_out = sum_out(block_order, resid, (down_parts[0], down_near, down_far))
    attn_chunks = call(
        attn_weights_body,
        [((LANES, wide), BF)] * 8,
        [normed_one, grad_qkv, grad_attn_all, attn_out],
        limit=20,
    )
    ticks = [tick_one, tick_two] if fast else []
    (small,) = call(
        small_body,
        [((4, model_dim), F32)],
        [block_order, gain_one, grad_gain_two.reshape(1, -1), head_sums, *ticks],
        scalars=1,
    )
    grad_one = scatter_ctx(one_parts)
    if fast:
        total, fourth = bar(add_low(near[3], third, total), far[0])
        last = (near[0], across_y(fourth), along_z(total))
        near, far = attn_chunks[:4], attn_chunks[4:]
        small = small + flip(small, "ctx", 4, 1)
        small = small + flip(small, "ctx", 4, 2)
        total, small_y = bar(
            add_low(near[1], across_y(far[1])), flip(small, "dp", dp_size, 1)
        )
        small = small + small_y
        total, small_z, last = bar(
            add_low(near[2], across_y(far[2]), along_z(total)), flip(small, "dp", dp_size, 2), last
        )
        small = small + small_z
        total, small_z = bar(
            add_low(near[3], across_y(far[3]), along_z(total)), flip(small, "dp", dp_size, 4)
        )
        small = small + small_z
        attn_last = (near[0], across_y(far[0]), along_z(total))
        ff_pieces = exchange_ctx(pieces_of_sum(last))
        attn_pieces = exchange_ctx(pieces_of_sum(attn_last))
        grad_g_out, grad_u_out, grad_d_out = land(ff_pieces, ff_widths)
        grad_q_out, grad_k_out, grad_v_out, grad_o_out = land(attn_pieces, attn_widths)
    else:
        grad_g_out, grad_u_out, grad_d_out = plain_sums(near + far, ff_widths)
        grad_q_out, grad_k_out, grad_v_out, grad_o_out = plain_sums(attn_chunks, attn_widths)
        small = sum_all(small, dp_size)
    _, first_pull = jax.vjp(lambda u: rms_scale(u, gains[0]), own_tokens)
    input_grad = sum_out(block_order, grad_resid + first_pull(sum_parts(grad_one))[0], ())
    norm_own = lax.dynamic_slice_in_dim(small[:2], lax.axis_index(ALL) * shard, shard, 1)
    head_sum = small[2:, :head_dim] + small[2:, head_dim : 2 * head_dim]
    return (
        layer_out[None],
        input_grad[None],
        grad_q_out,
        grad_k_out,
        grad_v_out,
        grad_o_out.T,
        grad_g_out,
        grad_u_out,
        grad_d_out.T,
        norm_own.astype(BF),
        head_sum.astype(BF),
    )


def solution(mesh):
    def step(*arrays):
        return on_device(mesh.shape["dp"], *arrays)

    in_specs = (
        P("dp", "ctx", None),
        P("dp", "ctx"),
        P(("dp", "ctx"), None),
        P(("dp", "ctx"), None),
        P(("dp", "ctx"), None),
        P(None, ("dp", "ctx")),
        P(("dp", "ctx"), None),
        P(("dp", "ctx"), None),
        P(None, ("dp", "ctx")),
        P(None, ("dp", "ctx")),
        P(),
        P("dp", "ctx", None),
    )
    out_specs = (
        P("dp", "ctx", None),
        P("dp", "ctx", None),
        P(("dp", "ctx"), None),
        P(("dp", "ctx"), None),
        P(("dp", "ctx"), None),
        P(None, ("dp", "ctx")),
        P(("dp", "ctx"), None),
        P(("dp", "ctx"), None),
        P(None, ("dp", "ctx")),
        P(None, ("dp", "ctx")),
        P(),
    )
    return jax.shard_map(step, mesh=mesh, in_specs=in_specs, out_specs=out_specs, check_vma=False)
```

```python
import functools

import jax
import jax.numpy as jnp
from jax import lax
from jax.experimental import pallas as pl
from jax.experimental.pallas import tpu as pltpu
from jax.sharding import PartitionSpec as P

EPS = 1e-05
THETA = 1000000.0
BF = jnp.bfloat16
F32 = jnp.float32
ALL = ("dp", "ctx")


def add_low(*terms):
    total = terms[0].astype(F32)
    for term in terms[1:]:
        total = total + term.astype(F32)
    return total.astype(BF)


def flip(value, axis, size, bits):
    return lax.ppermute(value, axis, [(i, i ^ bits) for i in range(size)])


def gather_ctx(own):
    core = flip(own, "ctx", 4, 1)
    across = flip(own, "ctx", 4, 2)
    return [own, core, across, flip(across, "ctx", 4, 1)]


def scatter_ctx(parts):
    far = flip(parts[3], "ctx", 4, 1)
    near = flip(parts[1], "ctx", 4, 1)
    return parts[0], near, flip(add_low(parts[2], far), "ctx", 4, 2)


def sum_parts(parts):
    return parts[0].astype(F32) + parts[1].astype(F32) + parts[2].astype(F32)


def exchange_ctx(parts):
    return [parts[0]] + [flip(parts[j], "ctx", 4, j) for j in range(1, 4)]


def place(parts, where, axis):
    size = parts[0].shape[axis]
    shape = list(parts[0].shape)
    shape[axis] = size * len(parts)
    out = jnp.zeros(shape, parts[0].dtype)
    for part, at in zip(parts, where):
        out = lax.dynamic_update_slice_in_dim(out, part, at * size, axis)
    return out


def bar(*trees):
    return lax.optimization_barrier(trees)


def ordered(dp_size):
    return dp_size == 8


def dp_order(dp_size):
    me = lax.axis_index("dp")
    return [((me - 2 * (i % 4)) % dp_size) ^ (i // 4) for i in range(dp_size)]


def across_y(value):
    return flip(value, "dp", 8, 1)


def along_z(value):
    return lax.ppermute(value, "dp", [(i, (i + 2) % 8) for i in range(8)])


def sum_all(value, dp_size):
    for bits in (1, 2):
        value = value + flip(value, "ctx", 4, bits)
    bits = 1
    while bits < dp_size:
        value = value + flip(value, "dp", dp_size, bits)
        bits *= 2
    return value


def dot(a, b):
    return lax.dot_general(a, b, (((1,), (0,)), ((), ())), preferred_element_type=F32)


def dot_nt(a, b):
    return lax.dot_general(a, b, (((1,), (1,)), ((), ())), preferred_element_type=F32)


def dot_tn(a, b):
    return lax.dot_general(a, b, (((0,), (0,)), ((), ())), preferred_element_type=F32)


VMEM = pl.BlockSpec(memory_space=pltpu.VMEM)
SMEM = pl.BlockSpec(memory_space=pltpu.SMEM)
LANES = 128
HIGH = lax.Precision.HIGHEST


HEAVY = 10**11


def call(body, outs, ins, scratch=(), scalars=0, limit=4, flops=1000000, held=False):
    def spec(shape):
        if held:
            return VMEM
        zeros = (0,) * len(shape)
        return pl.BlockSpec(tuple(shape), lambda i: zeros, pipeline_mode=pl.Buffered(1))

    return pl.pallas_call(
        body,
        out_shape=[jax.ShapeDtypeStruct(shape, kind) for shape, kind in outs],
        grid=() if held else (1,),
        in_specs=[SMEM] * scalars + [spec(x.shape) for x in ins[scalars:]],
        out_specs=[spec(shape) for shape, _ in outs],
        scratch_shapes=list(scratch),
        compiler_params=pltpu.CompilerParams(vmem_limit_bytes=limit << 20),
        cost_estimate=pl.CostEstimate(flops=flops, bytes_accessed=1000, transcendentals=0),
    )(*ins)


def pack_body(order_ref, tokens_ref, docs_ref, out_ref):
    rows = tokens_ref.shape[0]
    for i in range(tokens_ref.shape[1] // LANES):
        at = pl.ds(pl.multiple_of(order_ref[i] * LANES, LANES), LANES)
        out_ref[:rows, i * LANES : (i + 1) * LANES] = tokens_ref[:, at]
    if docs_ref is not None:
        below = jnp.broadcast_to(docs_ref[...].astype(F32), (16, rows)).astype(BF)
        out_ref[rows:, :rows] = below
        out_ref[rows:, rows:] = jnp.zeros((16, out_ref.shape[1] - rows), BF)


def pack_rows(order, rows, doc_row=None):
    if doc_row is None:
        body = lambda order_ref, rows_ref, out_ref: pack_body(order_ref, rows_ref, None, out_ref)
        return call(body, [(rows.shape, BF)], [order, rows], scalars=1)[0]
    shape = (rows.shape[0] + 16, rows.shape[1])
    return call(pack_body, [(shape, BF)], [order, rows, doc_row.reshape(1, -1)], scalars=1)[0]


def sum_body(order_ref, base_ref, *refs):
    parts, out_ref = refs[:-1], refs[-1]
    for i in range(base_ref.shape[1] // LANES):
        at = slice(i * LANES, (i + 1) * LANES)
        total = base_ref[:, at]
        if parts:
            part = parts[0][:, at].astype(F32)
            for ref in parts[1:]:
                part = part + ref[:, at].astype(F32)
            total = total + part
        to = pl.ds(pl.multiple_of(order_ref[i] * LANES, LANES), LANES)
        out_ref[:, to] = total.astype(BF)


def sum_out(order, base, parts):
    return call(sum_body, [(base.shape, BF)], [order, base, *parts], scalars=1)[0]


def lane_masks(rows):
    lane = lax.broadcasted_iota(jnp.int32, (rows, LANES), 1)
    return lane < 64, lax.rem(lane, 64) < 32


def half_sums(squares):
    row = lax.broadcasted_iota(jnp.int32, (LANES, LANES), 0) // 64
    col = lax.broadcasted_iota(jnp.int32, (LANES, LANES), 1) // 64
    return jnp.dot(
        squares, (row == col).astype(F32), preferred_element_type=F32, precision=HIGH
    )


def turn(value, first):
    return jnp.where(first, pltpu.roll(value, 96, 1), pltpu.roll(value, 32, 1))


def doubled(value, left):
    other = pltpu.roll(value, 64, 1)
    return jnp.where(left, value, other), jnp.where(left, other, value)


def prepare_body(rows, *refs):
    packs, blocks = refs[:4], refs[4:12]
    cos_ref, sin_ref, head_ref = refs[12:15]
    normed_ref, qk_pre_ref, q_ref, kd_ref, vd_ref, kt_ref, vt_ref = refs[15:22]
    wqkv_ref, wo_ref, gains_ref, all_ref = refs[22:26]
    for i, block in enumerate(blocks):
        at = i * LANES
        wqkv_ref[at : at + LANES, :] = block[:LANES, :512]
        wo_ref[at : at + LANES, :] = block[:LANES, 512:]
        gains_ref[:, at : at + LANES] = block[LANES : LANES + 8, :LANES].astype(F32)
    for j, pack in enumerate(packs):
        all_ref[j * rows : (j + 1) * rows, :] = pack[:rows, :]
    left, first = lane_masks(LANES)
    gain = gains_ref[0:1, :]
    q_gain, k_gain = head_ref[0:1, :], head_ref[1:2, :]

    def chunk(i, _):
        at = pl.ds(pl.multiple_of(i * LANES, LANES), LANES)
        x = all_ref[at, :].astype(F32)
        scale = lax.rsqrt(jnp.mean(x * x, -1, keepdims=True) + EPS)
        normed = (x * scale * gain).astype(BF)
        normed_ref[at, :] = normed
        pre = jnp.dot(normed, wqkv_ref[...], preferred_element_type=F32)
        qk_pre_ref[at, :] = pre[:, :384]
        cos, sin = cos_ref[at, :], sin_ref[at, :]
        turned = []
        for b in range(3):
            u = pre[:, b * LANES : (b + 1) * LANES]
            u = u * lax.rsqrt(half_sums(u * u) * (1.0 / 64) + EPS) * (k_gain if b == 2 else q_gain)
            turned.append(u * cos + turn(u, first) * sin)
        q_ref[0, at, :] = turned[0].astype(BF)
        q_ref[1, at, :] = turned[1].astype(BF)
        key, value = turned[2], pre[:, 384:]
        for both, flat, one in ((kd_ref, kt_ref, key), (vd_ref, vt_ref, value)):
            low, high = doubled(one, left)
            both[0, at, :] = low.astype(BF)
            both[1, at, :] = high.astype(BF)
            flat[:, at] = one.T.astype(BF)
        return 0

    lax.fori_loop(0, all_ref.shape[0] // LANES, chunk, 0)


def two_heads(block, left):
    zero = jnp.zeros_like(block)
    return jnp.concatenate([jnp.where(left, block, zero), jnp.where(left, zero, block)], 0)


def seen(start_row, first_key, rows, first_query):
    shape = (rows, 2 * rows)
    key = lax.broadcasted_iota(jnp.int32, shape, 0)
    mask = key + first_key >= start_row
    if first_query is not None:
        lane = lax.broadcasted_iota(jnp.int32, shape, 1)
        mask = mask & (key <= jnp.where(lane < rows, lane, lane - rows))
    return mask


LOG2E = 1.4426950408889634
SCORE = LOG2E / 8.0


def attend_body(rows, me_ref, first_ref, q_ref, kd_ref, vt_ref, start_ref, wo_ref, *refs):
    parts = refs[:4]
    out_ref, wide_ref, lse_ref, sum_ref, acc_ref = refs[4:9]
    me = me_ref[0]
    left = lax.broadcasted_iota(jnp.int32, (rows, LANES), 1) < 64

    def one(step, _):
        kv, a = step // 4, lax.rem(step, 4)
        at_q = pl.ds(pl.multiple_of((a ^ me) * rows, rows), rows)
        q2 = two_heads(q_ref[kv, at_q, :], left)
        start_row = start_ref[a ^ me]
        sum_ref[...] = jnp.zeros_like(sum_ref)
        acc_ref[...] = jnp.zeros_like(acc_ref)
        for d in range(3):

            @pl.when((a >= d) & (first_ref[a ^ me] < (a - d + 1) * rows))
            def _():
                at_k = pl.ds(pl.multiple_of(((a - d) ^ me) * rows, rows), rows)
                scores = dot_nt(kd_ref[kv, at_k, :], q2)
                mask = seen(start_row, (a - d) * rows, rows, a if d == 0 else None)
                p = jnp.where(mask, jnp.exp2(scores * SCORE), 0.0)
                sum_ref[...] += jnp.sum(p, 0, keepdims=True)
                half = pl.ds(pl.multiple_of(kv * 64, 64), 64)
                acc_ref[...] += dot(vt_ref[half, at_k], p.astype(BF))

        total = sum_ref[...]
        lse_ref[kv * 4 + (a ^ me)] = jnp.log2(total)
        mixed = acc_ref[...] / total
        mixed = jnp.concatenate([mixed[:, :rows], mixed[:, rows:]], 0).T
        wide_ref[kv, at_q, :] = mixed
        out_ref[at_q, columns(kv, LANES)] = mixed.astype(BF)
        return 0

    lax.fori_loop(0, 8, one, 0)
    for j in range(4):
        at = slice(j * rows, (j + 1) * rows)
        parts[j][...] = dot_nt(out_ref[at, :], wo_ref[...]).astype(BF)


def attend_back_body(rows, *refs):
    me_ref, first_ref = refs[:2]
    refs = refs[1:]
    g0, g1, g2, g3, q_ref, kd_ref, vd_ref, kt_ref, start_ref, wide_ref, lse_ref = refs[1:12]
    qk_pre_ref, cos_ref, sin_ref, head_ref, wqkv_ref, wo_ref, normed_ref, gains_ref = refs[12:20]
    parts, low_ref, head_sum_ref, gain_sum_ref, grad_ref = refs[20:24], *refs[24:28]
    mixed_ref, dq_ref, dk_ref, dv_ref, acc_ref = refs[28:33]
    me = me_ref[0]
    left = lax.broadcasted_iota(jnp.int32, (rows, LANES), 1) < 64
    for j, g in enumerate((g0, g1, g2, g3)):
        grad_ref[j * rows : (j + 1) * rows, :] = g[...]
        grad = dot(g[...], wo_ref[...]).astype(BF)
        mixed_ref[0, j * rows : (j + 1) * rows, :] = grad[:, :LANES]
        mixed_ref[1, j * rows : (j + 1) * rows, :] = grad[:, LANES:]
    dk_ref[...] = jnp.zeros_like(dk_ref)
    dv_ref[...] = jnp.zeros_like(dv_ref)
    pick = (
        lax.broadcasted_iota(jnp.int32, (8, LANES), 1) // 64
        == lax.broadcasted_iota(jnp.int32, (8, LANES), 0)
    ).astype(F32)

    def one(step, _):
        kv, a = step // 4, lax.rem(step, 4)
        at_q = pl.ds(pl.multiple_of((a ^ me) * rows, rows), rows)
        q2 = two_heads(q_ref[kv, at_q, :], left)
        grad = mixed_ref[kv, at_q, :]
        g2 = two_heads(grad, left)
        inner = lax.dot_general(
            pick,
            grad.astype(F32) * wide_ref[kv, at_q, :],
            (((1,), (1,)), ((), ())),
            preferred_element_type=F32,
            precision=HIGH,
        )
        inner = jnp.concatenate([inner[0:1], inner[1:2]], 1)
        lse = lse_ref[kv * 4 + (a ^ me)]
        start_row = start_ref[a ^ me]
        acc_ref[...] = jnp.zeros_like(acc_ref)
        for d in range(3):

            @pl.when((a >= d) & (first_ref[a ^ me] < (a - d + 1) * rows))
            def _():
                at_k = pl.ds(pl.multiple_of(((a - d) ^ me) * rows, rows), rows)
                scores = dot_nt(kd_ref[kv, at_k, :], q2)
                mask = seen(start_row, (a - d) * rows, rows, a if d == 0 else None)
                p = jnp.where(mask, jnp.exp2(scores * SCORE - lse), 0.0)
                gp = dot_nt(vd_ref[kv, at_k, :], g2)
                gs = (p * (gp - inner)).astype(BF)
                dv_ref[kv, at_k, :] += dot(p.astype(BF), g2)
                dk_ref[kv, at_k, :] += dot(gs, q2)
                half = pl.ds(pl.multiple_of(kv * 64, 64), 64)
                acc_ref[...] += dot(kt_ref[half, at_k], gs)

        both = acc_ref[...] * 0.125
        dq_ref[kv, at_q, :] = jnp.concatenate([both[:, :rows], both[:, rows:]], 0).T
        return 0

    lax.fori_loop(0, 8, one, 0)
    left, first = lane_masks(LANES)
    head_sum_ref[...] = jnp.zeros_like(head_sum_ref)

    def folded(ref, at):
        low, high = ref[0, at, :], ref[1, at, :]
        low, high = low + pltpu.roll(low, 64, 1), high + pltpu.roll(high, 64, 1)
        return jnp.where(left, low, high)

    def chunk(i, _):
        at = pl.ds(pl.multiple_of(i * LANES, LANES), LANES)
        cos, sin = cos_ref[at, :], sin_ref[at, :]
        for b in range(3):
            u = qk_pre_ref[at, b * LANES : (b + 1) * LANES]
            g = folded(dk_ref, at) * 0.125 if b == 2 else dq_ref[b, at, :]
            w = g * cos - turn(g, first) * sin
            row = 1 if b == 2 else 0
            gain = head_ref[row : row + 1, :]
            r = lax.rsqrt(half_sums(u * u) * (1.0 / 64) + EPS)
            head_sum_ref[row : row + 1, :] += jnp.sum(w * u * r, 0, keepdims=True)
            w = w * gain
            back = r * w - u * (r * r * r) * (half_sums(w * u) * (1.0 / 64))
            low_ref[at, b * LANES : (b + 1) * LANES] = back.astype(BF)
        low_ref[at, 384:] = folded(dv_ref, at).astype(BF)
        return 0

    lax.fori_loop(0, low_ref.shape[0] // LANES, chunk, 0)
    gain_sum = jnp.zeros((1, normed_ref.shape[1]), F32)
    for j in range(4):
        at = slice(j * rows, (j + 1) * rows)
        grad = dot_nt(low_ref[at, :], wqkv_ref[...])
        parts[j][...] = grad.astype(BF)
        gain_sum = gain_sum + jnp.sum(grad * normed_ref[at, :].astype(F32), 0, keepdims=True)
    gain_sum_ref[...] = gain_sum / gains_ref[0:1, :]


def columns(at, width):
    return pl.ds(pl.multiple_of(at * width, LANES), width)


def spread_body(widths, me_ref, *refs):
    weights, outs = refs[: len(widths)], refs[-4:]
    rows = weights[0].shape[0]
    me = me_ref[0]
    for j, out in enumerate(outs):
        start = 0
        for weight, width in zip(weights, widths):
            out[:rows, start : start + width] = weight[:, columns(me ^ j, width)]
            start += width
    if len(refs) > len(widths) + 4:
        gains = refs[len(widths)][...].astype(F32)
        gains = jnp.concatenate([gains, jnp.zeros((6, rows), F32)], 0)
        gains = jnp.concatenate([gains] * (LANES // rows), 1)
        lane = lax.broadcasted_iota(jnp.int32, (8, LANES), 1)
        gains = jnp.where(lane // rows == me, gains, 0.0).astype(BF)
        for out in outs:
            out[rows:, :] = jnp.zeros((8, out.shape[1]), BF)
            out[rows:, :LANES] = gains


def join_body(rows, me_ref, *refs):
    pieces, out = refs[:4], refs[4]
    me = me_ref[0]
    for j, piece in enumerate(pieces):
        out[pl.ds(pl.multiple_of((me ^ j) * rows, rows), rows), :] = piece[:rows, :]
    if pieces[0].shape[0] > rows:
        below = [piece[rows:, :].astype(F32) for piece in pieces]
        out[4 * rows :, :] = (below[0] + below[1] + below[2] + below[3]).astype(BF)


def part_body(me_ref, one_ref, two_ref, three_ref, *refs):
    outs, total_ref = refs[:4], refs[4]
    total = one_ref[...].astype(F32) + two_ref[...].astype(F32) + three_ref[...].astype(F32)
    total_ref[...] = total
    rows = outs[0].shape[0]
    for j, out in enumerate(outs):
        at = pl.ds(pl.multiple_of((me_ref[0] ^ j) * rows, rows), rows)
        out[...] = total_ref[at, :].astype(BF)


def land_body(widths, me_ref, *refs):
    pieces, outs = refs[:4], refs[4:]
    me = me_ref[0]
    start = 0
    for out, width in zip(outs, widths):
        for j, piece in enumerate(pieces):
            out[:, columns(me ^ j, width)] = piece[:, start : start + width]
        start += width


def small_body(order_ref, one_ref, two_ref, head_ref, *refs):
    out_ref = refs[-1]
    out_ref[...] = jnp.zeros_like(out_ref)
    for i in range(one_ref.shape[1] // LANES):
        at = columns(order_ref[i], LANES)
        out_ref[0:1, at] = one_ref[:, i * LANES : (i + 1) * LANES]
        out_ref[1:2, at] = two_ref[:, i * LANES : (i + 1) * LANES]
    out_ref[2:4, :LANES] = head_ref[0:2, :]


def feed_body(rows, pieces, *refs):
    normed, packs, weights = refs[:4], refs[4:8], refs[8 : 8 + pieces]
    parts = refs[8 + pieces : 12 + pieces]
    hidden_ref, gate_ref, up_ref, down_ref, normed_ref, grad_ref = refs[12 + pieces : 18 + pieces]
    w_ref, part_ref = refs[18 + pieces :]
    ff = hidden_ref.shape[1]
    row = 0
    for weight in weights:
        w_ref[row : row + weight.shape[0], :] = weight[...]
        down_ref[row : row + weight.shape[0], :] = weight[:, 2 * ff :]
        row += weight.shape[0]
    for j in range(4):
        normed_ref[j * rows : (j + 1) * rows, :] = normed[j][...]
        grad_ref[j * rows : (j + 1) * rows, :] = packs[j][...]

    def one(i, _):
        at = pl.ds(pl.multiple_of(i * rows, rows), rows)
        x = normed_ref[at, :]
        gate, up = dot(x, w_ref[:, :ff]), dot(x, w_ref[:, ff : 2 * ff])
        grad = dot(grad_ref[at, :], w_ref[:, 2 * ff :])
        sig = 1.0 / (1.0 + jnp.exp(-gate))
        silu = gate * sig
        hidden_ref[at, :] = (silu * up).astype(BF)
        grad_gate = (grad * up * (sig * (1.0 + gate * (1.0 - sig)))).astype(BF)
        grad_up = (grad * silu).astype(BF)
        gate_ref[at, :] = grad_gate
        up_ref[at, :] = grad_up
        total = dot_nt(grad_gate, w_ref[:, :ff]) + dot_nt(grad_up, w_ref[:, ff : 2 * ff])
        part_ref[at, :] = total.astype(BF)
        return 0

    lax.fori_loop(0, 4, one, 0)
    for j in range(4):
        parts[j][...] = part_ref[j * rows : (j + 1) * rows, :]


def down_body(rows, hidden_ref, down_ref, *parts):
    for j in range(4):
        at = slice(j * rows, (j + 1) * rows)
        parts[j][...] = dot_nt(hidden_ref[at, :], down_ref[...]).astype(BF)


def attn_weights_body(normed_ref, grad_qkv_ref, grad_ref, out_ref, *chunks):
    cut = grad_qkv_ref.shape[1]
    one = dot_tn(normed_ref[...], grad_qkv_ref[...]).astype(BF)
    two = dot_tn(grad_ref[...], out_ref[...]).astype(BF)
    for i, chunk in enumerate(chunks):
        at = slice(i * LANES, (i + 1) * LANES)
        chunk[:, :cut] = one[at]
        chunk[:, cut:] = two[at]


def rms_scale(values, gain_row):
    return values * lax.rsqrt(jnp.mean(values * values, -1, keepdims=True) + EPS) * gain_row


def place_all(pieces, me, widths):
    outs, start = [], 0
    for width in widths:
        cut = [p[:, start : start + width] for p in pieces]
        outs.append(place(cut, [me ^ j for j in range(4)], 1))
        start += width
    return outs


def on_device(
    dp_size,
    tokens,
    doc_ids,
    w_query,
    key_weight,
    value_weight,
    w_output,
    w_gate,
    w_up,
    w_down,
    norm_gains,
    head_norm_gains,
    out_grad,
):
    local_len, model_dim = tokens.shape[1:]
    tokens, out_grad, doc_row = tokens[0], out_grad[0], doc_ids[0]
    head_dim = head_norm_gains.shape[1]
    q_cols, kv_cols = w_query.shape[1] // 4, key_weight.shape[1] // 4
    shard = norm_gains.shape[1]
    ff_cols = w_gate.shape[1] // 4
    me = lax.axis_index("ctx")
    places = [me ^ j for j in range(4)]
    full_len = 4 * local_len
    fast = ordered(dp_size)
    block_order = jnp.stack(dp_order(dp_size)) if fast else jnp.arange(model_dim // LANES)
    block_order = block_order.astype(jnp.int32)
    me_row = me.reshape(1).astype(jnp.int32)
    attn_widths = (q_cols, kv_cols, kv_cols, q_cols)
    ff_widths = (ff_cols, ff_cols, ff_cols)
    wide, ff_wide = sum(attn_widths), sum(ff_widths)
    attn_local = [w_query, key_weight, value_weight, w_output.T]
    ff_local = [w_gate, w_up, w_down.T]

    pack = pack_rows(block_order, tokens, doc_row)
    grad_pack = pack_rows(block_order, out_grad)
    if fast:
        sent = call(
            functools.partial(spread_body, attn_widths),
            [((shard + 8, wide), BF)] * 4,
            [me_row, *attn_local, norm_gains],
            scalars=1,
        )
        ff_sent = call(
            functools.partial(spread_body, ff_widths),
            [((shard, ff_wide), BF)] * 4,
            [me_row, *ff_local],
            scalars=1,
        )
        got, ff_sent = bar(exchange_ctx(sent), ff_sent)
        ff_got = exchange_ctx(ff_sent)
        (block,) = call(
            functools.partial(join_body, shard),
            [((4 * shard + 8, wide), BF)],
            [me_row, *got],
            scalars=1,
        )
        y0, z1, pack, ff_got = bar(across_y(block), along_z(block), pack, ff_got)
        core_pack, far_pack = flip(pack, "ctx", 4, 1), flip(pack, "ctx", 4, 2)
        y1, z2 = bar(across_y(z1), along_z(z1))
        (ff_block,) = call(
            functools.partial(join_body, shard),
            [((4 * shard, ff_wide), BF)],
            [me_row, *ff_got],
            scalars=1,
        )
        y2, z3, far_pack, grad_pack, ff_block = bar(
            across_y(z2), along_z(z2), far_pack, grad_pack, ff_block
        )
        far_core_pack = flip(far_pack, "ctx", 4, 1)
        y3, ff_block, far_core_pack = bar(across_y(z3), ff_block, far_core_pack)
        ff_z1, ff_y0 = along_z(ff_block), across_y(ff_block)
        blocks = [block, z1, z2, z3, y0, y1, y2, y3]
    else:

        def pieces_of(weights):
            sent = []
            for at in places:
                cut = [
                    lax.dynamic_slice_in_dim(w, at * (w.shape[1] // 4), w.shape[1] // 4, 1)
                    for w in weights
                ]
                sent.append(jnp.concatenate(cut, 1))
            return sent

        def whole(weights):
            block = place(exchange_ctx(pieces_of(weights)), places, 0)
            return lax.all_gather(block, "dp", axis=0, tiled=True)

        gains = lax.all_gather(norm_gains, ALL, axis=1, tiled=True).reshape(2, -1, LANES)
        gains = jnp.pad(gains.transpose(1, 0, 2), ((0, 0), (0, 6), (0, wide - LANES)))
        blocks = jnp.concatenate([whole(attn_local).reshape(-1, LANES, wide), gains], 1)
        blocks = [blocks[i] for i in range(blocks.shape[0])]
        ff_w = [whole(ff_local)]
        core_pack, far_pack = flip(pack, "ctx", 4, 1), flip(pack, "ctx", 4, 2)
        far_core_pack = flip(far_pack, "ctx", 4, 1)

    packs = [pack, core_pack, far_pack, far_core_pack]
    core_grad, far_grad = flip(grad_pack, "ctx", 4, 1), flip(grad_pack, "ctx", 4, 2)
    docs = jnp.concatenate([p[local_len, :local_len] for p in packs])
    index = jnp.concatenate(
        [at * local_len + jnp.arange(local_len, dtype=jnp.int32) for at in places]
    )
    starts = jnp.sum((docs[None, :] < docs[:, None]).astype(jnp.int32), -1)
    positions = (index - starts).astype(F32)
    half = head_dim // 2
    lane = jnp.arange(LANES)
    freqs = THETA ** (-(2.0 * (lane % half).astype(F32)) / head_dim)
    angles = positions[:, None] * freqs
    cosine = jnp.cos(angles)
    sine = jnp.sin(angles) * jnp.where(lane % head_dim < half, -1.0, 1.0)
    starts = starts.reshape(4, local_len)
    firsts = starts[:, 0]
    starts = jnp.concatenate([starts, starts], 1).reshape(4, 1, 2 * local_len)
    head_gains = jnp.concatenate([head_norm_gains, head_norm_gains], 1).astype(F32)

    part_shapes = [((local_len, model_dim), BF)] * 4
    normed_one, qk_pre, queries, keys, values, keys_t, values_t, w_qkv, wo_t, gains = call(
        functools.partial(prepare_body, local_len),
        [
            ((full_len, model_dim), BF),
            ((full_len, q_cols + kv_cols), F32),
            ((2, full_len, LANES), BF),
            ((2, full_len, LANES), BF),
            ((2, full_len, LANES), BF),
            ((LANES, full_len), BF),
            ((LANES, full_len), BF),
            ((model_dim, q_cols + 2 * kv_cols), BF),
            ((model_dim, q_cols), BF),
            ((8, model_dim), F32),
        ],
        [*packs, *blocks, cosine, sine, head_gains],
        [pltpu.VMEM((full_len, model_dim), BF)],
        limit=28,
        flops=HEAVY,
    )
    if fast:
        queries, keys, ff_z1, ff_y0, core_grad, far_grad = bar(
            queries, keys, ff_z1, ff_y0, core_grad, far_grad
        )
        ff_z2, ff_y1 = along_z(ff_z1), across_y(ff_z1)
    grad_packs = [grad_pack, core_grad, far_grad, flip(far_grad, "ctx", 4, 1)]
    *resid_parts, attn_out, attn_wide, lse = call(
        functools.partial(attend_body, local_len),
        part_shapes
        + [
            ((full_len, q_cols), BF),
            ((2, full_len, LANES), F32),
            ((8, 1, 2 * local_len), F32),
        ],
        [me_row, firsts, queries, keys, values_t, starts, wo_t],
        [pltpu.VMEM((1, 2 * local_len), F32), pltpu.VMEM((head_dim, 2 * local_len), F32)],
        scalars=2,
        limit=20,
    )
    own_tokens = pack[:local_len].astype(F32)
    own_grad = grad_pack.astype(F32)
    near_one, far_one = flip(resid_parts[1], "ctx", 4, 1), flip(resid_parts[3], "ctx", 4, 1)
    far_one = add_low(resid_parts[2], far_one)
    if fast:
        far_one, ff_z2, ff_y1 = bar(far_one, ff_z2, ff_y1)
        ff_z3, ff_y2 = along_z(ff_z2), across_y(ff_z2)
    far_one = flip(far_one, "ctx", 4, 2)
    resid = own_tokens + sum_parts((resid_parts[0], near_one, far_one))
    normed_own = rms_scale(resid, gains[1]).astype(BF)
    normed_core, normed_far = flip(normed_own, "ctx", 4, 1), flip(normed_own, "ctx", 4, 2)
    if fast:
        normed_far, ff_z3, ff_y2 = bar(normed_far, ff_z3, ff_y2)
        cut = ff_block.shape[0] // 2
        ff_w = [ff_block, ff_z1, ff_z2, ff_z3, ff_y0, ff_y1, ff_y2]
        ff_w += [across_y(ff_z3[:cut]), along_z(ff_y2[cut:])]
    normed_two = [normed_own, normed_core, normed_far, flip(normed_far, "ctx", 4, 1)]

    ff_shape = ((full_len, ff_cols), BF)
    *two_parts, hidden, grad_gate, grad_up, w_down_own, normed_all, grad_all = call(
        functools.partial(feed_body, local_len, len(ff_w)),
        part_shapes
        + [ff_shape] * 3
        + [((model_dim, ff_cols), BF)]
        + [((full_len, model_dim), BF)] * 2,
        [*normed_two, *grad_packs, *ff_w],
        [pltpu.VMEM((model_dim, ff_wide), BF), pltpu.VMEM((full_len, model_dim), BF)],
        limit=32,
        held=True,
    )
    near_two, far_two = flip(two_parts[1], "ctx", 4, 1), flip(two_parts[3], "ctx", 4, 1)
    near_two, far_two, normed_all, grad_all = bar(near_two, far_two, normed_all, grad_all)
    far_two = flip(add_low(two_parts[2], far_two), "ctx", 4, 2)

    def ff_chunks(at):
        cut = [dot_tn(normed_all[:, at], g).astype(BF) for g in (grad_gate, grad_up)]
        cut.append(dot_tn(grad_all[:, at], hidden).astype(BF))
        rows = cut[0].shape[0] // 4
        return [
            jnp.concatenate([c[r * rows : (r + 1) * rows] for c in cut], 1) for r in range(4)
        ]

    def pieces_of_sum(last):
        wide = last[0].shape[1]
        return call(
            part_body,
            [((shard, wide), BF)] * 4,
            [me_row, *last],
            [pltpu.VMEM((4 * shard, wide), F32)],
            scalars=1,
            limit=12,
        )

    def land(pieces, widths):
        return call(
            functools.partial(land_body, widths),
            [((shard, 4 * width), BF) for width in widths],
            [me_row, *pieces],
            scalars=1,
        )

    def plain_sums(chunks, widths):
        mine = lax.psum_scatter(jnp.concatenate(chunks, 0), "dp", scatter_dimension=0, tiled=True)
        pieces = [lax.dynamic_slice_in_dim(mine, at * shard, shard, 0) for at in places]
        return place_all(exchange_ctx(pieces), me, widths)

    def tick(*values):
        def body(*refs):
            refs[-1][...] = jnp.zeros((8, LANES), BF)

        return pl.pallas_call(
            body,
            out_shape=jax.ShapeDtypeStruct((8, LANES), BF),
            in_specs=[pl.BlockSpec(memory_space=pl.ANY)] * len(values),
            out_specs=VMEM,
            cost_estimate=pl.CostEstimate(flops=HEAVY, bytes_accessed=1000, transcendentals=0),
        )(*values)

    middle = model_dim // 2
    far = ff_chunks(slice(middle, None))
    if fast:
        cut = 4 * shard // 2
        first, early = across_y(far[1][:cut]), along_z(far[1][cut:])
        grad_gate, grad_up, hidden, tick_one = bar(grad_gate, grad_up, hidden, tick(*far))
    near = ff_chunks(slice(0, middle))
    if fast:
        second = jnp.concatenate([far[2][:cut], add_low(far[2][cut:], early)], 0)
        total = jnp.concatenate([add_low(near[1][:cut], first), near[1][cut:]], 0)
        near_two, far_two, total, second = bar(near_two, far_two, total, second)
        total, second = along_z(total), across_y(second)
    grad_norm_two = sum_parts((two_parts[0], near_two, far_two))
    _, second_pull = jax.vjp(rms_scale, resid, gains[1])
    grad_resid_norm, grad_gain_two = second_pull(grad_norm_two)
    grad_resid = own_grad + grad_resid_norm
    (*down_parts,) = call(
        functools.partial(down_body, local_len), part_shapes, [hidden, w_down_own], limit=16
    )

    grad_low = grad_resid.astype(BF)
    grad_core, grad_far = flip(grad_low, "ctx", 4, 1), flip(grad_low, "ctx", 4, 2)
    if fast:
        grad_far, down_parts = bar(grad_far, down_parts)
    down_near, down_far = flip(down_parts[1], "ctx", 4, 1), flip(down_parts[3], "ctx", 4, 1)
    down_far = add_low(down_parts[2], down_far)
    grad_attn = [grad_low, grad_core, grad_far, flip(grad_far, "ctx", 4, 1)]
    if fast:
        total, third = bar(add_low(near[2], second, total), far[3])
        grad_attn, down_far, tick_two = bar(grad_attn, down_far, tick(total))
        total, third = along_z(total), across_y(third)
    down_far = flip(down_far, "ctx", 4, 2)
    *one_parts, grad_qkv, head_sums, gain_one, grad_attn_all = call(
        functools.partial(attend_back_body, local_len),
        part_shapes
        + [
            ((full_len, q_cols + 2 * kv_cols), BF),
            ((8, LANES), F32),
            ((1, model_dim), F32),
            ((full_len, model_dim), BF),
        ],
        [
            me_row,
            firsts,
            *grad_attn,
            queries,
            keys,
            values,
            keys_t,
            starts,
            attn_wide,
            lse,
            qk_pre,
            cosine,
            sine,
            head_gains,
            w_qkv,
            wo_t,
            normed_one,
            gains,
        ],
        [
            pltpu.VMEM((2, full_len, LANES), BF),
            pltpu.VMEM((2, full_len, LANES), F32),
            pltpu.VMEM((2, full_len, LANES), F32),
            pltpu.VMEM((2, full_len, LANES), F32),
            pltpu.VMEM((head_dim, 2 * local_len), F32),
        ],
        scalars=2,
        limit=24,
        held=True,
    )
    if fast:
        fourth, grad_qkv = bar(far[0], grad_qkv)
        fourth = across_y(fourth)
        total, grad_qkv = bar(add_low(near[3], third, total), grad_qkv)
        last = (near[0], fourth, along_z(total))
    layer_out = sum_out(block_order, resid, (down_parts[0], down_near, down_far))
    attn_chunks = call(
        attn_weights_body,
        [((LANES, wide), BF)] * 8,
        [normed_one, grad_qkv, grad_attn_all, attn_out],
        limit=20,
    )
    ticks = [tick_one, tick_two] if fast else []
    (small,) = call(
        small_body,
        [((4, model_dim), F32)],
        [block_order, gain_one, grad_gain_two.reshape(1, -1), head_sums, *ticks],
        scalars=1,
    )
    grad_one = scatter_ctx(one_parts)
    if fast:
        near, far = attn_chunks[:4], attn_chunks[4:]
        small = small + flip(small, "ctx", 4, 1)
        small = small + flip(small, "ctx", 4, 2)
        total, small_y, last = bar(
            add_low(near[1], across_y(far[1])), flip(small, "dp", dp_size, 1), last
        )
        small = small + small_y
        total, small_z = bar(
            add_low(near[2], across_y(far[2]), along_z(total)), flip(small, "dp", dp_size, 2)
        )
        small = small + small_z
        total, small_z = bar(
            add_low(near[3], across_y(far[3]), along_z(total)), flip(small, "dp", dp_size, 4)
        )
        small = small + small_z
        attn_last = (near[0], across_y(far[0]), along_z(total))
        ff_pieces = exchange_ctx(pieces_of_sum(last))
        attn_pieces = exchange_ctx(pieces_of_sum(attn_last))
        grad_g_out, grad_u_out, grad_d_out = land(ff_pieces, ff_widths)
        grad_q_out, grad_k_out, grad_v_out, grad_o_out = land(attn_pieces, attn_widths)
    else:
        grad_g_out, grad_u_out, grad_d_out = plain_sums(near + far, ff_widths)
        grad_q_out, grad_k_out, grad_v_out, grad_o_out = plain_sums(attn_chunks, attn_widths)
        small = sum_all(small, dp_size)
    _, first_pull = jax.vjp(lambda u: rms_scale(u, gains[0]), own_tokens)
    input_grad = sum_out(block_order, grad_resid + first_pull(sum_parts(grad_one))[0], ())
    norm_own = lax.dynamic_slice_in_dim(small[:2], lax.axis_index(ALL) * shard, shard, 1)
    head_sum = small[2:, :head_dim] + small[2:, head_dim : 2 * head_dim]
    return (
        layer_out[None],
        input_grad[None],
        grad_q_out,
        grad_k_out,
        grad_v_out,
        grad_o_out.T,
        grad_g_out,
        grad_u_out,
        grad_d_out.T,
        norm_own.astype(BF),
        head_sum.astype(BF),
    )


def solution(mesh):
    def step(*arrays):
        return on_device(mesh.shape["dp"], *arrays)

    in_specs = (
        P("dp", "ctx", None),
        P("dp", "ctx"),
        P(("dp", "ctx"), None),
        P(("dp", "ctx"), None),
        P(("dp", "ctx"), None),
        P(None, ("dp", "ctx")),
        P(("dp", "ctx"), None),
        P(("dp", "ctx"), None),
        P(None, ("dp", "ctx")),
        P(None, ("dp", "ctx")),
        P(),
        P("dp", "ctx", None),
    )
    out_specs = (
        P("dp", "ctx", None),
        P("dp", "ctx", None),
        P(("dp", "ctx"), None),
        P(("dp", "ctx"), None),
        P(("dp", "ctx"), None),
        P(None, ("dp", "ctx")),
        P(("dp", "ctx"), None),
        P(("dp", "ctx"), None),
        P(None, ("dp", "ctx")),
        P(None, ("dp", "ctx")),
        P(),
    )
    return jax.shard_map(step, mesh=mesh, in_specs=in_specs, out_specs=out_specs, check_vma=False)
```

```python
import functools

import jax
import jax.numpy as jnp
from jax import lax
from jax.experimental import pallas as pl
from jax.experimental.pallas import tpu as pltpu
from jax.sharding import PartitionSpec as P

EPS = 1e-05
THETA = 1000000.0
BF = jnp.bfloat16
F32 = jnp.float32
ALL = ("dp", "ctx")


def add_low(*terms):
    total = terms[0].astype(F32)
    for term in terms[1:]:
        total = total + term.astype(F32)
    return total.astype(BF)


def flip(value, axis, size, bits):
    return lax.ppermute(value, axis, [(i, i ^ bits) for i in range(size)])


def gather_ctx(own):
    core = flip(own, "ctx", 4, 1)
    across = flip(own, "ctx", 4, 2)
    return [own, core, across, flip(across, "ctx", 4, 1)]


def scatter_ctx(parts):
    far = flip(parts[3], "ctx", 4, 1)
    near = flip(parts[1], "ctx", 4, 1)
    return parts[0], near, flip(add_low(parts[2], far), "ctx", 4, 2)


def sum_parts(parts):
    return parts[0].astype(F32) + parts[1].astype(F32) + parts[2].astype(F32)


def exchange_ctx(parts):
    return [parts[0]] + [flip(parts[j], "ctx", 4, j) for j in range(1, 4)]


def place(parts, where, axis):
    size = parts[0].shape[axis]
    shape = list(parts[0].shape)
    shape[axis] = size * len(parts)
    out = jnp.zeros(shape, parts[0].dtype)
    for part, at in zip(parts, where):
        out = lax.dynamic_update_slice_in_dim(out, part, at * size, axis)
    return out


def bar(*trees):
    return lax.optimization_barrier(trees)


def ordered(dp_size):
    return dp_size == 8


def dp_order(dp_size):
    me = lax.axis_index("dp")
    return [((me - 2 * (i % 4)) % dp_size) ^ (i // 4) for i in range(dp_size)]


def across_y(value):
    return flip(value, "dp", 8, 1)


def along_z(value):
    return lax.ppermute(value, "dp", [(i, (i + 2) % 8) for i in range(8)])


def sum_all(value, dp_size):
    for bits in (1, 2):
        value = value + flip(value, "ctx", 4, bits)
    bits = 1
    while bits < dp_size:
        value = value + flip(value, "dp", dp_size, bits)
        bits *= 2
    return value


def dot(a, b):
    return lax.dot_general(a, b, (((1,), (0,)), ((), ())), preferred_element_type=F32)


def dot_nt(a, b):
    return lax.dot_general(a, b, (((1,), (1,)), ((), ())), preferred_element_type=F32)


def dot_tn(a, b):
    return lax.dot_general(a, b, (((0,), (0,)), ((), ())), preferred_element_type=F32)


VMEM = pl.BlockSpec(memory_space=pltpu.VMEM)
SMEM = pl.BlockSpec(memory_space=pltpu.SMEM)
LANES = 128
HIGH = lax.Precision.HIGHEST


HEAVY = 10**11


def call(body, outs, ins, scratch=(), scalars=0, limit=4, flops=1000000, held=False):
    def spec(shape):
        if held:
            return VMEM
        zeros = (0,) * len(shape)
        return pl.BlockSpec(tuple(shape), lambda i: zeros, pipeline_mode=pl.Buffered(1))

    return pl.pallas_call(
        body,
        out_shape=[jax.ShapeDtypeStruct(shape, kind) for shape, kind in outs],
        grid=() if held else (1,),
        in_specs=[SMEM] * scalars + [spec(x.shape) for x in ins[scalars:]],
        out_specs=[spec(shape) for shape, _ in outs],
        scratch_shapes=list(scratch),
        compiler_params=pltpu.CompilerParams(vmem_limit_bytes=limit << 20),
        cost_estimate=pl.CostEstimate(flops=flops, bytes_accessed=1000, transcendentals=0),
    )(*ins)


def pack_body(order_ref, tokens_ref, docs_ref, out_ref):
    rows = tokens_ref.shape[0]
    for i in range(tokens_ref.shape[1] // LANES):
        at = pl.ds(pl.multiple_of(order_ref[i] * LANES, LANES), LANES)
        out_ref[:rows, i * LANES : (i + 1) * LANES] = tokens_ref[:, at]
    if docs_ref is not None:
        below = jnp.broadcast_to(docs_ref[...].astype(F32), (16, rows)).astype(BF)
        out_ref[rows:, :rows] = below
        out_ref[rows:, rows:] = jnp.zeros((16, out_ref.shape[1] - rows), BF)


def pack_rows(order, rows, doc_row=None):
    if doc_row is None:
        body = lambda order_ref, rows_ref, out_ref: pack_body(order_ref, rows_ref, None, out_ref)
        return call(body, [(rows.shape, BF)], [order, rows], scalars=1)[0]
    shape = (rows.shape[0] + 16, rows.shape[1])
    return call(pack_body, [(shape, BF)], [order, rows, doc_row.reshape(1, -1)], scalars=1)[0]


def sum_body(order_ref, base_ref, *refs):
    parts, out_ref = refs[:-1], refs[-1]
    for i in range(base_ref.shape[1] // LANES):
        at = slice(i * LANES, (i + 1) * LANES)
        total = base_ref[:, at]
        if parts:
            part = parts[0][:, at].astype(F32)
            for ref in parts[1:]:
                part = part + ref[:, at].astype(F32)
            total = total + part
        to = pl.ds(pl.multiple_of(order_ref[i] * LANES, LANES), LANES)
        out_ref[:, to] = total.astype(BF)


def sum_out(order, base, parts):
    return call(sum_body, [(base.shape, BF)], [order, base, *parts], scalars=1)[0]


def lane_masks(rows):
    lane = lax.broadcasted_iota(jnp.int32, (rows, LANES), 1)
    return lane < 64, lax.rem(lane, 64) < 32


def half_sums(squares):
    row = lax.broadcasted_iota(jnp.int32, (LANES, LANES), 0) // 64
    col = lax.broadcasted_iota(jnp.int32, (LANES, LANES), 1) // 64
    return jnp.dot(
        squares, (row == col).astype(F32), preferred_element_type=F32, precision=HIGH
    )


def turn(value, first):
    return jnp.where(first, pltpu.roll(value, 96, 1), pltpu.roll(value, 32, 1))


def doubled(value, left):
    other = pltpu.roll(value, 64, 1)
    return jnp.where(left, value, other), jnp.where(left, other, value)


def prepare_body(rows, *refs):
    packs, blocks = refs[:4], refs[4:12]
    cos_ref, sin_ref, head_ref = refs[12:15]
    normed_ref, qk_pre_ref, q_ref, kd_ref, vd_ref, kt_ref, vt_ref = refs[15:22]
    wqkv_ref, wo_ref, gains_ref, all_ref = refs[22:26]
    for i, block in enumerate(blocks):
        at = i * LANES
        wqkv_ref[at : at + LANES, :] = block[:LANES, :512]
        wo_ref[at : at + LANES, :] = block[:LANES, 512:]
        gains_ref[:, at : at + LANES] = block[LANES : LANES + 8, :LANES].astype(F32)
    for j, pack in enumerate(packs):
        all_ref[j * rows : (j + 1) * rows, :] = pack[:rows, :]
    left, first = lane_masks(LANES)
    gain = gains_ref[0:1, :]
    q_gain, k_gain = head_ref[0:1, :], head_ref[1:2, :]

    def chunk(i, _):
        at = pl.ds(pl.multiple_of(i * LANES, LANES), LANES)
        x = all_ref[at, :].astype(F32)
        scale = lax.rsqrt(jnp.mean(x * x, -1, keepdims=True) + EPS)
        normed = (x * scale * gain).astype(BF)
        normed_ref[at, :] = normed
        pre = jnp.dot(normed, wqkv_ref[...], preferred_element_type=F32)
        qk_pre_ref[at, :] = pre[:, :384]
        cos, sin = cos_ref[at, :], sin_ref[at, :]
        turned = []
        for b in range(3):
            u = pre[:, b * LANES : (b + 1) * LANES]
            u = u * lax.rsqrt(half_sums(u * u) * (1.0 / 64) + EPS) * (k_gain if b == 2 else q_gain)
            turned.append(u * cos + turn(u, first) * sin)
        q_ref[0, at, :] = turned[0].astype(BF)
        q_ref[1, at, :] = turned[1].astype(BF)
        key, value = turned[2], pre[:, 384:]
        for both, flat, one in ((kd_ref, kt_ref, key), (vd_ref, vt_ref, value)):
            low, high = doubled(one, left)
            both[0, at, :] = low.astype(BF)
            both[1, at, :] = high.astype(BF)
            flat[:, at] = one.T.astype(BF)
        return 0

    lax.fori_loop(0, all_ref.shape[0] // LANES, chunk, 0)


def two_heads(block, left):
    zero = jnp.zeros_like(block)
    return jnp.concatenate([jnp.where(left, block, zero), jnp.where(left, zero, block)], 0)


def seen(start_row, first_key, rows, first_query):
    shape = (rows, 2 * rows)
    key = lax.broadcasted_iota(jnp.int32, shape, 0)
    mask = key + first_key >= start_row
    if first_query is not None:
        lane = lax.broadcasted_iota(jnp.int32, shape, 1)
        mask = mask & (key <= jnp.where(lane < rows, lane, lane - rows))
    return mask


LOG2E = 1.4426950408889634
SCORE = LOG2E / 8.0


def attend_body(rows, me_ref, first_ref, q_ref, kd_ref, vt_ref, start_ref, wo_ref, *refs):
    parts = refs[:4]
    out_ref, wide_ref, lse_ref, sum_ref, acc_ref = refs[4:9]
    me = me_ref[0]
    left = lax.broadcasted_iota(jnp.int32, (rows, LANES), 1) < 64

    def one(step, _):
        kv, a = step // 4, lax.rem(step, 4)
        at_q = pl.ds(pl.multiple_of((a ^ me) * rows, rows), rows)
        q2 = two_heads(q_ref[kv, at_q, :], left)
        start_row = start_ref[a ^ me]
        sum_ref[...] = jnp.zeros_like(sum_ref)
        acc_ref[...] = jnp.zeros_like(acc_ref)
        for d in range(3):

            @pl.when((a >= d) & (first_ref[a ^ me] < (a - d + 1) * rows))
            def _():
                at_k = pl.ds(pl.multiple_of(((a - d) ^ me) * rows, rows), rows)
                scores = dot_nt(kd_ref[kv, at_k, :], q2)
                mask = seen(start_row, (a - d) * rows, rows, a if d == 0 else None)
                p = jnp.where(mask, jnp.exp2(scores * SCORE), 0.0)
                sum_ref[...] += jnp.sum(p, 0, keepdims=True)
                half = pl.ds(pl.multiple_of(kv * 64, 64), 64)
                acc_ref[...] += dot(vt_ref[half, at_k], p.astype(BF))

        total = sum_ref[...]
        lse_ref[kv * 4 + (a ^ me)] = jnp.log2(total)
        mixed = acc_ref[...] / total
        mixed = jnp.concatenate([mixed[:, :rows], mixed[:, rows:]], 0).T
        wide_ref[kv, at_q, :] = mixed
        out_ref[at_q, columns(kv, LANES)] = mixed.astype(BF)
        return 0

    lax.fori_loop(0, 8, one, 0)
    for j in range(4):
        at = slice(j * rows, (j + 1) * rows)
        parts[j][...] = dot_nt(out_ref[at, :], wo_ref[...]).astype(BF)


def attend_back_body(rows, *refs):
    me_ref, first_ref = refs[:2]
    refs = refs[1:]
    g0, g1, g2, g3, q_ref, kd_ref, vd_ref, kt_ref, start_ref, wide_ref, lse_ref = refs[1:12]
    qk_pre_ref, cos_ref, sin_ref, head_ref, wqkv_ref, wo_ref, normed_ref, gains_ref = refs[12:20]
    parts, low_ref, head_sum_ref, gain_sum_ref, grad_ref = refs[20:24], *refs[24:28]
    mixed_ref, dq_ref, dk_ref, dv_ref, acc_ref = refs[28:33]
    me = me_ref[0]
    left = lax.broadcasted_iota(jnp.int32, (rows, LANES), 1) < 64
    for j, g in enumerate((g0, g1, g2, g3)):
        grad_ref[j * rows : (j + 1) * rows, :] = g[...]
        grad = dot(g[...], wo_ref[...]).astype(BF)
        mixed_ref[0, j * rows : (j + 1) * rows, :] = grad[:, :LANES]
        mixed_ref[1, j * rows : (j + 1) * rows, :] = grad[:, LANES:]
    dk_ref[...] = jnp.zeros_like(dk_ref)
    dv_ref[...] = jnp.zeros_like(dv_ref)
    pick = (
        lax.broadcasted_iota(jnp.int32, (8, LANES), 1) // 64
        == lax.broadcasted_iota(jnp.int32, (8, LANES), 0)
    ).astype(F32)

    def one(step, _):
        kv, a = step // 4, lax.rem(step, 4)
        at_q = pl.ds(pl.multiple_of((a ^ me) * rows, rows), rows)
        q2 = two_heads(q_ref[kv, at_q, :], left)
        grad = mixed_ref[kv, at_q, :]
        g2 = two_heads(grad, left)
        inner = lax.dot_general(
            pick,
            grad.astype(F32) * wide_ref[kv, at_q, :],
            (((1,), (1,)), ((), ())),
            preferred_element_type=F32,
            precision=HIGH,
        )
        inner = jnp.concatenate([inner[0:1], inner[1:2]], 1)
        lse = lse_ref[kv * 4 + (a ^ me)]
        start_row = start_ref[a ^ me]
        acc_ref[...] = jnp.zeros_like(acc_ref)
        for d in range(3):

            @pl.when((a >= d) & (first_ref[a ^ me] < (a - d + 1) * rows))
            def _():
                at_k = pl.ds(pl.multiple_of(((a - d) ^ me) * rows, rows), rows)
                scores = dot_nt(kd_ref[kv, at_k, :], q2)
                mask = seen(start_row, (a - d) * rows, rows, a if d == 0 else None)
                p = jnp.where(mask, jnp.exp2(scores * SCORE - lse), 0.0)
                gp = dot_nt(vd_ref[kv, at_k, :], g2)
                gs = (p * (gp - inner)).astype(BF)
                dv_ref[kv, at_k, :] += dot(p.astype(BF), g2)
                dk_ref[kv, at_k, :] += dot(gs, q2)
                half = pl.ds(pl.multiple_of(kv * 64, 64), 64)
                acc_ref[...] += dot(kt_ref[half, at_k], gs)

        both = acc_ref[...] * 0.125
        dq_ref[kv, at_q, :] = jnp.concatenate([both[:, :rows], both[:, rows:]], 0).T
        return 0

    lax.fori_loop(0, 8, one, 0)
    left, first = lane_masks(LANES)
    head_sum_ref[...] = jnp.zeros_like(head_sum_ref)

    def folded(ref, at):
        low, high = ref[0, at, :], ref[1, at, :]
        low, high = low + pltpu.roll(low, 64, 1), high + pltpu.roll(high, 64, 1)
        return jnp.where(left, low, high)

    def chunk(i, _):
        at = pl.ds(pl.multiple_of(i * LANES, LANES), LANES)
        cos, sin = cos_ref[at, :], sin_ref[at, :]
        for b in range(3):
            u = qk_pre_ref[at, b * LANES : (b + 1) * LANES]
            g = folded(dk_ref, at) * 0.125 if b == 2 else dq_ref[b, at, :]
            w = g * cos - turn(g, first) * sin
            row = 1 if b == 2 else 0
            gain = head_ref[row : row + 1, :]
            r = lax.rsqrt(half_sums(u * u) * (1.0 / 64) + EPS)
            head_sum_ref[row : row + 1, :] += jnp.sum(w * u * r, 0, keepdims=True)
            w = w * gain
            back = r * w - u * (r * r * r) * (half_sums(w * u) * (1.0 / 64))
            low_ref[at, b * LANES : (b + 1) * LANES] = back.astype(BF)
        low_ref[at, 384:] = folded(dv_ref, at).astype(BF)
        return 0

    lax.fori_loop(0, low_ref.shape[0] // LANES, chunk, 0)
    gain_sum = jnp.zeros((1, normed_ref.shape[1]), F32)
    for j in range(4):
        at = slice(j * rows, (j + 1) * rows)
        grad = dot_nt(low_ref[at, :], wqkv_ref[...])
        parts[j][...] = grad.astype(BF)
        gain_sum = gain_sum + jnp.sum(grad * normed_ref[at, :].astype(F32), 0, keepdims=True)
    gain_sum_ref[...] = gain_sum / gains_ref[0:1, :]


def columns(at, width):
    return pl.ds(pl.multiple_of(at * width, LANES), width)


def spread_body(widths, me_ref, *refs):
    weights, outs = refs[: len(widths)], refs[-4:]
    rows = weights[0].shape[0]
    me = me_ref[0]
    for j, out in enumerate(outs):
        start = 0
        for weight, width in zip(weights, widths):
            out[:rows, start : start + width] = weight[:, columns(me ^ j, width)]
            start += width
    if len(refs) > len(widths) + 4:
        gains = refs[len(widths)][...].astype(F32)
        gains = jnp.concatenate([gains, jnp.zeros((6, rows), F32)], 0)
        gains = jnp.concatenate([gains] * (LANES // rows), 1)
        lane = lax.broadcasted_iota(jnp.int32, (8, LANES), 1)
        gains = jnp.where(lane // rows == me, gains, 0.0).astype(BF)
        for out in outs:
            out[rows:, :] = jnp.zeros((8, out.shape[1]), BF)
            out[rows:, :LANES] = gains


def join_body(rows, me_ref, *refs):
    pieces, out = refs[:4], refs[4]
    me = me_ref[0]
    for j, piece in enumerate(pieces):
        out[pl.ds(pl.multiple_of((me ^ j) * rows, rows), rows), :] = piece[:rows, :]
    if pieces[0].shape[0] > rows:
        below = [piece[rows:, :].astype(F32) for piece in pieces]
        out[4 * rows :, :] = (below[0] + below[1] + below[2] + below[3]).astype(BF)


def part_body(me_ref, one_ref, two_ref, three_ref, *refs):
    outs, total_ref = refs[:4], refs[4]
    total = one_ref[...].astype(F32) + two_ref[...].astype(F32) + three_ref[...].astype(F32)
    total_ref[...] = total
    rows = outs[0].shape[0]
    for j, out in enumerate(outs):
        at = pl.ds(pl.multiple_of((me_ref[0] ^ j) * rows, rows), rows)
        out[...] = total_ref[at, :].astype(BF)


def land_body(widths, me_ref, *refs):
    pieces, outs = refs[:4], refs[4:]
    me = me_ref[0]
    start = 0
    for out, width in zip(outs, widths):
        for j, piece in enumerate(pieces):
            out[:, columns(me ^ j, width)] = piece[:, start : start + width]
        start += width


def small_body(order_ref, one_ref, two_ref, head_ref, *refs):
    out_ref = refs[-1]
    out_ref[...] = jnp.zeros_like(out_ref)
    for i in range(one_ref.shape[1] // LANES):
        at = columns(order_ref[i], LANES)
        out_ref[0:1, at] = one_ref[:, i * LANES : (i + 1) * LANES]
        out_ref[1:2, at] = two_ref[:, i * LANES : (i + 1) * LANES]
    out_ref[2:4, :LANES] = head_ref[0:2, :]


def feed_body(rows, pieces, *refs):
    normed, packs, weights = refs[:4], refs[4:8], refs[8 : 8 + pieces]
    hidden_ref, gate_ref, up_ref, w_ref, down_ref, normed_ref, grad_ref = refs[8 + pieces :]
    ff = hidden_ref.shape[1]
    row = 0
    for weight in weights:
        w_ref[row : row + weight.shape[0], :] = weight[:, : 2 * ff]
        down_ref[row : row + weight.shape[0], :] = weight[:, 2 * ff :]
        row += weight.shape[0]
    for j in range(4):
        normed_ref[j * rows : (j + 1) * rows, :] = normed[j][...]
        grad_ref[j * rows : (j + 1) * rows, :] = packs[j][...]

    def one(i, _):
        at = pl.ds(pl.multiple_of(i * rows, rows), rows)
        x = normed_ref[at, :]
        gate, up = dot(x, w_ref[:, :ff]), dot(x, w_ref[:, ff:])
        grad = dot(grad_ref[at, :], down_ref[...])
        sig = 1.0 / (1.0 + jnp.exp(-gate))
        silu = gate * sig
        hidden_ref[at, :] = (silu * up).astype(BF)
        gate_ref[at, :] = (grad * up * (sig * (1.0 + gate * (1.0 - sig)))).astype(BF)
        up_ref[at, :] = (grad * silu).astype(BF)
        return 0

    lax.fori_loop(0, 4, one, 0)


def feed_back_body(rows, gate_ref, up_ref, w_ref, *refs):
    parts, part_ref = refs[:4], refs[4]
    ff = gate_ref.shape[1]

    def one(i, _):
        at = pl.ds(pl.multiple_of(i * rows, rows), rows)
        total = dot_nt(gate_ref[at, :], w_ref[:, :ff]) + dot_nt(up_ref[at, :], w_ref[:, ff:])
        part_ref[at, :] = total.astype(BF)
        return 0

    lax.fori_loop(0, 4, one, 0)
    for j in range(4):
        parts[j][...] = part_ref[j * rows : (j + 1) * rows, :]


def down_body(rows, hidden_ref, down_ref, *parts):
    for j in range(4):
        at = slice(j * rows, (j + 1) * rows)
        parts[j][...] = dot_nt(hidden_ref[at, :], down_ref[...]).astype(BF)


def attn_weights_body(normed_ref, grad_qkv_ref, grad_ref, out_ref, *chunks):
    cut = grad_qkv_ref.shape[1]
    one = dot_tn(normed_ref[...], grad_qkv_ref[...]).astype(BF)
    two = dot_tn(grad_ref[...], out_ref[...]).astype(BF)
    for i, chunk in enumerate(chunks):
        at = slice(i * LANES, (i + 1) * LANES)
        chunk[:, :cut] = one[at]
        chunk[:, cut:] = two[at]


def rms_scale(values, gain_row):
    return values * lax.rsqrt(jnp.mean(values * values, -1, keepdims=True) + EPS) * gain_row


def place_all(pieces, me, widths):
    outs, start = [], 0
    for width in widths:
        cut = [p[:, start : start + width] for p in pieces]
        outs.append(place(cut, [me ^ j for j in range(4)], 1))
        start += width
    return outs


def on_device(
    dp_size,
    tokens,
    doc_ids,
    w_query,
    key_weight,
    value_weight,
    w_output,
    w_gate,
    w_up,
    w_down,
    norm_gains,
    head_norm_gains,
    out_grad,
):
    local_len, model_dim = tokens.shape[1:]
    tokens, out_grad, doc_row = tokens[0], out_grad[0], doc_ids[0]
    head_dim = head_norm_gains.shape[1]
    q_cols, kv_cols = w_query.shape[1] // 4, key_weight.shape[1] // 4
    shard = norm_gains.shape[1]
    ff_cols = w_gate.shape[1] // 4
    me = lax.axis_index("ctx")
    places = [me ^ j for j in range(4)]
    full_len = 4 * local_len
    fast = ordered(dp_size)
    block_order = jnp.stack(dp_order(dp_size)) if fast else jnp.arange(model_dim // LANES)
    block_order = block_order.astype(jnp.int32)
    me_row = me.reshape(1).astype(jnp.int32)
    attn_widths = (q_cols, kv_cols, kv_cols, q_cols)
    ff_widths = (ff_cols, ff_cols, ff_cols)
    wide, ff_wide = sum(attn_widths), sum(ff_widths)
    attn_local = [w_query, key_weight, value_weight, w_output.T]
    ff_local = [w_gate, w_up, w_down.T]

    pack = pack_rows(block_order, tokens, doc_row)
    grad_pack = pack_rows(block_order, out_grad)
    if fast:
        sent = call(
            functools.partial(spread_body, attn_widths),
            [((shard + 8, wide), BF)] * 4,
            [me_row, *attn_local, norm_gains],
            scalars=1,
        )
        ff_sent = call(
            functools.partial(spread_body, ff_widths),
            [((shard, ff_wide), BF)] * 4,
            [me_row, *ff_local],
            scalars=1,
        )
        got, ff_sent = bar(exchange_ctx(sent), ff_sent)
        ff_got = exchange_ctx(ff_sent)
        (block,) = call(
            functools.partial(join_body, shard),
            [((4 * shard + 8, wide), BF)],
            [me_row, *got],
            scalars=1,
        )
        y0, z1, pack, ff_got = bar(across_y(block), along_z(block), pack, ff_got)
        core_pack, far_pack = flip(pack, "ctx", 4, 1), flip(pack, "ctx", 4, 2)
        y1, z2 = bar(across_y(z1), along_z(z1))
        (ff_block,) = call(
            functools.partial(join_body, shard),
            [((4 * shard, ff_wide), BF)],
            [me_row, *ff_got],
            scalars=1,
        )
        y2, z3, far_pack, grad_pack, ff_block = bar(
            across_y(z2), along_z(z2), far_pack, grad_pack, ff_block
        )
        far_core_pack = flip(far_pack, "ctx", 4, 1)
        y3, ff_block, far_core_pack = bar(across_y(z3), ff_block, far_core_pack)
        ff_z1, ff_y0 = along_z(ff_block), across_y(ff_block)
        blocks = [block, z1, z2, z3, y0, y1, y2, y3]
    else:

        def pieces_of(weights):
            sent = []
            for at in places:
                cut = [
                    lax.dynamic_slice_in_dim(w, at * (w.shape[1] // 4), w.shape[1] // 4, 1)
                    for w in weights
                ]
                sent.append(jnp.concatenate(cut, 1))
            return sent

        def whole(weights):
            block = place(exchange_ctx(pieces_of(weights)), places, 0)
            return lax.all_gather(block, "dp", axis=0, tiled=True)

        gains = lax.all_gather(norm_gains, ALL, axis=1, tiled=True).reshape(2, -1, LANES)
        gains = jnp.pad(gains.transpose(1, 0, 2), ((0, 0), (0, 6), (0, wide - LANES)))
        blocks = jnp.concatenate([whole(attn_local).reshape(-1, LANES, wide), gains], 1)
        blocks = [blocks[i] for i in range(blocks.shape[0])]
        ff_w = [whole(ff_local)]
        core_pack, far_pack = flip(pack, "ctx", 4, 1), flip(pack, "ctx", 4, 2)
        far_core_pack = flip(far_pack, "ctx", 4, 1)

    packs = [pack, core_pack, far_pack, far_core_pack]
    core_grad, far_grad = flip(grad_pack, "ctx", 4, 1), flip(grad_pack, "ctx", 4, 2)
    docs = jnp.concatenate([p[local_len, :local_len] for p in packs])
    index = jnp.concatenate(
        [at * local_len + jnp.arange(local_len, dtype=jnp.int32) for at in places]
    )
    starts = jnp.sum((docs[None, :] < docs[:, None]).astype(jnp.int32), -1)
    positions = (index - starts).astype(F32)
    half = head_dim // 2
    lane = jnp.arange(LANES)
    freqs = THETA ** (-(2.0 * (lane % half).astype(F32)) / head_dim)
    angles = positions[:, None] * freqs
    cosine = jnp.cos(angles)
    sine = jnp.sin(angles) * jnp.where(lane % head_dim < half, -1.0, 1.0)
    starts = starts.reshape(4, local_len)
    firsts = starts[:, 0]
    starts = jnp.concatenate([starts, starts], 1).reshape(4, 1, 2 * local_len)
    head_gains = jnp.concatenate([head_norm_gains, head_norm_gains], 1).astype(F32)

    part_shapes = [((local_len, model_dim), BF)] * 4
    normed_one, qk_pre, queries, keys, values, keys_t, values_t, w_qkv, wo_t, gains = call(
        functools.partial(prepare_body, local_len),
        [
            ((full_len, model_dim), BF),
            ((full_len, q_cols + kv_cols), F32),
            ((2, full_len, LANES), BF),
            ((2, full_len, LANES), BF),
            ((2, full_len, LANES), BF),
            ((LANES, full_len), BF),
            ((LANES, full_len), BF),
            ((model_dim, q_cols + 2 * kv_cols), BF),
            ((model_dim, q_cols), BF),
            ((8, model_dim), F32),
        ],
        [*packs, *blocks, cosine, sine, head_gains],
        [pltpu.VMEM((full_len, model_dim), BF)],
        limit=28,
        flops=HEAVY,
    )
    if fast:
        queries, keys, ff_z1, ff_y0, core_grad, far_grad = bar(
            queries, keys, ff_z1, ff_y0, core_grad, far_grad
        )
        ff_z2, ff_y1 = along_z(ff_z1), across_y(ff_z1)
    grad_packs = [grad_pack, core_grad, far_grad, flip(far_grad, "ctx", 4, 1)]
    *resid_parts, attn_out, attn_wide, lse = call(
        functools.partial(attend_body, local_len),
        part_shapes
        + [
            ((full_len, q_cols), BF),
            ((2, full_len, LANES), F32),
            ((8, 1, 2 * local_len), F32),
        ],
        [me_row, firsts, queries, keys, values_t, starts, wo_t],
        [pltpu.VMEM((1, 2 * local_len), F32), pltpu.VMEM((head_dim, 2 * local_len), F32)],
        scalars=2,
        limit=20,
    )
    own_tokens = pack[:local_len].astype(F32)
    own_grad = grad_pack.astype(F32)
    near_one, far_one = flip(resid_parts[1], "ctx", 4, 1), flip(resid_parts[3], "ctx", 4, 1)
    far_one = add_low(resid_parts[2], far_one)
    if fast:
        far_one, ff_z2, ff_y1 = bar(far_one, ff_z2, ff_y1)
        ff_z3, ff_y2 = along_z(ff_z2), across_y(ff_z2)
    far_one = flip(far_one, "ctx", 4, 2)
    resid = own_tokens + sum_parts((resid_parts[0], near_one, far_one))
    normed_own = rms_scale(resid, gains[1]).astype(BF)
    normed_core, normed_far = flip(normed_own, "ctx", 4, 1), flip(normed_own, "ctx", 4, 2)
    if fast:
        normed_far, ff_z3, ff_y2 = bar(normed_far, ff_z3, ff_y2)
        cut = ff_block.shape[0] // 2
        ff_w = [ff_block, ff_z1, ff_z2, ff_z3, ff_y0, ff_y1, ff_y2]
        ff_w += [across_y(ff_z3[:cut]), along_z(ff_y2[cut:])]
    normed_two = [normed_own, normed_core, normed_far, flip(normed_far, "ctx", 4, 1)]

    ff_shape = ((full_len, ff_cols), BF)
    hidden, grad_gate, grad_up, w_own, w_down_own, normed_all, grad_all = call(
        functools.partial(feed_body, local_len, len(ff_w)),
        [ff_shape] * 3
        + [((model_dim, 2 * ff_cols), BF), ((model_dim, ff_cols), BF)]
        + [((full_len, model_dim), BF)] * 2,
        [*normed_two, *grad_packs, *ff_w],
        limit=16,
        held=True,
    )

    def ff_chunks(at):
        cut = [dot_tn(normed_all[:, at], g).astype(BF) for g in (grad_gate, grad_up)]
        cut.append(dot_tn(grad_all[:, at], hidden).astype(BF))
        rows = cut[0].shape[0] // 4
        return [
            jnp.concatenate([c[r * rows : (r + 1) * rows] for c in cut], 1) for r in range(4)
        ]

    def pieces_of_sum(last):
        wide = last[0].shape[1]
        return call(
            part_body,
            [((shard, wide), BF)] * 4,
            [me_row, *last],
            [pltpu.VMEM((4 * shard, wide), F32)],
            scalars=1,
            limit=12,
        )

    def land(pieces, widths):
        return call(
            functools.partial(land_body, widths),
            [((shard, 4 * width), BF) for width in widths],
            [me_row, *pieces],
            scalars=1,
        )

    def plain_sums(chunks, widths):
        mine = lax.psum_scatter(jnp.concatenate(chunks, 0), "dp", scatter_dimension=0, tiled=True)
        pieces = [lax.dynamic_slice_in_dim(mine, at * shard, shard, 0) for at in places]
        return place_all(exchange_ctx(pieces), me, widths)

    def tick(*values):
        def body(*refs):
            refs[-1][...] = jnp.zeros((8, LANES), BF)

        return pl.pallas_call(
            body,
            out_shape=jax.ShapeDtypeStruct((8, LANES), BF),
            in_specs=[pl.BlockSpec(memory_space=pl.ANY)] * len(values),
            out_specs=VMEM,
            cost_estimate=pl.CostEstimate(flops=HEAVY, bytes_accessed=1000, transcendentals=0),
        )(*values)

    middle = model_dim // 2
    far = ff_chunks(slice(middle, None))
    if fast:
        cut = 4 * shard // 2
        first, early = across_y(far[1][:cut]), along_z(far[1][cut:])
        far[1], grad_gate, grad_up = bar(far[1], grad_gate, grad_up)
    *two_parts, = call(
        functools.partial(feed_back_body, local_len),
        part_shapes,
        [grad_gate, grad_up, w_own],
        [pltpu.VMEM((full_len, model_dim), BF)],
        limit=8,
        held=True,
    )
    near_two, far_two = flip(two_parts[1], "ctx", 4, 1), flip(two_parts[3], "ctx", 4, 1)
    if fast:
        near_two, far_two, hidden, normed_all, grad_all = bar(near_two, far_two, hidden, normed_all, grad_all)
    near = ff_chunks(slice(0, middle))
    far_two = add_low(two_parts[2], far_two)
    if fast:
        second = jnp.concatenate([far[2][:cut], add_low(far[2][cut:], early)], 0)
        total = jnp.concatenate([add_low(near[1][:cut], first), near[1][cut:]], 0)
        far_two, total, second = bar(far_two, total, second)
        total, second = along_z(total), across_y(second)
    far_two = flip(far_two, "ctx", 4, 2)
    grad_norm_two = sum_parts((two_parts[0], near_two, far_two))
    _, second_pull = jax.vjp(rms_scale, resid, gains[1])
    grad_resid_norm, grad_gain_two = second_pull(grad_norm_two)
    grad_resid = own_grad + grad_resid_norm
    (*down_parts,) = call(
        functools.partial(down_body, local_len), part_shapes, [hidden, w_down_own], limit=16
    )

    grad_low = grad_resid.astype(BF)
    grad_core, grad_far = flip(grad_low, "ctx", 4, 1), flip(grad_low, "ctx", 4, 2)
    if fast:
        grad_far, down_parts = bar(grad_far, down_parts)
    down_near, down_far = flip(down_parts[1], "ctx", 4, 1), flip(down_parts[3], "ctx", 4, 1)
    down_far = add_low(down_parts[2], down_far)
    grad_attn = [grad_low, grad_core, grad_far, flip(grad_far, "ctx", 4, 1)]
    if fast:
        total, third = bar(add_low(near[2], second, total), far[3])
        grad_attn, down_far, tick_two = bar(grad_attn, down_far, tick(total))
        total, third = along_z(total), across_y(third)
    down_far = flip(down_far, "ctx", 4, 2)
    *one_parts, grad_qkv, head_sums, gain_one, grad_attn_all = call(
        functools.partial(attend_back_body, local_len),
        part_shapes
        + [
            ((full_len, q_cols + 2 * kv_cols), BF),
            ((8, LANES), F32),
            ((1, model_dim), F32),
            ((full_len, model_dim), BF),
        ],
        [
            me_row,
            firsts,
            *grad_attn,
            queries,
            keys,
            values,
            keys_t,
            starts,
            attn_wide,
            lse,
            qk_pre,
            cosine,
            sine,
            head_gains,
            w_qkv,
            wo_t,
            normed_one,
            gains,
        ],
        [
            pltpu.VMEM((2, full_len, LANES), BF),
            pltpu.VMEM((2, full_len, LANES), F32),
            pltpu.VMEM((2, full_len, LANES), F32),
            pltpu.VMEM((2, full_len, LANES), F32),
            pltpu.VMEM((head_dim, 2 * local_len), F32),
        ],
        scalars=2,
        limit=24,
        held=True,
    )
    if fast:
        fourth, grad_qkv = bar(far[0], grad_qkv)
        fourth = across_y(fourth)
        total, grad_qkv = bar(add_low(near[3], third, total), grad_qkv)
        last = (near[0], fourth, along_z(total))
    layer_out = sum_out(block_order, resid, (down_parts[0], down_near, down_far))
    attn_chunks = call(
        attn_weights_body,
        [((LANES, wide), BF)] * 8,
        [normed_one, grad_qkv, grad_attn_all, attn_out],
        limit=20,
    )
    ticks = [tick_two] if fast else []
    (small,) = call(
        small_body,
        [((4, model_dim), F32)],
        [block_order, gain_one, grad_gain_two.reshape(1, -1), head_sums, *ticks],
        scalars=1,
    )
    grad_one = scatter_ctx(one_parts)
    if fast:
        near, far = attn_chunks[:4], attn_chunks[4:]
        total, last = bar(add_low(near[1], across_y(far[1])), last)
        ff_pieces = pieces_of_sum(last)
        total, small_core = bar(
            add_low(near[2], across_y(far[2]), along_z(total)), flip(small, "ctx", 4, 1)
        )
        small = small + small_core
        small = small + flip(small, "ctx", 4, 2)
        total, small_y = bar(
            add_low(near[3], across_y(far[3]), along_z(total)), flip(small, "dp", dp_size, 1)
        )
        small = small + small_y
        attn_last = (near[0], across_y(far[0]), along_z(total))
        attn_last, small_z, ff_got = bar(
            attn_last, flip(small, "dp", dp_size, 2), exchange_ctx(ff_pieces)
        )
        small = small + small_z
        small = small + flip(small, "dp", dp_size, 4)
        attn_pieces = exchange_ctx(pieces_of_sum(attn_last))
        grad_g_out, grad_u_out, grad_d_out = land(ff_got, ff_widths)
        grad_q_out, grad_k_out, grad_v_out, grad_o_out = land(attn_pieces, attn_widths)
    else:
        grad_g_out, grad_u_out, grad_d_out = plain_sums(near + far, ff_widths)
        grad_q_out, grad_k_out, grad_v_out, grad_o_out = plain_sums(attn_chunks, attn_widths)
        small = sum_all(small, dp_size)
    _, first_pull = jax.vjp(lambda u: rms_scale(u, gains[0]), own_tokens)
    input_grad = sum_out(block_order, grad_resid + first_pull(sum_parts(grad_one))[0], ())
    norm_own = lax.dynamic_slice_in_dim(small[:2], lax.axis_index(ALL) * shard, shard, 1)
    head_sum = small[2:, :head_dim] + small[2:, head_dim : 2 * head_dim]
    return (
        layer_out[None],
        input_grad[None],
        grad_q_out,
        grad_k_out,
        grad_v_out,
        grad_o_out.T,
        grad_g_out,
        grad_u_out,
        grad_d_out.T,
        norm_own.astype(BF),
        head_sum.astype(BF),
    )


def solution(mesh):
    def step(*arrays):
        return on_device(mesh.shape["dp"], *arrays)

    in_specs = (
        P("dp", "ctx", None),
        P("dp", "ctx"),
        P(("dp", "ctx"), None),
        P(("dp", "ctx"), None),
        P(("dp", "ctx"), None),
        P(None, ("dp", "ctx")),
        P(("dp", "ctx"), None),
        P(("dp", "ctx"), None),
        P(None, ("dp", "ctx")),
        P(None, ("dp", "ctx")),
        P(),
        P("dp", "ctx", None),
    )
    out_specs = (
        P("dp", "ctx", None),
        P("dp", "ctx", None),
        P(("dp", "ctx"), None),
        P(("dp", "ctx"), None),
        P(("dp", "ctx"), None),
        P(None, ("dp", "ctx")),
        P(("dp", "ctx"), None),
        P(("dp", "ctx"), None),
        P(None, ("dp", "ctx")),
        P(None, ("dp", "ctx")),
        P(),
    )
    return jax.shard_map(step, mesh=mesh, in_specs=in_specs, out_specs=out_specs, check_vma=False)
```

```python
import functools

import jax
import jax.numpy as jnp
from jax import lax
from jax.experimental import pallas as pl
from jax.experimental.pallas import tpu as pltpu
from jax.sharding import PartitionSpec as P

EPS = 1e-05
THETA = 1000000.0
BF = jnp.bfloat16
F32 = jnp.float32
ALL = ("dp", "ctx")


def add_low(*terms):
    total = terms[0].astype(F32)
    for term in terms[1:]:
        total = total + term.astype(F32)
    return total.astype(BF)


def flip(value, axis, size, bits):
    return lax.ppermute(value, axis, [(i, i ^ bits) for i in range(size)])


def gather_ctx(own):
    core = flip(own, "ctx", 4, 1)
    across = flip(own, "ctx", 4, 2)
    return [own, core, across, flip(across, "ctx", 4, 1)]


def scatter_ctx(parts):
    far = flip(parts[3], "ctx", 4, 1)
    near = flip(parts[1], "ctx", 4, 1)
    return parts[0], near, flip(add_low(parts[2], far), "ctx", 4, 2)


def sum_parts(parts):
    return parts[0].astype(F32) + parts[1].astype(F32) + parts[2].astype(F32)


def exchange_ctx(parts):
    return [parts[0]] + [flip(parts[j], "ctx", 4, j) for j in range(1, 4)]


def place(parts, where, axis):
    size = parts[0].shape[axis]
    shape = list(parts[0].shape)
    shape[axis] = size * len(parts)
    out = jnp.zeros(shape, parts[0].dtype)
    for part, at in zip(parts, where):
        out = lax.dynamic_update_slice_in_dim(out, part, at * size, axis)
    return out


def bar(*trees):
    return lax.optimization_barrier(trees)


def ordered(dp_size):
    return dp_size == 8


def dp_order(dp_size):
    me = lax.axis_index("dp")
    return [((me - 2 * (i % 4)) % dp_size) ^ (i // 4) for i in range(dp_size)]


def across_y(value):
    return flip(value, "dp", 8, 1)


def along_z(value):
    return lax.ppermute(value, "dp", [(i, (i + 2) % 8) for i in range(8)])


def sum_all(value, dp_size):
    for bits in (1, 2):
        value = value + flip(value, "ctx", 4, bits)
    bits = 1
    while bits < dp_size:
        value = value + flip(value, "dp", dp_size, bits)
        bits *= 2
    return value


def dot(a, b):
    return lax.dot_general(a, b, (((1,), (0,)), ((), ())), preferred_element_type=F32)


def dot_nt(a, b):
    return lax.dot_general(a, b, (((1,), (1,)), ((), ())), preferred_element_type=F32)


def dot_tn(a, b):
    return lax.dot_general(a, b, (((0,), (0,)), ((), ())), preferred_element_type=F32)


VMEM = pl.BlockSpec(memory_space=pltpu.VMEM)
SMEM = pl.BlockSpec(memory_space=pltpu.SMEM)
LANES = 128
HIGH = lax.Precision.HIGHEST


HEAVY = 10**11


def call(body, outs, ins, scratch=(), scalars=0, limit=4, flops=1000000, held=False):
    def spec(shape):
        if held:
            return VMEM
        zeros = (0,) * len(shape)
        return pl.BlockSpec(tuple(shape), lambda i: zeros, pipeline_mode=pl.Buffered(1))

    return pl.pallas_call(
        body,
        out_shape=[jax.ShapeDtypeStruct(shape, kind) for shape, kind in outs],
        grid=() if held else (1,),
        in_specs=[SMEM] * scalars + [spec(x.shape) for x in ins[scalars:]],
        out_specs=[spec(shape) for shape, _ in outs],
        scratch_shapes=list(scratch),
        compiler_params=pltpu.CompilerParams(vmem_limit_bytes=limit << 20),
        cost_estimate=pl.CostEstimate(flops=flops, bytes_accessed=1000, transcendentals=0),
    )(*ins)


def pack_body(order_ref, tokens_ref, docs_ref, out_ref):
    rows = tokens_ref.shape[0]

    def one(i, _):
        out_ref[:rows, columns(i, LANES)] = tokens_ref[:, columns(order_ref[i], LANES)]
        return 0

    lax.fori_loop(0, tokens_ref.shape[1] // LANES, one, 0)
    if docs_ref is not None:
        below = jnp.broadcast_to(docs_ref[...].astype(F32), (16, rows)).astype(BF)
        out_ref[rows:, :rows] = below
        out_ref[rows:, rows:] = jnp.zeros((16, out_ref.shape[1] - rows), BF)


def pack_rows(order, rows, doc_row=None):
    if doc_row is None:
        body = lambda order_ref, rows_ref, out_ref: pack_body(order_ref, rows_ref, None, out_ref)
        return call(body, [(rows.shape, BF)], [order, rows], scalars=1)[0]
    shape = (rows.shape[0] + 16, rows.shape[1])
    return call(pack_body, [(shape, BF)], [order, rows, doc_row.reshape(1, -1)], scalars=1)[0]


def sum_body(order_ref, base_ref, *refs):
    parts, out_ref = refs[:-1], refs[-1]

    def one(i, _):
        at = columns(i, LANES)
        total = base_ref[:, at]
        if parts:
            part = parts[0][:, at].astype(F32)
            for ref in parts[1:]:
                part = part + ref[:, at].astype(F32)
            total = total + part
        out_ref[:, columns(order_ref[i], LANES)] = total.astype(BF)
        return 0

    lax.fori_loop(0, base_ref.shape[1] // LANES, one, 0)


def sum_out(order, base, parts):
    return call(sum_body, [(base.shape, BF)], [order, base, *parts], scalars=1)[0]


def by_blocks(count, rows, body):
    def one(i, _):
        body(pl.ds(pl.multiple_of(i * rows, rows), rows))
        return 0

    lax.fori_loop(0, count, one, 0)


def move(target, to, source, start, rows):
    step = 32

    def one(i, _):
        goal = pl.ds(pl.multiple_of(to + i * step, step), step)
        target[goal, :] = source[pl.ds(pl.multiple_of(start + i * step, step), step), :]
        return 0

    lax.fori_loop(0, rows // step, one, 0)


def hand_out(ref, parts):
    rows = parts[0].shape[0]
    for j, part in enumerate(parts):
        move(part, 0, ref, j * rows, rows)


def lane_masks(rows):
    lane = lax.broadcasted_iota(jnp.int32, (rows, LANES), 1)
    return lane < 64, lax.rem(lane, 64) < 32


def half_sums(squares):
    row = lax.broadcasted_iota(jnp.int32, (LANES, LANES), 0) // 64
    col = lax.broadcasted_iota(jnp.int32, (LANES, LANES), 1) // 64
    return jnp.dot(
        squares, (row == col).astype(F32), preferred_element_type=F32, precision=HIGH
    )


def turn(value, first):
    return jnp.where(first, pltpu.roll(value, 96, 1), pltpu.roll(value, 32, 1))


def doubled(value, left):
    other = pltpu.roll(value, 64, 1)
    return jnp.where(left, value, other), jnp.where(left, other, value)


def prepare_body(rows, *refs):
    packs, blocks = refs[:4], refs[4:12]
    cos_ref, sin_ref, head_ref = refs[12:15]
    normed_ref, qk_pre_ref, q_ref, kd_ref, vd_ref, kt_ref, vt_ref = refs[15:22]
    wqkv_ref, wo_ref, gains_ref, all_ref = refs[22:26]
    for i, block in enumerate(blocks):
        at = i * LANES
        wqkv_ref[at : at + LANES, :] = block[:LANES, :512]
        wo_ref[at : at + LANES, :] = block[:LANES, 512:]
        gains_ref[:, at : at + LANES] = block[LANES : LANES + 8, :LANES].astype(F32)
    for j, pack in enumerate(packs):
        move(all_ref, j * rows, pack, 0, rows)
    left, first = lane_masks(LANES)
    gain = gains_ref[0:1, :]
    q_gain, k_gain = head_ref[0:1, :], head_ref[1:2, :]

    def chunk(i, _):
        at = pl.ds(pl.multiple_of(i * LANES, LANES), LANES)
        x = all_ref[at, :].astype(F32)
        scale = lax.rsqrt(jnp.mean(x * x, -1, keepdims=True) + EPS)
        normed = (x * scale * gain).astype(BF)
        normed_ref[at, :] = normed
        pre = jnp.dot(normed, wqkv_ref[...], preferred_element_type=F32)
        qk_pre_ref[at, :] = pre[:, :384]
        cos, sin = cos_ref[at, :], sin_ref[at, :]
        turned = []
        for b in range(3):
            u = pre[:, b * LANES : (b + 1) * LANES]
            u = u * lax.rsqrt(half_sums(u * u) * (1.0 / 64) + EPS) * (k_gain if b == 2 else q_gain)
            turned.append(u * cos + turn(u, first) * sin)
        q_ref[0, at, :] = turned[0].astype(BF)
        q_ref[1, at, :] = turned[1].astype(BF)
        key, value = turned[2], pre[:, 384:]
        for both, flat, one in ((kd_ref, kt_ref, key), (vd_ref, vt_ref, value)):
            low, high = doubled(one, left)
            both[0, at, :] = low.astype(BF)
            both[1, at, :] = high.astype(BF)
            flat[:, at] = one.T.astype(BF)
        return 0

    lax.fori_loop(0, all_ref.shape[0] // LANES, chunk, 0)


def two_heads(block, left):
    zero = jnp.zeros_like(block)
    return jnp.concatenate([jnp.where(left, block, zero), jnp.where(left, zero, block)], 0)


def seen(start_row, first_key, rows, first_query):
    shape = (rows, 2 * rows)
    key = lax.broadcasted_iota(jnp.int32, shape, 0)
    mask = key + first_key >= start_row
    if first_query is not None:
        lane = lax.broadcasted_iota(jnp.int32, shape, 1)
        mask = mask & (key <= jnp.where(lane < rows, lane, lane - rows))
    return mask


LOG2E = 1.4426950408889634
SCORE = LOG2E / 8.0


def attend_body(rows, me_ref, first_ref, q_ref, kd_ref, vt_ref, start_ref, wo_ref, *refs):
    parts = refs[:4]
    out_ref, wide_ref, lse_ref, sum_ref, acc_ref, part_ref = refs[4:10]
    me = me_ref[0]
    left = lax.broadcasted_iota(jnp.int32, (rows, LANES), 1) < 64

    def one(step, _):
        kv, a = step // 4, lax.rem(step, 4)
        at_q = pl.ds(pl.multiple_of((a ^ me) * rows, rows), rows)
        q2 = two_heads(q_ref[kv, at_q, :], left)
        start_row = start_ref[a ^ me]
        sum_ref[...] = jnp.zeros_like(sum_ref)
        acc_ref[...] = jnp.zeros_like(acc_ref)
        for d in range(3):

            @pl.when((a >= d) & (first_ref[a ^ me] < (a - d + 1) * rows))
            def _():
                at_k = pl.ds(pl.multiple_of(((a - d) ^ me) * rows, rows), rows)
                scores = dot_nt(kd_ref[kv, at_k, :], q2)
                mask = seen(start_row, (a - d) * rows, rows, a if d == 0 else None)
                p = jnp.where(mask, jnp.exp2(scores * SCORE), 0.0)
                sum_ref[...] += jnp.sum(p, 0, keepdims=True)
                half = pl.ds(pl.multiple_of(kv * 64, 64), 64)
                acc_ref[...] += dot(vt_ref[half, at_k], p.astype(BF))

        total = sum_ref[...]
        lse_ref[kv * 4 + (a ^ me)] = jnp.log2(total)
        mixed = acc_ref[...] / total
        mixed = jnp.concatenate([mixed[:, :rows], mixed[:, rows:]], 0).T
        wide_ref[kv, at_q, :] = mixed
        out_ref[at_q, columns(kv, LANES)] = mixed.astype(BF)
        return 0

    lax.fori_loop(0, 8, one, 0)

    def project(at):
        part_ref[at, :] = dot_nt(out_ref[at, :], wo_ref[...]).astype(BF)

    by_blocks(4, rows, project)
    hand_out(part_ref, parts)


def attend_back_body(rows, *refs):
    me_ref, first_ref = refs[:2]
    refs = refs[1:]
    g0, g1, g2, g3, q_ref, kd_ref, vd_ref, kt_ref, start_ref, wide_ref, lse_ref = refs[1:12]
    qk_pre_ref, cos_ref, sin_ref, head_ref, wqkv_ref, wo_ref, normed_ref, gains_ref = refs[12:20]
    parts, low_ref, head_sum_ref, gain_sum_ref, grad_ref = refs[20:24], *refs[24:28]
    mixed_ref, dq_ref, dk_ref, dv_ref, acc_ref = refs[28:33]
    me = me_ref[0]
    left = lax.broadcasted_iota(jnp.int32, (rows, LANES), 1) < 64
    for j, g in enumerate((g0, g1, g2, g3)):
        move(grad_ref, j * rows, g, 0, rows)

    def mix(at):
        grad = dot(grad_ref[at, :], wo_ref[...]).astype(BF)
        mixed_ref[0, at, :] = grad[:, :LANES]
        mixed_ref[1, at, :] = grad[:, LANES:]

    by_blocks(4, rows, mix)
    dk_ref[...] = jnp.zeros_like(dk_ref)
    dv_ref[...] = jnp.zeros_like(dv_ref)
    pick = (
        lax.broadcasted_iota(jnp.int32, (8, LANES), 1) // 64
        == lax.broadcasted_iota(jnp.int32, (8, LANES), 0)
    ).astype(F32)

    def one(step, _):
        kv, a = step // 4, lax.rem(step, 4)
        at_q = pl.ds(pl.multiple_of((a ^ me) * rows, rows), rows)
        q2 = two_heads(q_ref[kv, at_q, :], left)
        grad = mixed_ref[kv, at_q, :]
        g2 = two_heads(grad, left)
        inner = lax.dot_general(
            pick,
            grad.astype(F32) * wide_ref[kv, at_q, :],
            (((1,), (1,)), ((), ())),
            preferred_element_type=F32,
            precision=HIGH,
        )
        inner = jnp.concatenate([inner[0:1], inner[1:2]], 1)
        lse = lse_ref[kv * 4 + (a ^ me)]
        start_row = start_ref[a ^ me]
        acc_ref[...] = jnp.zeros_like(acc_ref)
        for d in range(3):

            @pl.when((a >= d) & (first_ref[a ^ me] < (a - d + 1) * rows))
            def _():
                at_k = pl.ds(pl.multiple_of(((a - d) ^ me) * rows, rows), rows)
                scores = dot_nt(kd_ref[kv, at_k, :], q2)
                mask = seen(start_row, (a - d) * rows, rows, a if d == 0 else None)
                p = jnp.where(mask, jnp.exp2(scores * SCORE - lse), 0.0)
                gp = dot_nt(vd_ref[kv, at_k, :], g2)
                gs = (p * (gp - inner)).astype(BF)
                dv_ref[kv, at_k, :] += dot(p.astype(BF), g2)
                dk_ref[kv, at_k, :] += dot(gs, q2)
                half = pl.ds(pl.multiple_of(kv * 64, 64), 64)
                acc_ref[...] += dot(kt_ref[half, at_k], gs)

        both = acc_ref[...] * 0.125
        dq_ref[kv, at_q, :] = jnp.concatenate([both[:, :rows], both[:, rows:]], 0).T
        return 0

    lax.fori_loop(0, 8, one, 0)
    left, first = lane_masks(LANES)
    head_sum_ref[...] = jnp.zeros_like(head_sum_ref)

    def folded(ref, at):
        low, high = ref[0, at, :], ref[1, at, :]
        low, high = low + pltpu.roll(low, 64, 1), high + pltpu.roll(high, 64, 1)
        return jnp.where(left, low, high)

    def chunk(i, _):
        at = pl.ds(pl.multiple_of(i * LANES, LANES), LANES)
        cos, sin = cos_ref[at, :], sin_ref[at, :]
        for b in range(3):
            u = qk_pre_ref[at, b * LANES : (b + 1) * LANES]
            g = folded(dk_ref, at) * 0.125 if b == 2 else dq_ref[b, at, :]
            w = g * cos - turn(g, first) * sin
            row = 1 if b == 2 else 0
            gain = head_ref[row : row + 1, :]
            r = lax.rsqrt(half_sums(u * u) * (1.0 / 64) + EPS)
            head_sum_ref[row : row + 1, :] += jnp.sum(w * u * r, 0, keepdims=True)
            w = w * gain
            back = r * w - u * (r * r * r) * (half_sums(w * u) * (1.0 / 64))
            low_ref[at, b * LANES : (b + 1) * LANES] = back.astype(BF)
        low_ref[at, 384:] = folded(dv_ref, at).astype(BF)
        return 0

    lax.fori_loop(0, low_ref.shape[0] // LANES, chunk, 0)
    gain_sum = jnp.zeros((1, normed_ref.shape[1]), F32)
    for j in range(4):
        at = slice(j * rows, (j + 1) * rows)
        grad = dot_nt(low_ref[at, :], wqkv_ref[...])
        parts[j][...] = grad.astype(BF)
        gain_sum = gain_sum + jnp.sum(grad * normed_ref[at, :].astype(F32), 0, keepdims=True)
    gain_sum_ref[...] = gain_sum / gains_ref[0:1, :]


def columns(at, width):
    return pl.ds(pl.multiple_of(at * width, LANES), width)


def spread_body(widths, me_ref, *refs):
    weights, outs = refs[: len(widths)], refs[-4:]
    rows = weights[0].shape[0]
    me = me_ref[0]
    for j, out in enumerate(outs):
        start = 0
        for weight, width in zip(weights, widths):
            out[:rows, start : start + width] = weight[:, columns(me ^ j, width)]
            start += width
    if len(refs) > len(widths) + 4:
        gains = refs[len(widths)][...].astype(F32)
        gains = jnp.concatenate([gains, jnp.zeros((6, rows), F32)], 0)
        gains = jnp.concatenate([gains] * (LANES // rows), 1)
        lane = lax.broadcasted_iota(jnp.int32, (8, LANES), 1)
        gains = jnp.where(lane // rows == me, gains, 0.0).astype(BF)
        for out in outs:
            out[rows:, :] = jnp.zeros((8, out.shape[1]), BF)
            out[rows:, :LANES] = gains


def join_body(rows, me_ref, *refs):
    pieces, out = refs[:4], refs[4]
    me = me_ref[0]
    for j, piece in enumerate(pieces):
        out[pl.ds(pl.multiple_of((me ^ j) * rows, rows), rows), :] = piece[:rows, :]
    if pieces[0].shape[0] > rows:
        below = [piece[rows:, :].astype(F32) for piece in pieces]
        out[4 * rows :, :] = (below[0] + below[1] + below[2] + below[3]).astype(BF)


def part_body(me_ref, one_ref, two_ref, three_ref, *refs):
    outs, total_ref = refs[:4], refs[4]
    total = one_ref[...].astype(F32) + two_ref[...].astype(F32) + three_ref[...].astype(F32)
    total_ref[...] = total
    rows = outs[0].shape[0]
    for j, out in enumerate(outs):
        at = pl.ds(pl.multiple_of((me_ref[0] ^ j) * rows, rows), rows)
        out[...] = total_ref[at, :].astype(BF)


def land_body(widths, me_ref, *refs):
    pieces, outs = refs[:4], refs[4:]
    me = me_ref[0]
    start = 0
    for out, width in zip(outs, widths):
        for j, piece in enumerate(pieces):
            out[:, columns(me ^ j, width)] = piece[:, start : start + width]
        start += width


def small_body(order_ref, one_ref, two_ref, head_ref, *refs):
    out_ref = refs[-1]
    out_ref[...] = jnp.zeros_like(out_ref)
    for i in range(one_ref.shape[1] // LANES):
        at = columns(order_ref[i], LANES)
        out_ref[0:1, at] = one_ref[:, i * LANES : (i + 1) * LANES]
        out_ref[1:2, at] = two_ref[:, i * LANES : (i + 1) * LANES]
    out_ref[2:4, :LANES] = head_ref[0:2, :]


def feed_body(rows, pieces, *refs):
    normed, packs, weights = refs[:4], refs[4:8], refs[8 : 8 + pieces]
    hidden_ref, gate_ref, up_ref, w_ref, down_ref, normed_ref, grad_ref = refs[8 + pieces :]
    ff = hidden_ref.shape[1]
    row = 0
    for weight in weights:
        move(w_ref, row, weight.at[:, : 2 * ff], 0, weight.shape[0])
        move(down_ref, row, weight.at[:, 2 * ff :], 0, weight.shape[0])
        row += weight.shape[0]
    for j in range(4):
        move(normed_ref, j * rows, normed[j], 0, rows)
        move(grad_ref, j * rows, packs[j], 0, rows)

    def one(i, _):
        at = pl.ds(pl.multiple_of(i * rows, rows), rows)
        x = normed_ref[at, :]
        gate, up = dot(x, w_ref[:, :ff]), dot(x, w_ref[:, ff:])
        grad = dot(grad_ref[at, :], down_ref[...])
        sig = 1.0 / (1.0 + jnp.exp(-gate))
        silu = gate * sig
        hidden_ref[at, :] = (silu * up).astype(BF)
        gate_ref[at, :] = (grad * up * (sig * (1.0 + gate * (1.0 - sig)))).astype(BF)
        up_ref[at, :] = (grad * silu).astype(BF)
        return 0

    lax.fori_loop(0, 4, one, 0)


def feed_back_body(rows, gate_ref, up_ref, w_ref, *refs):
    parts, part_ref = refs[:4], refs[4]
    ff = gate_ref.shape[1]

    def one(i, _):
        at = pl.ds(pl.multiple_of(i * rows, rows), rows)
        total = dot_nt(gate_ref[at, :], w_ref[:, :ff]) + dot_nt(up_ref[at, :], w_ref[:, ff:])
        part_ref[at, :] = total.astype(BF)
        return 0

    lax.fori_loop(0, 4, one, 0)
    hand_out(part_ref, parts)


def down_body(rows, hidden_ref, down_ref, *refs):
    parts, part_ref = refs[:4], refs[4]

    def one(at):
        part_ref[at, :] = dot_nt(hidden_ref[at, :], down_ref[...]).astype(BF)

    by_blocks(4, rows, one)
    hand_out(part_ref, parts)


def attn_weights_body(normed_ref, grad_qkv_ref, grad_ref, out_ref, *chunks):
    cut = grad_qkv_ref.shape[1]
    chunks, whole_ref = chunks[:-1], chunks[-1]
    width = 2 * LANES

    def one(i, _):
        at = columns(i, width)
        whole_ref[at, :cut] = dot_tn(normed_ref[:, at], grad_qkv_ref[...]).astype(BF)
        whole_ref[at, cut:] = dot_tn(grad_ref[:, at], out_ref[...]).astype(BF)
        return 0

    lax.fori_loop(0, whole_ref.shape[0] // width, one, 0)
    hand_out(whole_ref, chunks)


def rms_scale(values, gain_row):
    return values * lax.rsqrt(jnp.mean(values * values, -1, keepdims=True) + EPS) * gain_row


def place_all(pieces, me, widths):
    outs, start = [], 0
    for width in widths:
        cut = [p[:, start : start + width] for p in pieces]
        outs.append(place(cut, [me ^ j for j in range(4)], 1))
        start += width
    return outs


def on_device(
    dp_size,
    tokens,
    doc_ids,
    w_query,
    key_weight,
    value_weight,
    w_output,
    w_gate,
    w_up,
    w_down,
    norm_gains,
    head_norm_gains,
    out_grad,
):
    local_len, model_dim = tokens.shape[1:]
    tokens, out_grad, doc_row = tokens[0], out_grad[0], doc_ids[0]
    head_dim = head_norm_gains.shape[1]
    q_cols, kv_cols = w_query.shape[1] // 4, key_weight.shape[1] // 4
    shard = norm_gains.shape[1]
    ff_cols = w_gate.shape[1] // 4
    me = lax.axis_index("ctx")
    places = [me ^ j for j in range(4)]
    full_len = 4 * local_len
    fast = ordered(dp_size)
    block_order = jnp.stack(dp_order(dp_size)) if fast else jnp.arange(model_dim // LANES)
    block_order = block_order.astype(jnp.int32)
    me_row = me.reshape(1).astype(jnp.int32)
    attn_widths = (q_cols, kv_cols, kv_cols, q_cols)
    ff_widths = (ff_cols, ff_cols, ff_cols)
    wide, ff_wide = sum(attn_widths), sum(ff_widths)
    attn_local = [w_query, key_weight, value_weight, w_output.T]
    ff_local = [w_gate, w_up, w_down.T]

    pack = pack_rows(block_order, tokens, doc_row)
    grad_pack = pack_rows(block_order, out_grad)
    if fast:
        sent = call(
            functools.partial(spread_body, attn_widths),
            [((shard + 8, wide), BF)] * 4,
            [me_row, *attn_local, norm_gains],
            scalars=1,
        )
        ff_sent = call(
            functools.partial(spread_body, ff_widths),
            [((shard, ff_wide), BF)] * 4,
            [me_row, *ff_local],
            scalars=1,
        )
        got, ff_sent = bar(exchange_ctx(sent), ff_sent)
        ff_got = exchange_ctx(ff_sent)
        (block,) = call(
            functools.partial(join_body, shard),
            [((4 * shard + 8, wide), BF)],
            [me_row, *got],
            scalars=1,
        )
        y0, z1, pack, ff_got = bar(across_y(block), along_z(block), pack, ff_got)
        core_pack, far_pack = flip(pack, "ctx", 4, 1), flip(pack, "ctx", 4, 2)
        y1, z2 = bar(across_y(z1), along_z(z1))
        (ff_block,) = call(
            functools.partial(join_body, shard),
            [((4 * shard, ff_wide), BF)],
            [me_row, *ff_got],
            scalars=1,
        )
        y2, z3, far_pack, grad_pack, ff_block = bar(
            across_y(z2), along_z(z2), far_pack, grad_pack, ff_block
        )
        far_core_pack = flip(far_pack, "ctx", 4, 1)
        y3, ff_block, far_core_pack = bar(across_y(z3), ff_block, far_core_pack)
        ff_z1, ff_y0 = along_z(ff_block), across_y(ff_block)
        blocks = [block, z1, z2, z3, y0, y1, y2, y3]
    else:

        def pieces_of(weights):
            sent = []
            for at in places:
                cut = [
                    lax.dynamic_slice_in_dim(w, at * (w.shape[1] // 4), w.shape[1] // 4, 1)
                    for w in weights
                ]
                sent.append(jnp.concatenate(cut, 1))
            return sent

        def whole(weights):
            block = place(exchange_ctx(pieces_of(weights)), places, 0)
            return lax.all_gather(block, "dp", axis=0, tiled=True)

        gains = lax.all_gather(norm_gains, ALL, axis=1, tiled=True).reshape(2, -1, LANES)
        gains = jnp.pad(gains.transpose(1, 0, 2), ((0, 0), (0, 6), (0, wide - LANES)))
        blocks = jnp.concatenate([whole(attn_local).reshape(-1, LANES, wide), gains], 1)
        blocks = [blocks[i] for i in range(blocks.shape[0])]
        ff_w = [whole(ff_local)]
        core_pack, far_pack = flip(pack, "ctx", 4, 1), flip(pack, "ctx", 4, 2)
        far_core_pack = flip(far_pack, "ctx", 4, 1)

    packs = [pack, core_pack, far_pack, far_core_pack]
    core_grad, far_grad = flip(grad_pack, "ctx", 4, 1), flip(grad_pack, "ctx", 4, 2)
    docs = jnp.concatenate([p[local_len, :local_len] for p in packs])
    index = jnp.concatenate(
        [at * local_len + jnp.arange(local_len, dtype=jnp.int32) for at in places]
    )
    starts = jnp.sum((docs[None, :] < docs[:, None]).astype(jnp.int32), -1)
    positions = (index - starts).astype(F32)
    half = head_dim // 2
    lane = jnp.arange(LANES)
    freqs = THETA ** (-(2.0 * (lane % half).astype(F32)) / head_dim)
    angles = positions[:, None] * freqs
    cosine = jnp.cos(angles)
    sine = jnp.sin(angles) * jnp.where(lane % head_dim < half, -1.0, 1.0)
    starts = starts.reshape(4, local_len)
    firsts = starts[:, 0]
    starts = jnp.concatenate([starts, starts], 1).reshape(4, 1, 2 * local_len)
    head_gains = jnp.concatenate([head_norm_gains, head_norm_gains], 1).astype(F32)

    part_shapes = [((local_len, model_dim), BF)] * 4
    normed_one, qk_pre, queries, keys, values, keys_t, values_t, w_qkv, wo_t, gains = call(
        functools.partial(prepare_body, local_len),
        [
            ((full_len, model_dim), BF),
            ((full_len, q_cols + kv_cols), F32),
            ((2, full_len, LANES), BF),
            ((2, full_len, LANES), BF),
            ((2, full_len, LANES), BF),
            ((LANES, full_len), BF),
            ((LANES, full_len), BF),
            ((model_dim, q_cols + 2 * kv_cols), BF),
            ((model_dim, q_cols), BF),
            ((8, model_dim), F32),
        ],
        [*packs, *blocks, cosine, sine, head_gains],
        [pltpu.VMEM((full_len, model_dim), BF)],
        limit=28,
        flops=HEAVY,
    )
    if fast:
        queries, keys, ff_z1, ff_y0, core_grad, far_grad = bar(
            queries, keys, ff_z1, ff_y0, core_grad, far_grad
        )
        ff_z2, ff_y1 = along_z(ff_z1), across_y(ff_z1)
    grad_packs = [grad_pack, core_grad, far_grad, flip(far_grad, "ctx", 4, 1)]
    *resid_parts, attn_out, attn_wide, lse = call(
        functools.partial(attend_body, local_len),
        part_shapes
        + [
            ((full_len, q_cols), BF),
            ((2, full_len, LANES), F32),
            ((8, 1, 2 * local_len), F32),
        ],
        [me_row, firsts, queries, keys, values_t, starts, wo_t],
        [
            pltpu.VMEM((1, 2 * local_len), F32),
            pltpu.VMEM((head_dim, 2 * local_len), F32),
            pltpu.VMEM((full_len, model_dim), BF),
        ],
        scalars=2,
        limit=20,
    )
    own_tokens = pack[:local_len].astype(F32)
    own_grad = grad_pack.astype(F32)
    near_one, far_one = flip(resid_parts[1], "ctx", 4, 1), flip(resid_parts[3], "ctx", 4, 1)
    far_one = add_low(resid_parts[2], far_one)
    if fast:
        far_one, ff_z2, ff_y1 = bar(far_one, ff_z2, ff_y1)
        ff_z3, ff_y2 = along_z(ff_z2), across_y(ff_z2)
    far_one = flip(far_one, "ctx", 4, 2)
    resid = own_tokens + sum_parts((resid_parts[0], near_one, far_one))
    normed_own = rms_scale(resid, gains[1]).astype(BF)
    normed_core, normed_far = flip(normed_own, "ctx", 4, 1), flip(normed_own, "ctx", 4, 2)
    if fast:
        normed_far, ff_z3, ff_y2 = bar(normed_far, ff_z3, ff_y2)
        cut = ff_block.shape[0] // 2
        ff_w = [ff_block, ff_z1, ff_z2, ff_z3, ff_y0, ff_y1, ff_y2]
        ff_w += [across_y(ff_z3[:cut]), along_z(ff_y2[cut:])]
    normed_two = [normed_own, normed_core, normed_far, flip(normed_far, "ctx", 4, 1)]

    ff_shape = ((full_len, ff_cols), BF)
    hidden, grad_gate, grad_up, w_own, w_down_own, normed_all, grad_all = call(
        functools.partial(feed_body, local_len, len(ff_w)),
        [ff_shape] * 3
        + [((model_dim, 2 * ff_cols), BF), ((model_dim, ff_cols), BF)]
        + [((full_len, model_dim), BF)] * 2,
        [*normed_two, *grad_packs, *ff_w],
        limit=16,
        held=True,
    )

    def ff_chunks(at):
        cut = [dot_tn(normed_all[:, at], g).astype(BF) for g in (grad_gate, grad_up)]
        cut.append(dot_tn(grad_all[:, at], hidden).astype(BF))
        rows = cut[0].shape[0] // 4
        return [
            jnp.concatenate([c[r * rows : (r + 1) * rows] for c in cut], 1) for r in range(4)
        ]

    def pieces_of_sum(last):
        wide = last[0].shape[1]
        return call(
            part_body,
            [((shard, wide), BF)] * 4,
            [me_row, *last],
            [pltpu.VMEM((4 * shard, wide), F32)],
            scalars=1,
            limit=12,
        )

    def land(pieces, widths):
        return call(
            functools.partial(land_body, widths),
            [((shard, 4 * width), BF) for width in widths],
            [me_row, *pieces],
            scalars=1,
        )

    def plain_sums(chunks, widths):
        mine = lax.psum_scatter(jnp.concatenate(chunks, 0), "dp", scatter_dimension=0, tiled=True)
        pieces = [lax.dynamic_slice_in_dim(mine, at * shard, shard, 0) for at in places]
        return place_all(exchange_ctx(pieces), me, widths)

    def tick(*values):
        def body(*refs):
            refs[-1][...] = jnp.zeros((8, LANES), BF)

        return pl.pallas_call(
            body,
            out_shape=jax.ShapeDtypeStruct((8, LANES), BF),
            in_specs=[pl.BlockSpec(memory_space=pl.ANY)] * len(values),
            out_specs=VMEM,
            cost_estimate=pl.CostEstimate(flops=HEAVY, bytes_accessed=1000, transcendentals=0),
        )(*values)

    middle = model_dim // 2
    far = ff_chunks(slice(middle, None))
    if fast:
        cut = 4 * shard // 2
        first, early = across_y(far[1][:cut]), along_z(far[1][cut:])
        far[1], grad_gate, grad_up = bar(far[1], grad_gate, grad_up)
    *two_parts, = call(
        functools.partial(feed_back_body, local_len),
        part_shapes,
        [grad_gate, grad_up, w_own],
        [pltpu.VMEM((full_len, model_dim), BF)],
        limit=8,
        held=True,
    )
    near_two, far_two = flip(two_parts[1], "ctx", 4, 1), flip(two_parts[3], "ctx", 4, 1)
    if fast:
        near_two, far_two, hidden, normed_all, grad_all = bar(near_two, far_two, hidden, normed_all, grad_all)
    near = ff_chunks(slice(0, middle))
    far_two = add_low(two_parts[2], far_two)
    if fast:
        second = jnp.concatenate([far[2][:cut], add_low(far[2][cut:], early)], 0)
        total = jnp.concatenate([add_low(near[1][:cut], first), near[1][cut:]], 0)
        far_two, total, second = bar(far_two, total, second)
        total, second = along_z(total), across_y(second)
    far_two = flip(far_two, "ctx", 4, 2)
    grad_norm_two = sum_parts((two_parts[0], near_two, far_two))
    _, second_pull = jax.vjp(rms_scale, resid, gains[1])
    grad_resid_norm, grad_gain_two = second_pull(grad_norm_two)
    grad_resid = own_grad + grad_resid_norm
    (*down_parts,) = call(
        functools.partial(down_body, local_len),
        part_shapes,
        [hidden, w_down_own],
        [pltpu.VMEM((full_len, model_dim), BF)],
        limit=18,
    )

    grad_low = grad_resid.astype(BF)
    grad_core, grad_far = flip(grad_low, "ctx", 4, 1), flip(grad_low, "ctx", 4, 2)
    if fast:
        grad_far, down_parts = bar(grad_far, down_parts)
    down_near, down_far = flip(down_parts[1], "ctx", 4, 1), flip(down_parts[3], "ctx", 4, 1)
    down_far = add_low(down_parts[2], down_far)
    grad_attn = [grad_low, grad_core, grad_far, flip(grad_far, "ctx", 4, 1)]
    if fast:
        total, third = bar(add_low(near[2], second, total), far[3])
        grad_attn, down_far, tick_two = bar(grad_attn, down_far, tick(total))
        total, third = along_z(total), across_y(third)
    down_far = flip(down_far, "ctx", 4, 2)
    *one_parts, grad_qkv, head_sums, gain_one, grad_attn_all = call(
        functools.partial(attend_back_body, local_len),
        part_shapes
        + [
            ((full_len, q_cols + 2 * kv_cols), BF),
            ((8, LANES), F32),
            ((1, model_dim), F32),
            ((full_len, model_dim), BF),
        ],
        [
            me_row,
            firsts,
            *grad_attn,
            queries,
            keys,
            values,
            keys_t,
            starts,
            attn_wide,
            lse,
            qk_pre,
            cosine,
            sine,
            head_gains,
            w_qkv,
            wo_t,
            normed_one,
            gains,
        ],
        [
            pltpu.VMEM((2, full_len, LANES), BF),
            pltpu.VMEM((2, full_len, LANES), F32),
            pltpu.VMEM((2, full_len, LANES), F32),
            pltpu.VMEM((2, full_len, LANES), F32),
            pltpu.VMEM((head_dim, 2 * local_len), F32),
        ],
        scalars=2,
        limit=24,
        held=True,
    )
    if fast:
        fourth, grad_qkv = bar(far[0], grad_qkv)
        fourth = across_y(fourth)
        total, grad_qkv = bar(add_low(near[3], third, total), grad_qkv)
        last = (near[0], fourth, along_z(total))
    layer_out = sum_out(block_order, resid, (down_parts[0], down_near, down_far))
    attn_chunks = call(
        attn_weights_body,
        [((LANES, wide), BF)] * 8,
        [normed_one, grad_qkv, grad_attn_all, attn_out],
        [pltpu.VMEM((model_dim, wide), BF)],
        limit=20,
    )
    ticks = [tick_two] if fast else []
    (small,) = call(
        small_body,
        [((4, model_dim), F32)],
        [block_order, gain_one, grad_gain_two.reshape(1, -1), head_sums, *ticks],
        scalars=1,
    )
    grad_one = scatter_ctx(one_parts)
    if fast:
        near, far = attn_chunks[:4], attn_chunks[4:]
        total, last = bar(add_low(near[1], across_y(far[1])), last)
        ff_pieces = pieces_of_sum(last)
        total, small_core = bar(
            add_low(near[2], across_y(far[2]), along_z(total)), flip(small, "ctx", 4, 1)
        )
        small = small + small_core
        small = small + flip(small, "ctx", 4, 2)
        total, small_y = bar(
            add_low(near[3], across_y(far[3]), along_z(total)), flip(small, "dp", dp_size, 1)
        )
        small = small + small_y
        attn_last = (near[0], across_y(far[0]), along_z(total))
        attn_last, small_z, ff_got = bar(
            attn_last, flip(small, "dp", dp_size, 2), exchange_ctx(ff_pieces)
        )
        small = small + small_z
        small = small + flip(small, "dp", dp_size, 4)
        attn_pieces = exchange_ctx(pieces_of_sum(attn_last))
        grad_g_out, grad_u_out, grad_d_out = land(ff_got, ff_widths)
        grad_q_out, grad_k_out, grad_v_out, grad_o_out = land(attn_pieces, attn_widths)
    else:
        grad_g_out, grad_u_out, grad_d_out = plain_sums(near + far, ff_widths)
        grad_q_out, grad_k_out, grad_v_out, grad_o_out = plain_sums(attn_chunks, attn_widths)
        small = sum_all(small, dp_size)
    _, first_pull = jax.vjp(lambda u: rms_scale(u, gains[0]), own_tokens)
    input_grad = sum_out(block_order, grad_resid + first_pull(sum_parts(grad_one))[0], ())
    norm_own = lax.dynamic_slice_in_dim(small[:2], lax.axis_index(ALL) * shard, shard, 1)
    head_sum = small[2:, :head_dim] + small[2:, head_dim : 2 * head_dim]
    return (
        layer_out[None],
        input_grad[None],
        grad_q_out,
        grad_k_out,
        grad_v_out,
        grad_o_out.T,
        grad_g_out,
        grad_u_out,
        grad_d_out.T,
        norm_own.astype(BF),
        head_sum.astype(BF),
    )


def solution(mesh):
    def step(*arrays):
        return on_device(mesh.shape["dp"], *arrays)

    in_specs = (
        P("dp", "ctx", None),
        P("dp", "ctx"),
        P(("dp", "ctx"), None),
        P(("dp", "ctx"), None),
        P(("dp", "ctx"), None),
        P(None, ("dp", "ctx")),
        P(("dp", "ctx"), None),
        P(("dp", "ctx"), None),
        P(None, ("dp", "ctx")),
        P(None, ("dp", "ctx")),
        P(),
        P("dp", "ctx", None),
    )
    out_specs = (
        P("dp", "ctx", None),
        P("dp", "ctx", None),
        P(("dp", "ctx"), None),
        P(("dp", "ctx"), None),
        P(("dp", "ctx"), None),
        P(None, ("dp", "ctx")),
        P(("dp", "ctx"), None),
        P(("dp", "ctx"), None),
        P(None, ("dp", "ctx")),
        P(None, ("dp", "ctx")),
        P(),
    )
    return jax.shard_map(step, mesh=mesh, in_specs=in_specs, out_specs=out_specs, check_vma=False)
```

```python
import functools

import jax
import jax.numpy as jnp
from jax import lax
from jax.experimental import pallas as pl
from jax.experimental.pallas import tpu as pltpu
from jax.sharding import PartitionSpec as P

EPS = 1e-05
THETA = 1000000.0
BF = jnp.bfloat16
F32 = jnp.float32
ALL = ("dp", "ctx")


def add_low(*terms):
    total = terms[0].astype(F32)
    for term in terms[1:]:
        total = total + term.astype(F32)
    return total.astype(BF)


def flip(value, axis, size, bits):
    return lax.ppermute(value, axis, [(i, i ^ bits) for i in range(size)])


def gather_ctx(own):
    core = flip(own, "ctx", 4, 1)
    across = flip(own, "ctx", 4, 2)
    return [own, core, across, flip(across, "ctx", 4, 1)]


def scatter_ctx(parts):
    far = flip(parts[3], "ctx", 4, 1)
    near = flip(parts[1], "ctx", 4, 1)
    return parts[0], near, flip(add_low(parts[2], far), "ctx", 4, 2)


def sum_parts(parts):
    return parts[0].astype(F32) + parts[1].astype(F32) + parts[2].astype(F32)


def exchange_ctx(parts):
    return [parts[0]] + [flip(parts[j], "ctx", 4, j) for j in range(1, 4)]


def place(parts, where, axis):
    size = parts[0].shape[axis]
    shape = list(parts[0].shape)
    shape[axis] = size * len(parts)
    out = jnp.zeros(shape, parts[0].dtype)
    for part, at in zip(parts, where):
        out = lax.dynamic_update_slice_in_dim(out, part, at * size, axis)
    return out


def bar(*trees):
    return lax.optimization_barrier(trees)


def ordered(dp_size):
    return dp_size == 8


def dp_order(dp_size):
    me = lax.axis_index("dp")
    return [((me - 2 * (i % 4)) % dp_size) ^ (i // 4) for i in range(dp_size)]


def across_y(value):
    return flip(value, "dp", 8, 1)


def along_z(value):
    return lax.ppermute(value, "dp", [(i, (i + 2) % 8) for i in range(8)])


def sum_all(value, dp_size):
    for bits in (1, 2):
        value = value + flip(value, "ctx", 4, bits)
    bits = 1
    while bits < dp_size:
        value = value + flip(value, "dp", dp_size, bits)
        bits *= 2
    return value


def dot(a, b):
    return lax.dot_general(a, b, (((1,), (0,)), ((), ())), preferred_element_type=F32)


def dot_nt(a, b):
    return lax.dot_general(a, b, (((1,), (1,)), ((), ())), preferred_element_type=F32)


def dot_tn(a, b):
    return lax.dot_general(a, b, (((0,), (0,)), ((), ())), preferred_element_type=F32)


VMEM = pl.BlockSpec(memory_space=pltpu.VMEM)
SMEM = pl.BlockSpec(memory_space=pltpu.SMEM)
LANES = 128
HIGH = lax.Precision.HIGHEST


HEAVY = 10**11


def call(body, outs, ins, scratch=(), scalars=0, limit=4, flops=1000000, held=False):
    def spec(shape):
        if held:
            return VMEM
        zeros = (0,) * len(shape)
        return pl.BlockSpec(tuple(shape), lambda i: zeros, pipeline_mode=pl.Buffered(1))

    return pl.pallas_call(
        body,
        out_shape=[jax.ShapeDtypeStruct(shape, kind) for shape, kind in outs],
        grid=() if held else (1,),
        in_specs=[SMEM] * scalars + [spec(x.shape) for x in ins[scalars:]],
        out_specs=[spec(shape) for shape, _ in outs],
        scratch_shapes=list(scratch),
        compiler_params=pltpu.CompilerParams(vmem_limit_bytes=limit << 20),
        cost_estimate=pl.CostEstimate(flops=flops, bytes_accessed=1000, transcendentals=0),
    )(*ins)


def pack_body(order_ref, tokens_ref, docs_ref, out_ref):
    rows = tokens_ref.shape[0]

    def one(i, _):
        out_ref[:rows, columns(i, LANES)] = tokens_ref[:, columns(order_ref[i], LANES)]
        return 0

    lax.fori_loop(0, tokens_ref.shape[1] // LANES, one, 0)
    if docs_ref is not None:
        below = jnp.broadcast_to(docs_ref[...].astype(F32), (16, rows)).astype(BF)
        out_ref[rows:, :rows] = below
        out_ref[rows:, rows:] = jnp.zeros((16, out_ref.shape[1] - rows), BF)


def pack_rows(order, rows, doc_row=None):
    if doc_row is None:
        body = lambda order_ref, rows_ref, out_ref: pack_body(order_ref, rows_ref, None, out_ref)
        return call(body, [(rows.shape, BF)], [order, rows], scalars=1)[0]
    shape = (rows.shape[0] + 16, rows.shape[1])
    return call(pack_body, [(shape, BF)], [order, rows, doc_row.reshape(1, -1)], scalars=1)[0]


def sum_body(order_ref, base_ref, *refs):
    parts, out_ref = refs[:-1], refs[-1]

    def one(i, _):
        at = columns(i, LANES)
        total = base_ref[:, at]
        if parts:
            part = parts[0][:, at].astype(F32)
            for ref in parts[1:]:
                part = part + ref[:, at].astype(F32)
            total = total + part
        out_ref[:, columns(order_ref[i], LANES)] = total.astype(BF)
        return 0

    lax.fori_loop(0, base_ref.shape[1] // LANES, one, 0)


def sum_out(order, base, parts):
    return call(sum_body, [(base.shape, BF)], [order, base, *parts], scalars=1)[0]


def by_blocks(count, rows, body):
    def one(i, _):
        body(pl.ds(pl.multiple_of(i * rows, rows), rows))
        return 0

    lax.fori_loop(0, count, one, 0)


def move(target, to, source, start, rows):
    step = 32

    def one(i, _):
        goal = pl.ds(pl.multiple_of(to + i * step, step), step)
        target[goal, :] = source[pl.ds(pl.multiple_of(start + i * step, step), step), :]
        return 0

    lax.fori_loop(0, rows // step, one, 0)


def hand_out(ref, parts):
    rows = parts[0].shape[0]
    for j, part in enumerate(parts):
        move(part, 0, ref, j * rows, rows)


def lane_masks(rows):
    lane = lax.broadcasted_iota(jnp.int32, (rows, LANES), 1)
    return lane < 64, lax.rem(lane, 64) < 32


def half_sums(squares):
    row = lax.broadcasted_iota(jnp.int32, (LANES, LANES), 0) // 64
    col = lax.broadcasted_iota(jnp.int32, (LANES, LANES), 1) // 64
    return jnp.dot(
        squares, (row == col).astype(F32), preferred_element_type=F32, precision=HIGH
    )


def turn(value, first):
    return jnp.where(first, pltpu.roll(value, 96, 1), pltpu.roll(value, 32, 1))


def doubled(value, left):
    other = pltpu.roll(value, 64, 1)
    return jnp.where(left, value, other), jnp.where(left, other, value)


def prepare_body(rows, *refs):
    packs, blocks = refs[:4], refs[4:12]
    table_ref, head_ref = refs[12:14]
    normed_ref, saved_ref, q_ref, kd_ref, rest_ref, kt_ref, vt_ref = refs[14:21]
    wo_ref, gains_ref, all_ref = refs[21:24]
    for i, block in enumerate(blocks):
        at = i * LANES
        rest_ref[at : at + LANES, 256:] = block[:LANES, :512]
        wo_ref[at : at + LANES, :] = block[:LANES, 512:]
        gains_ref[:, at : at + LANES] = block[LANES : LANES + 8, :LANES].astype(F32)
    for j, pack in enumerate(packs):
        move(all_ref, j * rows, pack, 0, rows)
    left, first = lane_masks(LANES)
    gain = gains_ref[0:1, :]
    q_gain, k_gain = head_ref[0:1, :], head_ref[1:2, :]

    def chunk(i, _):
        at = pl.ds(pl.multiple_of(i * LANES, LANES), LANES)
        x = all_ref[at, :].astype(F32)
        scale = lax.rsqrt(jnp.mean(x * x, -1, keepdims=True) + EPS)
        normed = (x * scale * gain).astype(BF)
        normed_ref[at, :] = normed
        pre = jnp.dot(normed, rest_ref[:, 256:], preferred_element_type=F32)
        saved_ref[at, :384] = pre[:, :384]
        saved_ref[at, 384:] = table_ref[at, :]
        cos, sin = doubled(table_ref[at, :], left)
        turned = []
        for b in range(3):
            u = pre[:, b * LANES : (b + 1) * LANES]
            u = u * lax.rsqrt(half_sums(u * u) * (1.0 / 64) + EPS) * (k_gain if b == 2 else q_gain)
            turned.append(u * cos + turn(u, first) * sin)
        q_ref[0, at, :] = turned[0].astype(BF)
        q_ref[1, at, :] = turned[1].astype(BF)
        key, value = turned[2], pre[:, 384:]
        low, high = doubled(key, left)
        kd_ref[0, at, :] = low.astype(BF)
        kd_ref[1, at, :] = high.astype(BF)
        kt_ref[:, at] = key.T.astype(BF)
        low, high = doubled(value, left)
        rest_ref[at, :LANES] = low.astype(BF)
        rest_ref[at, LANES:256] = high.astype(BF)
        vt_ref[:, at] = value.T.astype(BF)
        return 0

    lax.fori_loop(0, all_ref.shape[0] // LANES, chunk, 0)


def two_heads(block, left):
    zero = jnp.zeros_like(block)
    return jnp.concatenate([jnp.where(left, block, zero), jnp.where(left, zero, block)], 0)


def seen(start_row, first_key, rows, first_query):
    shape = (rows, 2 * rows)
    key = lax.broadcasted_iota(jnp.int32, shape, 0)
    mask = key + first_key >= start_row
    if first_query is not None:
        lane = lax.broadcasted_iota(jnp.int32, shape, 1)
        mask = mask & (key <= jnp.where(lane < rows, lane, lane - rows))
    return mask


LOG2E = 1.4426950408889634
SCORE = LOG2E / 8.0


def attend_body(rows, me_ref, first_ref, q_ref, kd_ref, vt_ref, start_ref, wo_ref, *refs):
    parts = refs[:4]
    out_ref, wide_ref, lse_ref, sum_ref, acc_ref, part_ref = refs[4:10]
    me = me_ref[0]
    left = lax.broadcasted_iota(jnp.int32, (rows, LANES), 1) < 64

    def one(step, _):
        kv, a = step // 4, lax.rem(step, 4)
        at_q = pl.ds(pl.multiple_of((a ^ me) * rows, rows), rows)
        q2 = two_heads(q_ref[kv, at_q, :], left)
        start_row = start_ref[a ^ me]
        sum_ref[...] = jnp.zeros_like(sum_ref)
        acc_ref[...] = jnp.zeros_like(acc_ref)
        for d in range(3):

            @pl.when((a >= d) & (first_ref[a ^ me] < (a - d + 1) * rows))
            def _():
                at_k = pl.ds(pl.multiple_of(((a - d) ^ me) * rows, rows), rows)
                scores = dot_nt(kd_ref[kv, at_k, :], q2)
                mask = seen(start_row, (a - d) * rows, rows, a if d == 0 else None)
                p = jnp.where(mask, jnp.exp2(scores * SCORE), 0.0)
                sum_ref[...] += jnp.sum(p, 0, keepdims=True)
                half = pl.ds(pl.multiple_of(kv * 64, 64), 64)
                acc_ref[...] += dot(vt_ref[half, at_k], p.astype(BF))

        total = sum_ref[...]
        lse_ref[kv * 4 + (a ^ me)] = jnp.log2(total)
        mixed = acc_ref[...] / total
        mixed = jnp.concatenate([mixed[:, :rows], mixed[:, rows:]], 0).T
        wide_ref[kv, at_q, :] = mixed
        out_ref[at_q, columns(kv, LANES)] = mixed.astype(BF)
        return 0

    lax.fori_loop(0, 8, one, 0)

    def project(at):
        part_ref[at, :] = dot_nt(out_ref[at, :], wo_ref[...]).astype(BF)

    by_blocks(4, rows, project)
    hand_out(part_ref, parts)


def attend_back_body(rows, *refs):
    me_ref, first_ref = refs[:2]
    refs = refs[1:]
    g0, g1, g2, g3, q_ref, kd_ref, rest_ref, kt_ref, start_ref, wide_ref, lse_ref = refs[1:12]
    saved_ref, head_ref, wo_ref, normed_ref, gains_ref = refs[12:17]
    parts, low_ref, head_sum_ref, gain_sum_ref, grad_ref = refs[17:21], *refs[21:25]
    mixed_ref, dq_ref, dk_ref, dv_ref, acc_ref = refs[25:30]
    me = me_ref[0]
    left = lax.broadcasted_iota(jnp.int32, (rows, LANES), 1) < 64
    for j, g in enumerate((g0, g1, g2, g3)):
        move(grad_ref, j * rows, g, 0, rows)

    def mix(at):
        grad = dot(grad_ref[at, :], wo_ref[...]).astype(BF)
        mixed_ref[0, at, :] = grad[:, :LANES]
        mixed_ref[1, at, :] = grad[:, LANES:]

    by_blocks(4, rows, mix)
    dk_ref[...] = jnp.zeros_like(dk_ref)
    dv_ref[...] = jnp.zeros_like(dv_ref)
    pick = (
        lax.broadcasted_iota(jnp.int32, (8, LANES), 1) // 64
        == lax.broadcasted_iota(jnp.int32, (8, LANES), 0)
    ).astype(F32)

    def one(step, _):
        kv, a = step // 4, lax.rem(step, 4)
        at_q = pl.ds(pl.multiple_of((a ^ me) * rows, rows), rows)
        q2 = two_heads(q_ref[kv, at_q, :], left)
        grad = mixed_ref[kv, at_q, :]
        g2 = two_heads(grad, left)
        inner = lax.dot_general(
            pick,
            grad.astype(F32) * wide_ref[kv, at_q, :],
            (((1,), (1,)), ((), ())),
            preferred_element_type=F32,
            precision=HIGH,
        )
        inner = jnp.concatenate([inner[0:1], inner[1:2]], 1)
        lse = lse_ref[kv * 4 + (a ^ me)]
        start_row = start_ref[a ^ me]
        acc_ref[...] = jnp.zeros_like(acc_ref)
        for d in range(3):

            @pl.when((a >= d) & (first_ref[a ^ me] < (a - d + 1) * rows))
            def _():
                at_k = pl.ds(pl.multiple_of(((a - d) ^ me) * rows, rows), rows)
                scores = dot_nt(kd_ref[kv, at_k, :], q2)
                mask = seen(start_row, (a - d) * rows, rows, a if d == 0 else None)
                p = jnp.where(mask, jnp.exp2(scores * SCORE - lse), 0.0)
                gp = dot_nt(rest_ref[at_k, columns(kv, LANES)], g2)
                gs = (p * (gp - inner)).astype(BF)
                dv_ref[kv, at_k, :] += dot(p.astype(BF), g2)
                dk_ref[kv, at_k, :] += dot(gs, q2)
                half = pl.ds(pl.multiple_of(kv * 64, 64), 64)
                acc_ref[...] += dot(kt_ref[half, at_k], gs)

        both = acc_ref[...] * 0.125
        dq_ref[kv, at_q, :] = jnp.concatenate([both[:, :rows], both[:, rows:]], 0).T
        return 0

    lax.fori_loop(0, 8, one, 0)
    left, first = lane_masks(LANES)
    head_sum_ref[...] = jnp.zeros_like(head_sum_ref)

    def folded(ref, at):
        low, high = ref[0, at, :], ref[1, at, :]
        low, high = low + pltpu.roll(low, 64, 1), high + pltpu.roll(high, 64, 1)
        return jnp.where(left, low, high)

    def chunk(i, _):
        at = pl.ds(pl.multiple_of(i * LANES, LANES), LANES)
        cos, sin = doubled(saved_ref[at, 384:], left)
        for b in range(3):
            u = saved_ref[at, b * LANES : (b + 1) * LANES]
            g = folded(dk_ref, at) * 0.125 if b == 2 else dq_ref[b, at, :]
            w = g * cos - turn(g, first) * sin
            row = 1 if b == 2 else 0
            gain = head_ref[row : row + 1, :]
            r = lax.rsqrt(half_sums(u * u) * (1.0 / 64) + EPS)
            head_sum_ref[row : row + 1, :] += jnp.sum(w * u * r, 0, keepdims=True)
            w = w * gain
            back = r * w - u * (r * r * r) * (half_sums(w * u) * (1.0 / 64))
            low_ref[at, b * LANES : (b + 1) * LANES] = back.astype(BF)
        low_ref[at, 384:] = folded(dv_ref, at).astype(BF)
        return 0

    lax.fori_loop(0, low_ref.shape[0] // LANES, chunk, 0)
    gain_sum = jnp.zeros((1, normed_ref.shape[1]), F32)
    for j in range(4):
        at = slice(j * rows, (j + 1) * rows)
        grad = dot_nt(low_ref[at, :], rest_ref[:, 256:])
        parts[j][...] = grad.astype(BF)
        gain_sum = gain_sum + jnp.sum(grad * normed_ref[at, :].astype(F32), 0, keepdims=True)
    gain_sum_ref[...] = gain_sum / gains_ref[0:1, :]


def columns(at, width):
    return pl.ds(pl.multiple_of(at * width, LANES), width)


def spread_body(widths, me_ref, *refs):
    weights, outs = refs[: len(widths)], refs[-4:]
    rows = weights[0].shape[0]
    me = me_ref[0]
    for j, out in enumerate(outs):
        start = 0
        for weight, width in zip(weights, widths):
            out[:rows, start : start + width] = weight[:, columns(me ^ j, width)]
            start += width
    if len(refs) > len(widths) + 4:
        gains = refs[len(widths)][...].astype(F32)
        gains = jnp.concatenate([gains, jnp.zeros((6, rows), F32)], 0)
        gains = jnp.concatenate([gains] * (LANES // rows), 1)
        lane = lax.broadcasted_iota(jnp.int32, (8, LANES), 1)
        gains = jnp.where(lane // rows == me, gains, 0.0).astype(BF)
        for out in outs:
            out[rows:, :] = jnp.zeros((8, out.shape[1]), BF)
            out[rows:, :LANES] = gains


def join_body(rows, me_ref, *refs):
    pieces, out = refs[:4], refs[4]
    me = me_ref[0]
    for j, piece in enumerate(pieces):
        out[pl.ds(pl.multiple_of((me ^ j) * rows, rows), rows), :] = piece[:rows, :]
    if pieces[0].shape[0] > rows:
        below = [piece[rows:, :].astype(F32) for piece in pieces]
        out[4 * rows :, :] = (below[0] + below[1] + below[2] + below[3]).astype(BF)


def part_body(me_ref, one_ref, two_ref, three_ref, *refs):
    outs, total_ref = refs[:4], refs[4]
    total = one_ref[...].astype(F32) + two_ref[...].astype(F32) + three_ref[...].astype(F32)
    total_ref[...] = total
    rows = outs[0].shape[0]
    for j, out in enumerate(outs):
        at = pl.ds(pl.multiple_of((me_ref[0] ^ j) * rows, rows), rows)
        out[...] = total_ref[at, :].astype(BF)


def land_body(widths, me_ref, *refs):
    pieces, outs = refs[:4], refs[4:]
    me = me_ref[0]
    start = 0
    for out, width in zip(outs, widths):
        for j, piece in enumerate(pieces):
            out[:, columns(me ^ j, width)] = piece[:, start : start + width]
        start += width


def small_body(order_ref, one_ref, two_ref, head_ref, *refs):
    out_ref = refs[-1]
    out_ref[...] = jnp.zeros_like(out_ref)
    for i in range(one_ref.shape[1] // LANES):
        at = columns(order_ref[i], LANES)
        out_ref[0:1, at] = one_ref[:, i * LANES : (i + 1) * LANES]
        out_ref[1:2, at] = two_ref[:, i * LANES : (i + 1) * LANES]
    out_ref[2:4, :LANES] = head_ref[0:2, :]


def feed_body(rows, pieces, *refs):
    normed, packs, weights = refs[:4], refs[4:8], refs[8 : 8 + pieces]
    hidden_ref, gate_ref, up_ref, w_ref, down_ref, normed_ref, grad_ref = refs[8 + pieces :]
    ff = hidden_ref.shape[1]
    row = 0
    for weight in weights:
        move(w_ref, row, weight.at[:, : 2 * ff], 0, weight.shape[0])
        move(down_ref, row, weight.at[:, 2 * ff :], 0, weight.shape[0])
        row += weight.shape[0]
    for j in range(4):
        move(normed_ref, j * rows, normed[j], 0, rows)
        move(grad_ref, j * rows, packs[j], 0, rows)

    def one(i, _):
        at = pl.ds(pl.multiple_of(i * rows, rows), rows)
        x = normed_ref[at, :]
        gate, up = dot(x, w_ref[:, :ff]), dot(x, w_ref[:, ff:])
        grad = dot(grad_ref[at, :], down_ref[...])
        sig = 1.0 / (1.0 + jnp.exp(-gate))
        silu = gate * sig
        hidden_ref[at, :] = (silu * up).astype(BF)
        gate_ref[at, :] = (grad * up * (sig * (1.0 + gate * (1.0 - sig)))).astype(BF)
        up_ref[at, :] = (grad * silu).astype(BF)
        return 0

    lax.fori_loop(0, 4, one, 0)


def feed_back_body(rows, gate_ref, up_ref, w_ref, *refs):
    parts, part_ref = refs[:4], refs[4]
    ff = gate_ref.shape[1]

    def one(i, _):
        at = pl.ds(pl.multiple_of(i * rows, rows), rows)
        total = dot_nt(gate_ref[at, :], w_ref[:, :ff]) + dot_nt(up_ref[at, :], w_ref[:, ff:])
        part_ref[at, :] = total.astype(BF)
        return 0

    lax.fori_loop(0, 4, one, 0)
    hand_out(part_ref, parts)


def down_body(rows, hidden_ref, down_ref, *refs):
    parts, part_ref = refs[:4], refs[4]

    def one(at):
        part_ref[at, :] = dot_nt(hidden_ref[at, :], down_ref[...]).astype(BF)

    by_blocks(4, rows, one)
    hand_out(part_ref, parts)


def attn_weights_body(normed_ref, grad_qkv_ref, grad_ref, out_ref, *chunks):
    cut = grad_qkv_ref.shape[1]
    chunks, whole_ref = chunks[:-1], chunks[-1]
    width = 2 * LANES

    def one(i, _):
        at = columns(i, width)
        whole_ref[at, :cut] = dot_tn(normed_ref[:, at], grad_qkv_ref[...]).astype(BF)
        whole_ref[at, cut:] = dot_tn(grad_ref[:, at], out_ref[...]).astype(BF)
        return 0

    lax.fori_loop(0, whole_ref.shape[0] // width, one, 0)
    hand_out(whole_ref, chunks)


def rms_scale(values, gain_row):
    return values * lax.rsqrt(jnp.mean(values * values, -1, keepdims=True) + EPS) * gain_row


def place_all(pieces, me, widths):
    outs, start = [], 0
    for width in widths:
        cut = [p[:, start : start + width] for p in pieces]
        outs.append(place(cut, [me ^ j for j in range(4)], 1))
        start += width
    return outs


def on_device(
    dp_size,
    tokens,
    doc_ids,
    w_query,
    key_weight,
    value_weight,
    w_output,
    w_gate,
    w_up,
    w_down,
    norm_gains,
    head_norm_gains,
    out_grad,
):
    local_len, model_dim = tokens.shape[1:]
    tokens, out_grad, doc_row = tokens[0], out_grad[0], doc_ids[0]
    head_dim = head_norm_gains.shape[1]
    q_cols, kv_cols = w_query.shape[1] // 4, key_weight.shape[1] // 4
    shard = norm_gains.shape[1]
    ff_cols = w_gate.shape[1] // 4
    me = lax.axis_index("ctx")
    places = [me ^ j for j in range(4)]
    full_len = 4 * local_len
    fast = ordered(dp_size)
    block_order = jnp.stack(dp_order(dp_size)) if fast else jnp.arange(model_dim // LANES)
    block_order = block_order.astype(jnp.int32)
    me_row = me.reshape(1).astype(jnp.int32)
    attn_widths = (q_cols, kv_cols, kv_cols, q_cols)
    ff_widths = (ff_cols, ff_cols, ff_cols)
    wide, ff_wide = sum(attn_widths), sum(ff_widths)
    attn_local = [w_query, key_weight, value_weight, w_output.T]
    ff_local = [w_gate, w_up, w_down.T]

    pack = pack_rows(block_order, tokens, doc_row)
    grad_pack = pack_rows(block_order, out_grad)
    if fast:
        sent = call(
            functools.partial(spread_body, attn_widths),
            [((shard + 8, wide), BF)] * 4,
            [me_row, *attn_local, norm_gains],
            scalars=1,
        )
        ff_sent = call(
            functools.partial(spread_body, ff_widths),
            [((shard, ff_wide), BF)] * 4,
            [me_row, *ff_local],
            scalars=1,
        )
        got, ff_sent = bar(exchange_ctx(sent), ff_sent)
        ff_got = exchange_ctx(ff_sent)
        (block,) = call(
            functools.partial(join_body, shard),
            [((4 * shard + 8, wide), BF)],
            [me_row, *got],
            scalars=1,
        )
        y0, z1, pack, ff_got = bar(across_y(block), along_z(block), pack, ff_got)
        core_pack, far_pack = flip(pack, "ctx", 4, 1), flip(pack, "ctx", 4, 2)
        y1, z2 = bar(across_y(z1), along_z(z1))
        (ff_block,) = call(
            functools.partial(join_body, shard),
            [((4 * shard, ff_wide), BF)],
            [me_row, *ff_got],
            scalars=1,
        )
        y2, z3, far_pack, grad_pack, ff_block = bar(
            across_y(z2), along_z(z2), far_pack, grad_pack, ff_block
        )
        far_core_pack = flip(far_pack, "ctx", 4, 1)
        y3, ff_block, far_core_pack = bar(across_y(z3), ff_block, far_core_pack)
        ff_z1, ff_y0 = along_z(ff_block), across_y(ff_block)
        blocks = [block, z1, z2, z3, y0, y1, y2, y3]
    else:

        def pieces_of(weights):
            sent = []
            for at in places:
                cut = [
                    lax.dynamic_slice_in_dim(w, at * (w.shape[1] // 4), w.shape[1] // 4, 1)
                    for w in weights
                ]
                sent.append(jnp.concatenate(cut, 1))
            return sent

        def whole(weights):
            block = place(exchange_ctx(pieces_of(weights)), places, 0)
            return lax.all_gather(block, "dp", axis=0, tiled=True)

        gains = lax.all_gather(norm_gains, ALL, axis=1, tiled=True).reshape(2, -1, LANES)
        gains = jnp.pad(gains.transpose(1, 0, 2), ((0, 0), (0, 6), (0, wide - LANES)))
        blocks = jnp.concatenate([whole(attn_local).reshape(-1, LANES, wide), gains], 1)
        blocks = [blocks[i] for i in range(blocks.shape[0])]
        ff_w = [whole(ff_local)]
        core_pack, far_pack = flip(pack, "ctx", 4, 1), flip(pack, "ctx", 4, 2)
        far_core_pack = flip(far_pack, "ctx", 4, 1)

    packs = [pack, core_pack, far_pack, far_core_pack]
    core_grad, far_grad = flip(grad_pack, "ctx", 4, 1), flip(grad_pack, "ctx", 4, 2)
    docs = jnp.concatenate([p[local_len, :local_len] for p in packs])
    index = jnp.concatenate(
        [at * local_len + jnp.arange(local_len, dtype=jnp.int32) for at in places]
    )
    starts = jnp.sum((docs[None, :] < docs[:, None]).astype(jnp.int32), -1)
    positions = (index - starts).astype(F32)
    half = head_dim // 2
    lane = jnp.arange(LANES)
    freqs = THETA ** (-(2.0 * (lane % half).astype(F32)) / head_dim)
    angles = positions[:, None] * freqs
    sine = jnp.sin(angles) * jnp.where(lane % head_dim < half, -1.0, 1.0)
    table = jnp.where(lane < head_dim, jnp.cos(angles), sine)
    starts = starts.reshape(4, local_len)
    firsts = starts[:, 0]
    starts = jnp.concatenate([starts, starts], 1).reshape(4, 1, 2 * local_len)
    head_gains = jnp.concatenate([head_norm_gains, head_norm_gains], 1).astype(F32)

    part_shapes = [((local_len, model_dim), BF)] * 4
    normed_one, saved, queries, keys, rest, keys_t, values_t, wo_t, gains = call(
        functools.partial(prepare_body, local_len),
        [
            ((full_len, model_dim), BF),
            ((full_len, q_cols + kv_cols + LANES), F32),
            ((2, full_len, LANES), BF),
            ((2, full_len, LANES), BF),
            ((full_len, 2 * LANES + q_cols + 2 * kv_cols), BF),
            ((LANES, full_len), BF),
            ((LANES, full_len), BF),
            ((model_dim, q_cols), BF),
            ((8, model_dim), F32),
        ],
        [*packs, *blocks, table, head_gains],
        [pltpu.VMEM((full_len, model_dim), BF)],
        limit=28,
        flops=HEAVY,
    )
    if fast:
        queries, keys, ff_z1, ff_y0, core_grad, far_grad = bar(
            queries, keys, ff_z1, ff_y0, core_grad, far_grad
        )
        ff_z2, ff_y1 = along_z(ff_z1), across_y(ff_z1)
    grad_packs = [grad_pack, core_grad, far_grad, flip(far_grad, "ctx", 4, 1)]
    *resid_parts, attn_out, attn_wide, lse = call(
        functools.partial(attend_body, local_len),
        part_shapes
        + [
            ((full_len, q_cols), BF),
            ((2, full_len, LANES), F32),
            ((8, 1, 2 * local_len), F32),
        ],
        [me_row, firsts, queries, keys, values_t, starts, wo_t],
        [
            pltpu.VMEM((1, 2 * local_len), F32),
            pltpu.VMEM((head_dim, 2 * local_len), F32),
            pltpu.VMEM((full_len, model_dim), BF),
        ],
        scalars=2,
        limit=20,
    )
    own_tokens = pack[:local_len].astype(F32)
    own_grad = grad_pack.astype(F32)
    near_one, far_one = flip(resid_parts[1], "ctx", 4, 1), flip(resid_parts[3], "ctx", 4, 1)
    far_one = add_low(resid_parts[2], far_one)
    if fast:
        far_one, ff_z2, ff_y1 = bar(far_one, ff_z2, ff_y1)
        ff_z3, ff_y2 = along_z(ff_z2), across_y(ff_z2)
    far_one = flip(far_one, "ctx", 4, 2)
    resid = own_tokens + sum_parts((resid_parts[0], near_one, far_one))
    normed_own = rms_scale(resid, gains[1]).astype(BF)
    normed_core, normed_far = flip(normed_own, "ctx", 4, 1), flip(normed_own, "ctx", 4, 2)
    if fast:
        normed_far, ff_z3, ff_y2 = bar(normed_far, ff_z3, ff_y2)
        cut = ff_block.shape[0] // 2
        ff_w = [ff_block, ff_z1, ff_z2, ff_z3, ff_y0, ff_y1, ff_y2]
        ff_w += [across_y(ff_z3[:cut]), along_z(ff_y2[cut:])]
    normed_two = [normed_own, normed_core, normed_far, flip(normed_far, "ctx", 4, 1)]

    ff_shape = ((full_len, ff_cols), BF)
    hidden, grad_gate, grad_up, w_own, w_down_own, normed_all, grad_all = call(
        functools.partial(feed_body, local_len, len(ff_w)),
        [ff_shape] * 3
        + [((model_dim, 2 * ff_cols), BF), ((model_dim, ff_cols), BF)]
        + [((full_len, model_dim), BF)] * 2,
        [*normed_two, *grad_packs, *ff_w],
        limit=16,
        held=True,
    )

    def ff_chunks(at):
        cut = [dot_tn(normed_all[:, at], g).astype(BF) for g in (grad_gate, grad_up)]
        cut.append(dot_tn(grad_all[:, at], hidden).astype(BF))
        rows = cut[0].shape[0] // 4
        return [
            jnp.concatenate([c[r * rows : (r + 1) * rows] for c in cut], 1) for r in range(4)
        ]

    def pieces_of_sum(last):
        wide = last[0].shape[1]
        return call(
            part_body,
            [((shard, wide), BF)] * 4,
            [me_row, *last],
            [pltpu.VMEM((4 * shard, wide), F32)],
            scalars=1,
            limit=12,
        )

    def land(pieces, widths):
        return call(
            functools.partial(land_body, widths),
            [((shard, 4 * width), BF) for width in widths],
            [me_row, *pieces],
            scalars=1,
        )

    def plain_sums(chunks, widths):
        mine = lax.psum_scatter(jnp.concatenate(chunks, 0), "dp", scatter_dimension=0, tiled=True)
        pieces = [lax.dynamic_slice_in_dim(mine, at * shard, shard, 0) for at in places]
        return place_all(exchange_ctx(pieces), me, widths)

    def tick(*values):
        def body(*refs):
            refs[-1][...] = jnp.zeros((8, LANES), BF)

        return pl.pallas_call(
            body,
            out_shape=jax.ShapeDtypeStruct((8, LANES), BF),
            in_specs=[pl.BlockSpec(memory_space=pl.ANY)] * len(values),
            out_specs=VMEM,
            cost_estimate=pl.CostEstimate(flops=HEAVY, bytes_accessed=1000, transcendentals=0),
        )(*values)

    middle = model_dim // 2
    far = ff_chunks(slice(middle, None))
    if fast:
        cut = 4 * shard // 2
        first, early = across_y(far[1][:cut]), along_z(far[1][cut:])
        far[1], grad_gate, grad_up = bar(far[1], grad_gate, grad_up)
    *two_parts, = call(
        functools.partial(feed_back_body, local_len),
        part_shapes,
        [grad_gate, grad_up, w_own],
        [pltpu.VMEM((full_len, model_dim), BF)],
        limit=8,
        held=True,
    )
    near_two, far_two = flip(two_parts[1], "ctx", 4, 1), flip(two_parts[3], "ctx", 4, 1)
    if fast:
        near_two, far_two, hidden, normed_all, grad_all = bar(near_two, far_two, hidden, normed_all, grad_all)
    near = ff_chunks(slice(0, middle))
    far_two = add_low(two_parts[2], far_two)
    if fast:
        second = jnp.concatenate([far[2][:cut], add_low(far[2][cut:], early)], 0)
        total = jnp.concatenate([add_low(near[1][:cut], first), near[1][cut:]], 0)
        far_two, total, second = bar(far_two, total, second)
        total, second = along_z(total), across_y(second)
    far_two = flip(far_two, "ctx", 4, 2)
    grad_norm_two = sum_parts((two_parts[0], near_two, far_two))
    _, second_pull = jax.vjp(rms_scale, resid, gains[1])
    grad_resid_norm, grad_gain_two = second_pull(grad_norm_two)
    grad_resid = own_grad + grad_resid_norm
    (*down_parts,) = call(
        functools.partial(down_body, local_len),
        part_shapes,
        [hidden, w_down_own],
        [pltpu.VMEM((full_len, model_dim), BF)],
        limit=18,
    )

    grad_low = grad_resid.astype(BF)
    grad_core, grad_far = flip(grad_low, "ctx", 4, 1), flip(grad_low, "ctx", 4, 2)
    if fast:
        grad_far, down_parts = bar(grad_far, down_parts)
    down_near, down_far = flip(down_parts[1], "ctx", 4, 1), flip(down_parts[3], "ctx", 4, 1)
    down_far = add_low(down_parts[2], down_far)
    grad_attn = [grad_low, grad_core, grad_far, flip(grad_far, "ctx", 4, 1)]
    if fast:
        total, third = bar(add_low(near[2], second, total), far[3])
        grad_attn, down_far, tick_two = bar(grad_attn, down_far, tick(total))
        total, third, fourth = along_z(total), across_y(third), across_y(far[0])
    down_far = flip(down_far, "ctx", 4, 2)
    *one_parts, grad_qkv, head_sums, gain_one, grad_attn_all = call(
        functools.partial(attend_back_body, local_len),
        part_shapes
        + [
            ((full_len, q_cols + 2 * kv_cols), BF),
            ((8, LANES), F32),
            ((1, model_dim), F32),
            ((full_len, model_dim), BF),
        ],
        [
            me_row,
            firsts,
            *grad_attn,
            queries,
            keys,
            rest,
            keys_t,
            starts,
            attn_wide,
            lse,
            saved,
            head_gains,
            wo_t,
            normed_one,
            gains,
        ],
        [
            pltpu.VMEM((2, full_len, LANES), BF),
            pltpu.VMEM((2, full_len, LANES), F32),
            pltpu.VMEM((2, full_len, LANES), F32),
            pltpu.VMEM((2, full_len, LANES), F32),
            pltpu.VMEM((head_dim, 2 * local_len), F32),
        ],
        scalars=2,
        limit=24,
        held=True,
    )
    if fast:
        total, grad_qkv = bar(add_low(near[3], third, total), grad_qkv)
        last = (near[0], fourth, along_z(total))
    layer_out = sum_out(block_order, resid, (down_parts[0], down_near, down_far))
    attn_chunks = call(
        attn_weights_body,
        [((LANES, wide), BF)] * 8,
        [normed_one, grad_qkv, grad_attn_all, attn_out],
        [pltpu.VMEM((model_dim, wide), BF)],
        limit=20,
    )
    ticks = [tick_two] if fast else []
    (small,) = call(
        small_body,
        [((4, model_dim), F32)],
        [block_order, gain_one, grad_gain_two.reshape(1, -1), head_sums, *ticks],
        scalars=1,
    )
    grad_one = scatter_ctx(one_parts)
    if fast:
        near, far = attn_chunks[:4], attn_chunks[4:]
        total, last = bar(add_low(near[1], across_y(far[1])), last)
        ff_pieces = pieces_of_sum(last)
        total, small_core = bar(
            add_low(near[2], across_y(far[2]), along_z(total)), flip(small, "ctx", 4, 1)
        )
        small = small + small_core
        small = small + flip(small, "ctx", 4, 2)
        total, small_y = bar(
            add_low(near[3], across_y(far[3]), along_z(total)), flip(small, "dp", dp_size, 1)
        )
        small = small + small_y
        attn_last = (near[0], across_y(far[0]), along_z(total))
        attn_last, small_z, ff_got = bar(
            attn_last, flip(small, "dp", dp_size, 2), exchange_ctx(ff_pieces)
        )
        small = small + small_z
        small = small + flip(small, "dp", dp_size, 4)
        attn_pieces = exchange_ctx(pieces_of_sum(attn_last))
        grad_g_out, grad_u_out, grad_d_out = land(ff_got, ff_widths)
        grad_q_out, grad_k_out, grad_v_out, grad_o_out = land(attn_pieces, attn_widths)
    else:
        grad_g_out, grad_u_out, grad_d_out = plain_sums(near + far, ff_widths)
        grad_q_out, grad_k_out, grad_v_out, grad_o_out = plain_sums(attn_chunks, attn_widths)
        small = sum_all(small, dp_size)
    _, first_pull = jax.vjp(lambda u: rms_scale(u, gains[0]), own_tokens)
    input_grad = sum_out(block_order, grad_resid + first_pull(sum_parts(grad_one))[0], ())
    norm_own = lax.dynamic_slice_in_dim(small[:2], lax.axis_index(ALL) * shard, shard, 1)
    head_sum = small[2:, :head_dim] + small[2:, head_dim : 2 * head_dim]
    return (
        layer_out[None],
        input_grad[None],
        grad_q_out,
        grad_k_out,
        grad_v_out,
        grad_o_out.T,
        grad_g_out,
        grad_u_out,
        grad_d_out.T,
        norm_own.astype(BF),
        head_sum.astype(BF),
    )


def solution(mesh):
    def step(*arrays):
        return on_device(mesh.shape["dp"], *arrays)

    in_specs = (
        P("dp", "ctx", None),
        P("dp", "ctx"),
        P(("dp", "ctx"), None),
        P(("dp", "ctx"), None),
        P(("dp", "ctx"), None),
        P(None, ("dp", "ctx")),
        P(("dp", "ctx"), None),
        P(("dp", "ctx"), None),
        P(None, ("dp", "ctx")),
        P(None, ("dp", "ctx")),
        P(),
        P("dp", "ctx", None),
    )
    out_specs = (
        P("dp", "ctx", None),
        P("dp", "ctx", None),
        P(("dp", "ctx"), None),
        P(("dp", "ctx"), None),
        P(("dp", "ctx"), None),
        P(None, ("dp", "ctx")),
        P(("dp", "ctx"), None),
        P(("dp", "ctx"), None),
        P(None, ("dp", "ctx")),
        P(None, ("dp", "ctx")),
        P(),
    )
    return jax.shard_map(step, mesh=mesh, in_specs=in_specs, out_specs=out_specs, check_vma=False)
```

```python
import functools

import jax
import jax.numpy as jnp
from jax import lax
from jax.experimental import pallas as pl
from jax.experimental.pallas import tpu as pltpu
from jax.sharding import PartitionSpec as P

EPS = 1e-05
THETA = 1000000.0
BF = jnp.bfloat16
F32 = jnp.float32
ALL = ("dp", "ctx")


def add_low(*terms):
    total = terms[0].astype(F32)
    for term in terms[1:]:
        total = total + term.astype(F32)
    return total.astype(BF)


def flip(value, axis, size, bits):
    return lax.ppermute(value, axis, [(i, i ^ bits) for i in range(size)])


def gather_ctx(own):
    core = flip(own, "ctx", 4, 1)
    across = flip(own, "ctx", 4, 2)
    return [own, core, across, flip(across, "ctx", 4, 1)]


def scatter_ctx(parts):
    far = flip(parts[3], "ctx", 4, 1)
    near = flip(parts[1], "ctx", 4, 1)
    return parts[0], near, flip(add_low(parts[2], far), "ctx", 4, 2)


def sum_parts(parts):
    return parts[0].astype(F32) + parts[1].astype(F32) + parts[2].astype(F32)


def exchange_ctx(parts):
    return [parts[0]] + [flip(parts[j], "ctx", 4, j) for j in range(1, 4)]


def place(parts, where, axis):
    size = parts[0].shape[axis]
    shape = list(parts[0].shape)
    shape[axis] = size * len(parts)
    out = jnp.zeros(shape, parts[0].dtype)
    for part, at in zip(parts, where):
        out = lax.dynamic_update_slice_in_dim(out, part, at * size, axis)
    return out


def bar(*trees):
    return lax.optimization_barrier(trees)


def ordered(dp_size):
    return dp_size == 8


def dp_order(dp_size):
    me = lax.axis_index("dp")
    return [((me - 2 * (i % 4)) % dp_size) ^ (i // 4) for i in range(dp_size)]


def across_y(value):
    return flip(value, "dp", 8, 1)


def along_z(value):
    return lax.ppermute(value, "dp", [(i, (i + 2) % 8) for i in range(8)])


def sum_all(value, dp_size):
    for bits in (1, 2):
        value = value + flip(value, "ctx", 4, bits)
    bits = 1
    while bits < dp_size:
        value = value + flip(value, "dp", dp_size, bits)
        bits *= 2
    return value


def dot(a, b):
    return lax.dot_general(a, b, (((1,), (0,)), ((), ())), preferred_element_type=F32)


def dot_nt(a, b):
    return lax.dot_general(a, b, (((1,), (1,)), ((), ())), preferred_element_type=F32)


def dot_tn(a, b):
    return lax.dot_general(a, b, (((0,), (0,)), ((), ())), preferred_element_type=F32)


VMEM = pl.BlockSpec(memory_space=pltpu.VMEM)
SMEM = pl.BlockSpec(memory_space=pltpu.SMEM)
LANES = 128
HIGH = lax.Precision.HIGHEST


HEAVY = 10**11


def call(body, outs, ins, scratch=(), scalars=0, limit=4, flops=1000000, held=False):
    def spec(shape):
        if held:
            return VMEM
        zeros = (0,) * len(shape)
        return pl.BlockSpec(tuple(shape), lambda i: zeros, pipeline_mode=pl.Buffered(1))

    return pl.pallas_call(
        body,
        out_shape=[jax.ShapeDtypeStruct(shape, kind) for shape, kind in outs],
        grid=() if held else (1,),
        in_specs=[SMEM] * scalars + [spec(x.shape) for x in ins[scalars:]],
        out_specs=[spec(shape) for shape, _ in outs],
        scratch_shapes=list(scratch),
        compiler_params=pltpu.CompilerParams(vmem_limit_bytes=limit << 20),
        cost_estimate=pl.CostEstimate(flops=flops, bytes_accessed=1000, transcendentals=0),
    )(*ins)


def pack_body(order_ref, tokens_ref, docs_ref, out_ref):
    rows = tokens_ref.shape[0]

    def one(i, _):
        out_ref[:rows, columns(i, LANES)] = tokens_ref[:, columns(order_ref[i], LANES)]
        return 0

    lax.fori_loop(0, tokens_ref.shape[1] // LANES, one, 0)
    if docs_ref is not None:
        below = jnp.broadcast_to(docs_ref[...].astype(F32), (16, rows)).astype(BF)
        out_ref[rows:, :rows] = below
        out_ref[rows:, rows:] = jnp.zeros((16, out_ref.shape[1] - rows), BF)


def pack_rows(order, rows, doc_row=None):
    if doc_row is None:
        body = lambda order_ref, rows_ref, out_ref: pack_body(order_ref, rows_ref, None, out_ref)
        return call(body, [(rows.shape, BF)], [order, rows], scalars=1)[0]
    shape = (rows.shape[0] + 16, rows.shape[1])
    return call(pack_body, [(shape, BF)], [order, rows, doc_row.reshape(1, -1)], scalars=1)[0]


def sum_body(order_ref, base_ref, *refs):
    parts, out_ref = refs[:-1], refs[-1]

    def one(i, _):
        at = columns(i, LANES)
        total = base_ref[:, at]
        if parts:
            part = parts[0][:, at].astype(F32)
            for ref in parts[1:]:
                part = part + ref[:, at].astype(F32)
            total = total + part
        out_ref[:, columns(order_ref[i], LANES)] = total.astype(BF)
        return 0

    lax.fori_loop(0, base_ref.shape[1] // LANES, one, 0)


def sum_out(order, base, parts):
    return call(sum_body, [(base.shape, BF)], [order, base, *parts], scalars=1)[0]


def by_blocks(count, rows, body):
    def one(i, _):
        body(pl.ds(pl.multiple_of(i * rows, rows), rows))
        return 0

    lax.fori_loop(0, count, one, 0)


def move(target, to, source, start, rows):
    step = 32

    def one(i, _):
        goal = pl.ds(pl.multiple_of(to + i * step, step), step)
        target[goal, :] = source[pl.ds(pl.multiple_of(start + i * step, step), step), :]
        return 0

    lax.fori_loop(0, rows // step, one, 0)


def hand_out(ref, parts):
    rows = parts[0].shape[0]
    for j, part in enumerate(parts):
        move(part, 0, ref, j * rows, rows)


def lane_masks(rows):
    lane = lax.broadcasted_iota(jnp.int32, (rows, LANES), 1)
    return lane < 64, lax.rem(lane, 64) < 32


def half_sums(squares):
    row = lax.broadcasted_iota(jnp.int32, (LANES, LANES), 0) // 64
    col = lax.broadcasted_iota(jnp.int32, (LANES, LANES), 1) // 64
    return jnp.dot(
        squares, (row == col).astype(F32), preferred_element_type=F32, precision=HIGH
    )


def turn(value, first):
    return jnp.where(first, pltpu.roll(value, 96, 1), pltpu.roll(value, 32, 1))


def doubled(value, left):
    other = pltpu.roll(value, 64, 1)
    return jnp.where(left, value, other), jnp.where(left, other, value)


def prepare_body(rows, *refs):
    packs, blocks = refs[:4], refs[4:12]
    table_ref, head_ref = refs[12:14]
    normed_ref, saved_ref, q_ref, kd_ref, rest_ref, kt_ref, vt_ref = refs[14:21]
    wo_ref, gains_ref, all_ref = refs[21:24]
    for i, block in enumerate(blocks):
        at = i * LANES
        rest_ref[at : at + LANES, 256:] = block[:LANES, :512]
        wo_ref[at : at + LANES, :] = block[:LANES, 512:]
        gains_ref[:, at : at + LANES] = block[LANES : LANES + 8, :LANES].astype(F32)
    for j, pack in enumerate(packs):
        move(all_ref, j * rows, pack, 0, rows)
    left, first = lane_masks(LANES)
    gain = gains_ref[0:1, :]
    q_gain, k_gain = head_ref[0:1, :], head_ref[1:2, :]

    def chunk(i, _):
        at = pl.ds(pl.multiple_of(i * LANES, LANES), LANES)
        x = all_ref[at, :].astype(F32)
        scale = lax.rsqrt(jnp.mean(x * x, -1, keepdims=True) + EPS)
        normed = (x * scale * gain).astype(BF)
        normed_ref[at, :] = normed
        pre = jnp.dot(normed, rest_ref[:, 256:], preferred_element_type=F32)
        saved_ref[at, :384] = pre[:, :384]
        saved_ref[at, 384:] = table_ref[at, :]
        cos, sin = doubled(table_ref[at, :], left)
        turned = []
        for b in range(3):
            u = pre[:, b * LANES : (b + 1) * LANES]
            u = u * lax.rsqrt(half_sums(u * u) * (1.0 / 64) + EPS) * (k_gain if b == 2 else q_gain)
            turned.append(u * cos + turn(u, first) * sin)
        q_ref[0, at, :] = turned[0].astype(BF)
        q_ref[1, at, :] = turned[1].astype(BF)
        key, value = turned[2], pre[:, 384:]
        low, high = doubled(key, left)
        kd_ref[0, at, :] = low.astype(BF)
        kd_ref[1, at, :] = high.astype(BF)
        kt_ref[:, at] = key.T.astype(BF)
        low, high = doubled(value, left)
        rest_ref[at, :LANES] = low.astype(BF)
        rest_ref[at, LANES:256] = high.astype(BF)
        vt_ref[:, at] = value.T.astype(BF)
        return 0

    lax.fori_loop(0, all_ref.shape[0] // LANES, chunk, 0)


def two_heads(block, left):
    zero = jnp.zeros_like(block)
    return jnp.concatenate([jnp.where(left, block, zero), jnp.where(left, zero, block)], 0)


def seen(start_row, first_key, rows, first_query):
    shape = (rows, 2 * rows)
    key = lax.broadcasted_iota(jnp.int32, shape, 0)
    mask = key + first_key >= start_row
    if first_query is not None:
        lane = lax.broadcasted_iota(jnp.int32, shape, 1)
        mask = mask & (key <= jnp.where(lane < rows, lane, lane - rows))
    return mask


LOG2E = 1.4426950408889634
SCORE = LOG2E / 8.0


def attend_body(rows, me_ref, first_ref, q_ref, kd_ref, vt_ref, start_ref, wo_ref, *refs):
    parts = refs[:4]
    out_ref, wide_ref, lse_ref, sum_ref, acc_ref, part_ref = refs[4:10]
    me = me_ref[0]
    left = lax.broadcasted_iota(jnp.int32, (rows, LANES), 1) < 64

    def one(step, _):
        kv, a = step // 4, lax.rem(step, 4)
        at_q = pl.ds(pl.multiple_of((a ^ me) * rows, rows), rows)
        q2 = two_heads(q_ref[kv, at_q, :], left)
        start_row = start_ref[a ^ me]
        sum_ref[...] = jnp.zeros_like(sum_ref)
        acc_ref[...] = jnp.zeros_like(acc_ref)
        for d in range(3):

            @pl.when((a >= d) & (first_ref[a ^ me] < (a - d + 1) * rows))
            def _():
                at_k = pl.ds(pl.multiple_of(((a - d) ^ me) * rows, rows), rows)
                scores = dot_nt(kd_ref[kv, at_k, :], q2)
                mask = seen(start_row, (a - d) * rows, rows, a if d == 0 else None)
                p = jnp.where(mask, jnp.exp2(scores * SCORE), 0.0)
                sum_ref[...] += jnp.sum(p, 0, keepdims=True)
                half = pl.ds(pl.multiple_of(kv * 64, 64), 64)
                acc_ref[...] += dot(vt_ref[half, at_k], p.astype(BF))

        total = sum_ref[...]
        lse_ref[kv * 4 + (a ^ me)] = jnp.log2(total)
        mixed = acc_ref[...] / total
        mixed = jnp.concatenate([mixed[:, :rows], mixed[:, rows:]], 0).T
        wide_ref[kv, at_q, :] = mixed
        out_ref[at_q, columns(kv, LANES)] = mixed.astype(BF)
        return 0

    lax.fori_loop(0, 8, one, 0)

    def project(at):
        part_ref[at, :] = dot_nt(out_ref[at, :], wo_ref[...]).astype(BF)

    by_blocks(4, rows, project)
    hand_out(part_ref, parts)


def attend_back_body(rows, *refs):
    me_ref, first_ref = refs[:2]
    refs = refs[1:]
    g0, g1, g2, g3, q_ref, kd_ref, rest_ref, kt_ref, start_ref, wide_ref, lse_ref = refs[1:12]
    saved_ref, head_ref, wo_ref, normed_ref, gains_ref = refs[12:17]
    parts, low_ref, head_sum_ref, gain_sum_ref, grad_ref = refs[17:21], *refs[21:25]
    mixed_ref, dq_ref, dk_ref, dv_ref, acc_ref = refs[25:30]
    me = me_ref[0]
    left = lax.broadcasted_iota(jnp.int32, (rows, LANES), 1) < 64
    for j, g in enumerate((g0, g1, g2, g3)):
        move(grad_ref, j * rows, g, 0, rows)

    def mix(at):
        grad = dot(grad_ref[at, :], wo_ref[...]).astype(BF)
        mixed_ref[0, at, :] = grad[:, :LANES]
        mixed_ref[1, at, :] = grad[:, LANES:]

    by_blocks(4, rows, mix)
    dk_ref[...] = jnp.zeros_like(dk_ref)
    dv_ref[...] = jnp.zeros_like(dv_ref)
    pick = (
        lax.broadcasted_iota(jnp.int32, (8, LANES), 1) // 64
        == lax.broadcasted_iota(jnp.int32, (8, LANES), 0)
    ).astype(F32)

    def one(step, _):
        kv, a = step // 4, lax.rem(step, 4)
        at_q = pl.ds(pl.multiple_of((a ^ me) * rows, rows), rows)
        q2 = two_heads(q_ref[kv, at_q, :], left)
        grad = mixed_ref[kv, at_q, :]
        g2 = two_heads(grad, left)
        inner = lax.dot_general(
            pick,
            grad.astype(F32) * wide_ref[kv, at_q, :],
            (((1,), (1,)), ((), ())),
            preferred_element_type=F32,
            precision=HIGH,
        )
        inner = jnp.concatenate([inner[0:1], inner[1:2]], 1)
        lse = lse_ref[kv * 4 + (a ^ me)]
        start_row = start_ref[a ^ me]
        acc_ref[...] = jnp.zeros_like(acc_ref)
        for d in range(3):

            @pl.when((a >= d) & (first_ref[a ^ me] < (a - d + 1) * rows))
            def _():
                at_k = pl.ds(pl.multiple_of(((a - d) ^ me) * rows, rows), rows)
                scores = dot_nt(kd_ref[kv, at_k, :], q2)
                mask = seen(start_row, (a - d) * rows, rows, a if d == 0 else None)
                p = jnp.where(mask, jnp.exp2(scores * SCORE - lse), 0.0)
                gp = dot_nt(rest_ref[at_k, columns(kv, LANES)], g2)
                gs = (p * (gp - inner)).astype(BF)
                dv_ref[kv, at_k, :] += dot(p.astype(BF), g2)
                dk_ref[kv, at_k, :] += dot(gs, q2)
                half = pl.ds(pl.multiple_of(kv * 64, 64), 64)
                acc_ref[...] += dot(kt_ref[half, at_k], gs)

        both = acc_ref[...] * 0.125
        dq_ref[kv, at_q, :] = jnp.concatenate([both[:, :rows], both[:, rows:]], 0).T
        return 0

    lax.fori_loop(0, 8, one, 0)
    left, first = lane_masks(LANES)
    head_sum_ref[...] = jnp.zeros_like(head_sum_ref)

    def folded(ref, at):
        low, high = ref[0, at, :], ref[1, at, :]
        low, high = low + pltpu.roll(low, 64, 1), high + pltpu.roll(high, 64, 1)
        return jnp.where(left, low, high)

    def chunk(i, _):
        at = pl.ds(pl.multiple_of(i * LANES, LANES), LANES)
        cos, sin = doubled(saved_ref[at, 384:], left)
        for b in range(3):
            u = saved_ref[at, b * LANES : (b + 1) * LANES]
            g = folded(dk_ref, at) * 0.125 if b == 2 else dq_ref[b, at, :]
            w = g * cos - turn(g, first) * sin
            row = 1 if b == 2 else 0
            gain = head_ref[row : row + 1, :]
            r = lax.rsqrt(half_sums(u * u) * (1.0 / 64) + EPS)
            head_sum_ref[row : row + 1, :] += jnp.sum(w * u * r, 0, keepdims=True)
            w = w * gain
            back = r * w - u * (r * r * r) * (half_sums(w * u) * (1.0 / 64))
            low_ref[at, b * LANES : (b + 1) * LANES] = back.astype(BF)
        low_ref[at, 384:] = folded(dv_ref, at).astype(BF)
        return 0

    lax.fori_loop(0, low_ref.shape[0] // LANES, chunk, 0)
    gain_sum = jnp.zeros((1, normed_ref.shape[1]), F32)
    for j in range(4):
        at = slice(j * rows, (j + 1) * rows)
        grad = dot_nt(low_ref[at, :], rest_ref[:, 256:])
        parts[j][...] = grad.astype(BF)
        gain_sum = gain_sum + jnp.sum(grad * normed_ref[at, :].astype(F32), 0, keepdims=True)
    gain_sum_ref[...] = gain_sum / gains_ref[0:1, :]


def columns(at, width):
    return pl.ds(pl.multiple_of(at * width, LANES), width)


def spread_body(widths, me_ref, *refs):
    weights, outs = refs[: len(widths)], refs[-4:]
    rows = weights[0].shape[0]
    me = me_ref[0]
    for j, out in enumerate(outs):
        start = 0
        for weight, width in zip(weights, widths):
            out[:rows, start : start + width] = weight[:, columns(me ^ j, width)]
            start += width
    if len(refs) > len(widths) + 4:
        gains = refs[len(widths)][...].astype(F32)
        gains = jnp.concatenate([gains, jnp.zeros((6, rows), F32)], 0)
        gains = jnp.concatenate([gains] * (LANES // rows), 1)
        lane = lax.broadcasted_iota(jnp.int32, (8, LANES), 1)
        gains = jnp.where(lane // rows == me, gains, 0.0).astype(BF)
        for out in outs:
            out[rows:, :] = jnp.zeros((8, out.shape[1]), BF)
            out[rows:, :LANES] = gains


def join_body(rows, me_ref, *refs):
    pieces, out = refs[:4], refs[4]
    me = me_ref[0]
    for j, piece in enumerate(pieces):
        out[pl.ds(pl.multiple_of((me ^ j) * rows, rows), rows), :] = piece[:rows, :]
    if pieces[0].shape[0] > rows:
        below = [piece[rows:, :].astype(F32) for piece in pieces]
        out[4 * rows :, :] = (below[0] + below[1] + below[2] + below[3]).astype(BF)


def part_body(me_ref, one_ref, two_ref, three_ref, *refs):
    outs, total_ref = refs[:4], refs[4]
    total = one_ref[...].astype(F32) + two_ref[...].astype(F32) + three_ref[...].astype(F32)
    total_ref[...] = total
    rows = outs[0].shape[0]
    for j, out in enumerate(outs):
        at = pl.ds(pl.multiple_of((me_ref[0] ^ j) * rows, rows), rows)
        out[...] = total_ref[at, :].astype(BF)


def land_body(widths, me_ref, *refs):
    pieces, outs = refs[:4], refs[4:]
    me = me_ref[0]
    start = 0
    for out, width in zip(outs, widths):
        for j, piece in enumerate(pieces):
            out[:, columns(me ^ j, width)] = piece[:, start : start + width]
        start += width


def small_body(order_ref, one_ref, two_ref, head_ref, *refs):
    out_ref = refs[-1]
    out_ref[...] = jnp.zeros_like(out_ref)
    for i in range(one_ref.shape[1] // LANES):
        at = columns(order_ref[i], LANES)
        out_ref[0:1, at] = one_ref[:, i * LANES : (i + 1) * LANES]
        out_ref[1:2, at] = two_ref[:, i * LANES : (i + 1) * LANES]
    out_ref[2:4, :LANES] = head_ref[0:2, :]


def feed_body(rows, pieces, *refs):
    normed, packs, weights = refs[:4], refs[4:8], refs[8 : 8 + pieces]
    hidden_ref, gate_ref, up_ref, w_ref, down_ref, normed_ref, grad_ref = refs[8 + pieces :]
    ff = hidden_ref.shape[1]
    row = 0
    for weight in weights:
        move(w_ref, row, weight.at[:, : 2 * ff], 0, weight.shape[0])
        move(down_ref, row, weight.at[:, 2 * ff :], 0, weight.shape[0])
        row += weight.shape[0]
    for j in range(4):
        move(normed_ref, j * rows, normed[j], 0, rows)
        move(grad_ref, j * rows, packs[j], 0, rows)

    def one(i, _):
        at = pl.ds(pl.multiple_of(i * rows, rows), rows)
        x = normed_ref[at, :]
        gate, up = dot(x, w_ref[:, :ff]), dot(x, w_ref[:, ff:])
        grad = dot(grad_ref[at, :], down_ref[...])
        sig = 1.0 / (1.0 + jnp.exp(-gate))
        silu = gate * sig
        hidden_ref[at, :] = (silu * up).astype(BF)
        gate_ref[at, :] = (grad * up * (sig * (1.0 + gate * (1.0 - sig)))).astype(BF)
        up_ref[at, :] = (grad * silu).astype(BF)
        return 0

    lax.fori_loop(0, 4, one, 0)


def feed_back_body(rows, gate_ref, up_ref, w_ref, *refs):
    parts, part_ref = refs[:4], refs[4]
    ff = gate_ref.shape[1]

    def one(i, _):
        at = pl.ds(pl.multiple_of(i * rows, rows), rows)
        total = dot_nt(gate_ref[at, :], w_ref[:, :ff]) + dot_nt(up_ref[at, :], w_ref[:, ff:])
        part_ref[at, :] = total.astype(BF)
        return 0

    lax.fori_loop(0, 4, one, 0)
    hand_out(part_ref, parts)


def down_body(rows, hidden_ref, down_ref, *refs):
    parts, part_ref = refs[:4], refs[4]

    def one(at):
        part_ref[at, :] = dot_nt(hidden_ref[at, :], down_ref[...]).astype(BF)

    by_blocks(4, rows, one)
    hand_out(part_ref, parts)


def attn_weights_body(normed_ref, grad_qkv_ref, grad_ref, out_ref, *chunks):
    cut = grad_qkv_ref.shape[1]
    chunks, whole_ref = chunks[:-1], chunks[-1]
    width = 2 * LANES

    def one(i, _):
        at = columns(i, width)
        whole_ref[at, :cut] = dot_tn(normed_ref[:, at], grad_qkv_ref[...]).astype(BF)
        whole_ref[at, cut:] = dot_tn(grad_ref[:, at], out_ref[...]).astype(BF)
        return 0

    lax.fori_loop(0, whole_ref.shape[0] // width, one, 0)
    hand_out(whole_ref, chunks)


def rms_scale(values, gain_row):
    return values * lax.rsqrt(jnp.mean(values * values, -1, keepdims=True) + EPS) * gain_row


def place_all(pieces, me, widths):
    outs, start = [], 0
    for width in widths:
        cut = [p[:, start : start + width] for p in pieces]
        outs.append(place(cut, [me ^ j for j in range(4)], 1))
        start += width
    return outs


def on_device(
    dp_size,
    tokens,
    doc_ids,
    w_query,
    key_weight,
    value_weight,
    w_output,
    w_gate,
    w_up,
    w_down,
    norm_gains,
    head_norm_gains,
    out_grad,
):
    local_len, model_dim = tokens.shape[1:]
    tokens, out_grad, doc_row = tokens[0], out_grad[0], doc_ids[0]
    head_dim = head_norm_gains.shape[1]
    q_cols, kv_cols = w_query.shape[1] // 4, key_weight.shape[1] // 4
    shard = norm_gains.shape[1]
    ff_cols = w_gate.shape[1] // 4
    me = lax.axis_index("ctx")
    places = [me ^ j for j in range(4)]
    full_len = 4 * local_len
    fast = ordered(dp_size)
    block_order = jnp.stack(dp_order(dp_size)) if fast else jnp.arange(model_dim // LANES)
    block_order = block_order.astype(jnp.int32)
    me_row = me.reshape(1).astype(jnp.int32)
    attn_widths = (q_cols, kv_cols, kv_cols, q_cols)
    ff_widths = (ff_cols, ff_cols, ff_cols)
    wide, ff_wide = sum(attn_widths), sum(ff_widths)
    attn_local = [w_query, key_weight, value_weight, w_output.T]
    ff_local = [w_gate, w_up, w_down.T]

    pack = pack_rows(block_order, tokens, doc_row)
    grad_pack = pack_rows(block_order, out_grad)
    if fast:
        sent = call(
            functools.partial(spread_body, attn_widths),
            [((shard + 8, wide), BF)] * 4,
            [me_row, *attn_local, norm_gains],
            scalars=1,
            limit=58,
        )
        ff_sent = call(
            functools.partial(spread_body, ff_widths),
            [((shard, ff_wide), BF)] * 4,
            [me_row, *ff_local],
            scalars=1,
        )
        got, ff_sent = bar(exchange_ctx(sent), ff_sent)
        ff_got = exchange_ctx(ff_sent)
        (block,) = call(
            functools.partial(join_body, shard),
            [((4 * shard + 8, wide), BF)],
            [me_row, *got],
            scalars=1,
        )
        y0, z1, pack, ff_got = bar(across_y(block), along_z(block), pack, ff_got)
        core_pack, far_pack = flip(pack, "ctx", 4, 1), flip(pack, "ctx", 4, 2)
        y1, z2 = bar(across_y(z1), along_z(z1))
        (ff_block,) = call(
            functools.partial(join_body, shard),
            [((4 * shard, ff_wide), BF)],
            [me_row, *ff_got],
            scalars=1,
        )
        y2, z3, far_pack, grad_pack, ff_block = bar(
            across_y(z2), along_z(z2), far_pack, grad_pack, ff_block
        )
        far_core_pack = flip(far_pack, "ctx", 4, 1)
        y3, ff_block, far_core_pack = bar(across_y(z3), ff_block, far_core_pack)
        ff_z1, ff_y0 = along_z(ff_block), across_y(ff_block)
        blocks = [block, z1, z2, z3, y0, y1, y2, y3]
    else:

        def pieces_of(weights):
            sent = []
            for at in places:
                cut = [
                    lax.dynamic_slice_in_dim(w, at * (w.shape[1] // 4), w.shape[1] // 4, 1)
                    for w in weights
                ]
                sent.append(jnp.concatenate(cut, 1))
            return sent

        def whole(weights):
            block = place(exchange_ctx(pieces_of(weights)), places, 0)
            return lax.all_gather(block, "dp", axis=0, tiled=True)

        gains = lax.all_gather(norm_gains, ALL, axis=1, tiled=True).reshape(2, -1, LANES)
        gains = jnp.pad(gains.transpose(1, 0, 2), ((0, 0), (0, 6), (0, wide - LANES)))
        blocks = jnp.concatenate([whole(attn_local).reshape(-1, LANES, wide), gains], 1)
        blocks = [blocks[i] for i in range(blocks.shape[0])]
        ff_w = [whole(ff_local)]
        core_pack, far_pack = flip(pack, "ctx", 4, 1), flip(pack, "ctx", 4, 2)
        far_core_pack = flip(far_pack, "ctx", 4, 1)

    packs = [pack, core_pack, far_pack, far_core_pack]
    core_grad, far_grad = flip(grad_pack, "ctx", 4, 1), flip(grad_pack, "ctx", 4, 2)
    docs = jnp.concatenate([p[local_len, :local_len] for p in packs])
    index = jnp.concatenate(
        [at * local_len + jnp.arange(local_len, dtype=jnp.int32) for at in places]
    )
    starts = jnp.sum((docs[None, :] < docs[:, None]).astype(jnp.int32), -1)
    positions = (index - starts).astype(F32)
    half = head_dim // 2
    lane = jnp.arange(LANES)
    freqs = THETA ** (-(2.0 * (lane % half).astype(F32)) / head_dim)
    angles = positions[:, None] * freqs
    sine = jnp.sin(angles) * jnp.where(lane % head_dim < half, -1.0, 1.0)
    table = jnp.where(lane < head_dim, jnp.cos(angles), sine)
    starts = starts.reshape(4, local_len)
    firsts = starts[:, 0]
    starts = jnp.concatenate([starts, starts], 1).reshape(4, 1, 2 * local_len)
    head_gains = jnp.concatenate([head_norm_gains, head_norm_gains], 1).astype(F32)

    part_shapes = [((local_len, model_dim), BF)] * 4
    normed_one, saved, queries, keys, rest, keys_t, values_t, wo_t, gains = call(
        functools.partial(prepare_body, local_len),
        [
            ((full_len, model_dim), BF),
            ((full_len, q_cols + kv_cols + LANES), F32),
            ((2, full_len, LANES), BF),
            ((2, full_len, LANES), BF),
            ((full_len, 2 * LANES + q_cols + 2 * kv_cols), BF),
            ((LANES, full_len), BF),
            ((LANES, full_len), BF),
            ((model_dim, q_cols), BF),
            ((8, model_dim), F32),
        ],
        [*packs, *blocks, table, head_gains],
        [pltpu.VMEM((full_len, model_dim), BF)],
        limit=28,
        flops=HEAVY,
    )
    if fast:
        queries, keys, ff_z1, ff_y0, core_grad, far_grad = bar(
            queries, keys, ff_z1, ff_y0, core_grad, far_grad
        )
        ff_z2, ff_y1 = along_z(ff_z1), across_y(ff_z1)
    grad_packs = [grad_pack, core_grad, far_grad, flip(far_grad, "ctx", 4, 1)]
    *resid_parts, attn_out, attn_wide, lse = call(
        functools.partial(attend_body, local_len),
        part_shapes
        + [
            ((full_len, q_cols), BF),
            ((2, full_len, LANES), F32),
            ((8, 1, 2 * local_len), F32),
        ],
        [me_row, firsts, queries, keys, values_t, starts, wo_t],
        [
            pltpu.VMEM((1, 2 * local_len), F32),
            pltpu.VMEM((head_dim, 2 * local_len), F32),
            pltpu.VMEM((full_len, model_dim), BF),
        ],
        scalars=2,
        limit=20,
    )
    own_tokens = pack[:local_len].astype(F32)
    own_grad = grad_pack.astype(F32)
    near_one, far_one = flip(resid_parts[1], "ctx", 4, 1), flip(resid_parts[3], "ctx", 4, 1)
    far_one = add_low(resid_parts[2], far_one)
    if fast:
        far_one, ff_z2, ff_y1 = bar(far_one, ff_z2, ff_y1)
        ff_z3, ff_y2 = along_z(ff_z2), across_y(ff_z2)
    far_one = flip(far_one, "ctx", 4, 2)
    resid = own_tokens + sum_parts((resid_parts[0], near_one, far_one))
    normed_own = rms_scale(resid, gains[1]).astype(BF)
    normed_core, normed_far = flip(normed_own, "ctx", 4, 1), flip(normed_own, "ctx", 4, 2)
    if fast:
        normed_far, ff_z3, ff_y2 = bar(normed_far, ff_z3, ff_y2)
        cut = ff_block.shape[0] // 2
        ff_w = [ff_block, ff_z1, ff_z2, ff_z3, ff_y0, ff_y1, ff_y2]
        ff_w += [across_y(ff_z3[:cut]), along_z(ff_y2[cut:])]
    normed_two = [normed_own, normed_core, normed_far, flip(normed_far, "ctx", 4, 1)]

    ff_shape = ((full_len, ff_cols), BF)
    hidden, grad_gate, grad_up, w_own, w_down_own, normed_all, grad_all = call(
        functools.partial(feed_body, local_len, len(ff_w)),
        [ff_shape] * 3
        + [((model_dim, 2 * ff_cols), BF), ((model_dim, ff_cols), BF)]
        + [((full_len, model_dim), BF)] * 2,
        [*normed_two, *grad_packs, *ff_w],
        limit=16,
        held=True,
    )

    def ff_chunks(at):
        cut = [dot_tn(normed_all[:, at], g).astype(BF) for g in (grad_gate, grad_up)]
        cut.append(dot_tn(grad_all[:, at], hidden).astype(BF))
        rows = cut[0].shape[0] // 4
        return [
            jnp.concatenate([c[r * rows : (r + 1) * rows] for c in cut], 1) for r in range(4)
        ]

    def pieces_of_sum(last):
        wide = last[0].shape[1]
        return call(
            part_body,
            [((shard, wide), BF)] * 4,
            [me_row, *last],
            [pltpu.VMEM((4 * shard, wide), F32)],
            scalars=1,
            limit=12,
        )

    def land(pieces, widths):
        return call(
            functools.partial(land_body, widths),
            [((shard, 4 * width), BF) for width in widths],
            [me_row, *pieces],
            scalars=1,
        )

    def plain_sums(chunks, widths):
        mine = lax.psum_scatter(jnp.concatenate(chunks, 0), "dp", scatter_dimension=0, tiled=True)
        pieces = [lax.dynamic_slice_in_dim(mine, at * shard, shard, 0) for at in places]
        return place_all(exchange_ctx(pieces), me, widths)

    def tick(*values):
        def body(*refs):
            refs[-1][...] = jnp.zeros((8, LANES), BF)

        return pl.pallas_call(
            body,
            out_shape=jax.ShapeDtypeStruct((8, LANES), BF),
            in_specs=[pl.BlockSpec(memory_space=pl.ANY)] * len(values),
            out_specs=VMEM,
            cost_estimate=pl.CostEstimate(flops=HEAVY, bytes_accessed=1000, transcendentals=0),
        )(*values)

    middle = model_dim // 2
    far = ff_chunks(slice(middle, None))
    if fast:
        cut = 4 * shard // 2
        first, early = across_y(far[1][:cut]), along_z(far[1][cut:])
        far[1], grad_gate, grad_up = bar(far[1], grad_gate, grad_up)
    *two_parts, = call(
        functools.partial(feed_back_body, local_len),
        part_shapes,
        [grad_gate, grad_up, w_own],
        [pltpu.VMEM((full_len, model_dim), BF)],
        limit=8,
        held=True,
    )
    near_two, far_two = flip(two_parts[1], "ctx", 4, 1), flip(two_parts[3], "ctx", 4, 1)
    if fast:
        near_two, far_two, hidden, normed_all, grad_all = bar(near_two, far_two, hidden, normed_all, grad_all)
    near = ff_chunks(slice(0, middle))
    far_two = add_low(two_parts[2], far_two)
    if fast:
        second = jnp.concatenate([far[2][:cut], add_low(far[2][cut:], early)], 0)
        total = jnp.concatenate([add_low(near[1][:cut], first), near[1][cut:]], 0)
        far_two, total, second = bar(far_two, total, second)
        total, second = along_z(total), across_y(second)
    far_two = flip(far_two, "ctx", 4, 2)
    grad_norm_two = sum_parts((two_parts[0], near_two, far_two))
    _, second_pull = jax.vjp(rms_scale, resid, gains[1])
    grad_resid_norm, grad_gain_two = second_pull(grad_norm_two)
    grad_resid = own_grad + grad_resid_norm
    (*down_parts,) = call(
        functools.partial(down_body, local_len),
        part_shapes,
        [hidden, w_down_own],
        [pltpu.VMEM((full_len, model_dim), BF)],
        limit=18,
    )

    grad_low = grad_resid.astype(BF)
    grad_core, grad_far = flip(grad_low, "ctx", 4, 1), flip(grad_low, "ctx", 4, 2)
    if fast:
        grad_far, down_parts = bar(grad_far, down_parts)
    down_near, down_far = flip(down_parts[1], "ctx", 4, 1), flip(down_parts[3], "ctx", 4, 1)
    down_far = add_low(down_parts[2], down_far)
    grad_attn = [grad_low, grad_core, grad_far, flip(grad_far, "ctx", 4, 1)]
    if fast:
        total, third = bar(add_low(near[2], second, total), far[3])
        grad_attn, down_far, tick_two = bar(grad_attn, down_far, tick(total))
        total, third, fourth = along_z(total), across_y(third), across_y(far[0])
    down_far = flip(down_far, "ctx", 4, 2)
    *one_parts, grad_qkv, head_sums, gain_one, grad_attn_all = call(
        functools.partial(attend_back_body, local_len),
        part_shapes
        + [
            ((full_len, q_cols + 2 * kv_cols), BF),
            ((8, LANES), F32),
            ((1, model_dim), F32),
            ((full_len, model_dim), BF),
        ],
        [
            me_row,
            firsts,
            *grad_attn,
            queries,
            keys,
            rest,
            keys_t,
            starts,
            attn_wide,
            lse,
            saved,
            head_gains,
            wo_t,
            normed_one,
            gains,
        ],
        [
            pltpu.VMEM((2, full_len, LANES), BF),
            pltpu.VMEM((2, full_len, LANES), F32),
            pltpu.VMEM((2, full_len, LANES), F32),
            pltpu.VMEM((2, full_len, LANES), F32),
            pltpu.VMEM((head_dim, 2 * local_len), F32),
        ],
        scalars=2,
        limit=24,
        held=True,
    )
    if fast:
        total, grad_qkv = bar(add_low(near[3], third, total), grad_qkv)
        last = (near[0], fourth, along_z(total))
    layer_out = sum_out(block_order, resid, (down_parts[0], down_near, down_far))
    attn_chunks = call(
        attn_weights_body,
        [((LANES, wide), BF)] * 8,
        [normed_one, grad_qkv, grad_attn_all, attn_out],
        [pltpu.VMEM((model_dim, wide), BF)],
        limit=20,
    )
    ticks = [tick_two] if fast else []
    (small,) = call(
        small_body,
        [((4, model_dim), F32)],
        [block_order, gain_one, grad_gain_two.reshape(1, -1), head_sums, *ticks],
        scalars=1,
    )
    grad_one = scatter_ctx(one_parts)
    if fast:
        near, far = attn_chunks[:4], attn_chunks[4:]
        total, last = bar(add_low(near[1], across_y(far[1])), last)
        ff_pieces = pieces_of_sum(last)
        total, small_core = bar(
            add_low(near[2], across_y(far[2]), along_z(total)), flip(small, "ctx", 4, 1)
        )
        small = small + small_core
        small = small + flip(small, "ctx", 4, 2)
        total, small_y = bar(
            add_low(near[3], across_y(far[3]), along_z(total)), flip(small, "dp", dp_size, 1)
        )
        small = small + small_y
        attn_last = (near[0], across_y(far[0]), along_z(total))
        attn_last, small_z, ff_got = bar(
            attn_last, flip(small, "dp", dp_size, 2), exchange_ctx(ff_pieces)
        )
        small = small + small_z
        small = small + flip(small, "dp", dp_size, 4)
        attn_pieces = exchange_ctx(pieces_of_sum(attn_last))
        grad_g_out, grad_u_out, grad_d_out = land(ff_got, ff_widths)
        grad_q_out, grad_k_out, grad_v_out, grad_o_out = land(attn_pieces, attn_widths)
    else:
        grad_g_out, grad_u_out, grad_d_out = plain_sums(near + far, ff_widths)
        grad_q_out, grad_k_out, grad_v_out, grad_o_out = plain_sums(attn_chunks, attn_widths)
        small = sum_all(small, dp_size)
    _, first_pull = jax.vjp(lambda u: rms_scale(u, gains[0]), own_tokens)
    input_grad = sum_out(block_order, grad_resid + first_pull(sum_parts(grad_one))[0], ())
    norm_own = lax.dynamic_slice_in_dim(small[:2], lax.axis_index(ALL) * shard, shard, 1)
    head_sum = small[2:, :head_dim] + small[2:, head_dim : 2 * head_dim]
    return (
        layer_out[None],
        input_grad[None],
        grad_q_out,
        grad_k_out,
        grad_v_out,
        grad_o_out.T,
        grad_g_out,
        grad_u_out,
        grad_d_out.T,
        norm_own.astype(BF),
        head_sum.astype(BF),
    )


def solution(mesh):
    def step(*arrays):
        return on_device(mesh.shape["dp"], *arrays)

    in_specs = (
        P("dp", "ctx", None),
        P("dp", "ctx"),
        P(("dp", "ctx"), None),
        P(("dp", "ctx"), None),
        P(("dp", "ctx"), None),
        P(None, ("dp", "ctx")),
        P(("dp", "ctx"), None),
        P(("dp", "ctx"), None),
        P(None, ("dp", "ctx")),
        P(None, ("dp", "ctx")),
        P(),
        P("dp", "ctx", None),
    )
    out_specs = (
        P("dp", "ctx", None),
        P("dp", "ctx", None),
        P(("dp", "ctx"), None),
        P(("dp", "ctx"), None),
        P(("dp", "ctx"), None),
        P(None, ("dp", "ctx")),
        P(("dp", "ctx"), None),
        P(("dp", "ctx"), None),
        P(None, ("dp", "ctx")),
        P(None, ("dp", "ctx")),
        P(),
    )
    return jax.shard_map(step, mesh=mesh, in_specs=in_specs, out_specs=out_specs, check_vma=False)
```
